32 devices in a mesh: dp: 32 (over z, y, x, core).
Axes of the slice: x: 2, y: 2, z: 4, core: 2. Of those that a mesh axis runs over, the one named last changes fastest.
Arguments:
- tokens: bfloat16 [2, 32, 256, 768], P(None, None, 'dp'), may hold values from -6 to 6
- lengths: int32 [2, 32], replicated, may hold values from 1 to 256, 5120 in all within a row
- order: int32 [2, 32], replicated, may hold values from 0 to 31, each once within a row
- weight_in: bfloat16 [768, 2304], P('dp'), may hold values from -0.3125 to 0.3125
- bias_in: bfloat16 [1536], P('dp'), may hold values from -1.5 to 1.5
- weight_mix: bfloat16 [768, 768], P('dp'), may hold values from -1.25 to 1.25
- bias_mix: bfloat16 [768], P('dp'), may hold values from -1.5 to 1.5
- gain_first: bfloat16 [768], P('dp'), may hold values from 0.25 to 1.75
- shift_first: bfloat16 [768], P('dp'), may hold values from -1.5 to 1.5
- weight_up: bfloat16 [768, 3072], P('dp'), may hold values from -0.21875 to 0.21875
- bias_up: bfloat16 [3072], P('dp'), may hold values from -1.5 to 1.5
- weight_down: bfloat16 [3072, 768], P('dp'), may hold values from -0.15625 to 0.15625
- bias_down: bfloat16 [768], P('dp'), may hold values from -1.5 to 1.5
- gain_second: bfloat16 [768], P('dp'), may hold values from 0.25 to 1.75
- shift_second: bfloat16 [768], P('dp'), may hold values from -1.5 to 1.5
- cotangent: bfloat16 [2, 32, 256, 768], P(None, None, 'dp'), may hold values from -6 to 6
Outputs:
- layer_out: bfloat16 [2, 32, 256, 768], P(None, None, 'dp')
- tokens_grad: bfloat16 [2, 32, 256, 768], P(None, None, 'dp')
- weight_in_grad: float32 [768, 2304], P('dp')
- bias_in_grad: float32 [1536], P('dp')
- weight_mix_grad: float32 [768, 768], P('dp')
- bias_mix_grad: float32 [768], P('dp')
- gain_first_grad: float32 [768], P('dp')
- shift_first_grad: float32 [768], P('dp')
- weight_up_grad: float32 [768, 3072], P('dp')
- bias_up_grad: float32 [3072], P('dp')
- weight_down_grad: float32 [3072, 768], P('dp')
- bias_down_grad: float32 [768], P('dp')
- gain_second_grad: float32 [768], P('dp')
- shift_second_grad: float32 [768], P('dp')
The draws below stay inside these ranges and needn't reach their ends.
Inputs may be any that keep to these rules, and one draw needn't show every extreme that they name: In each micro-batch the 32 lengths sum to 5120, and the longest is exactly 256. Each row of order names every input sequence of its micro-batch exactly once.
All inputs are finite; a program needn't handle non-finite values.
Results may differ from the reference program's by a relative error of at most 0.015.
The reference program's roundings to bfloat16 on the way count: a program that leaves them out, or rounds other values in their place, can miss the bound.
Values may be sent and summed in bfloat16 or wider, within the bound.
A program may use at most 128 MiB of HBM per device.

```python
import math
import jax
import jax.numpy as jnp
import numpy as np
from jax import lax

D = 768
H = 12
HD = 64
FF = 3072
L = 256
MB = 2
SEQS = 32


def block_levels(key, dims, shards, least, top_value):
    def one(position, blocks):
        heights = jax.random.uniform(jax.random.fold_in(jax.random.fold_in(key, 6), position), (blocks,), jnp.float32, least / len(shards), top_value / len(shards))
        return jnp.repeat(jnp.exp(heights), dims[position] // blocks).reshape((-1,) + (1,) * (len(dims) - position - 1))

    factor_of = one(*shards[0])
    for cut in shards[1:]:
        factor_of = factor_of * one(*cut)
    return factor_of


def length_profile(amount, total, bound, slope):
    portions = [(1 << 20) // math.isqrt(standing ** slope) + 1 for standing in range(2, amount + 1)]
    rest, counts = total - bound - (amount - 1), [1] * (amount - 1)
    while rest > 0:
        candidates = [i for i in range(amount - 1) if counts[i] < bound]
        whole, budget = sum([portions[i] for i in candidates]), rest
        for i in candidates:
            extra = min(bound - counts[i], max(1, budget * portions[i] // whole), rest)
            counts[i] = counts[i] + extra
            rest = rest - extra
    return np.array([bound] + counts)


def uneven(own_key, count, total, limit, slope):
    if count == 2:
        one = jax.random.randint(own_key, (), max(1, total - limit), min(limit, total - 1) + 1)
        return jnp.stack([one, total - one])
    tallies = jnp.asarray(length_profile(count, total, limit, slope), jnp.int32)
    twos = (count - 1) // 2
    source_of, sink = tallies[1:1 + 2 * twos:2], tallies[2:2 + 2 * twos:2]
    room = jnp.minimum(source_of - 1, limit - sink)
    moved = jax.random.randint(jax.random.fold_in(own_key, 1), (twos,), 0, 1 << 20) % (room + 1)
    tallies = tallies.at[1:1 + 2 * twos:2].set(source_of - moved).at[2:2 + 2 * twos:2].set(sink + moved)
    return tallies[jax.random.permutation(jax.random.fold_in(own_key, 2), count)]


def normal_values(own_key, extent, scale, limit, pieces=(), held_as=jnp.bfloat16):
    drawn = jax.random.normal(own_key, extent, jnp.float32) * scale
    if len(pieces) > 0:
        drawn = block_levels(own_key, extent, pieces, -0.22, 0.18) * drawn
    return jnp.clip(drawn, min=-limit, max=limit).astype(held_as)


def setup_inputs(seed: int = 0) -> dict:
    streams_of = jax.random.split(jax.random.key(seed), 17)
    tokens = normal_values(streams_of[0], (MB, SEQS, L, D), 1.0, 6.0, ((2, 32),))
    lengths = jax.vmap(lambda own: uneven(own, SEQS, SEQS * L * 5 // 8, L, 2))(jax.random.split(streams_of[1], MB)).reshape((MB, SEQS)).astype(jnp.int32)
    order = jax.vmap(lambda own: jax.random.permutation(own, SEQS))(jax.random.split(streams_of[2], MB)).reshape((MB, SEQS)).astype(jnp.int32)
    weight_in = normal_values(streams_of[3], (D, 3 * D), (D // 2) ** -0.5, 0.3125, ((0, 32),))
    bias_in = normal_values(streams_of[4], (2 * D,), 0.3, 1.5, ((0, 32),))
    weight_mix = normal_values(streams_of[5], (D, D), (D // 32) ** -0.5, 1.25, ((0, 32),))
    bias_mix = normal_values(streams_of[6], (D,), 0.3, 1.5, ((0, 32),))
    gain_first = jnp.clip(1.0 + 0.15 * jax.random.normal(streams_of[7], (D,), jnp.float32), 0.25, 1.75).astype(jnp.bfloat16)
    shift_first = normal_values(streams_of[8], (D,), 0.3, 1.5, ((0, 32),))
    weight_up = normal_values(streams_of[9], (D, FF), D ** -0.5, 0.21875, ((0, 32),))
    bias_up = normal_values(streams_of[10], (FF,), 0.3, 1.5, ((0, 32),))
    weight_down = normal_values(streams_of[11], (FF, D), (FF // 2) ** -0.5, 0.15625, ((0, 32),))
    bias_down = normal_values(streams_of[12], (D,), 0.3, 1.5, ((0, 32),))
    gain_second = jnp.clip(1.0 + 0.15 * jax.random.normal(streams_of[13], (D,), jnp.float32), 0.25, 1.75).astype(jnp.bfloat16)
    shift_second = normal_values(streams_of[14], (D,), 0.3, 1.5, ((0, 32),))
    cotangent = normal_values(streams_of[15], (MB, SEQS, L, D), 1.0, 6.0, ((2, 32),))
    return {"tokens": tokens, "lengths": lengths, "order": order, "weight_in": weight_in, "bias_in": bias_in, "weight_mix": weight_mix, "bias_mix": bias_mix, "gain_first": gain_first, "shift_first": shift_first, "weight_up": weight_up, "bias_up": bias_up, "weight_down": weight_down, "bias_down": bias_down, "gain_second": gain_second, "shift_second": shift_second, "cotangent": cotangent}


@jax.custom_vjp
def low(v):
    return lax.optimization_barrier(v.astype(jnp.bfloat16)).astype(jnp.float32)

@jax.custom_vjp
def low_back(v):
    return v

def low_keep(v):
    return (low(v), None)

def low_pass(kept, grad):
    return (grad,)

def back_keep(v):
    return (v, None)

def back_low(kept, grad):
    return (low(grad),)
low.defvjp(low_keep, low_pass)
low_back.defvjp(back_keep, back_low)
epsilon = 1e-12

def layer_norm(summed, norm_gain, norm_shift):
    row_mean = lax.optimization_barrier(jnp.mean(summed, -1, keepdims=True))
    centered = summed - row_mean
    variance = lax.optimization_barrier(jnp.mean(centered * centered, -1, keepdims=True))
    return centered * lax.rsqrt(variance + epsilon) * norm_gain + norm_shift

def encode(sequence, length, params):
    weight_in, bias_in, weight_mix, bias_mix, gain_first, shift_first, weight_up, bias_up, weight_down, bias_down, gain_second, shift_second = params
    highest = lax.Precision.HIGHEST
    bias_full = jnp.concatenate([bias_in[:D], jnp.zeros((D,), jnp.float32), bias_in[D:]])
    projected = low(low_back(jnp.dot(sequence, weight_in, precision=highest) + bias_full))
    queries = projected[:, :D].reshape(L, H, HD)
    key_block = projected[:, D:2 * D].reshape(L, H, HD)
    value_block = projected[:, 2 * D:].reshape(L, H, HD)
    scores = low_back(jnp.einsum('qhd,khd->hqk', queries, key_block, precision=highest) * 0.125)
    valid = jnp.arange(L, dtype=jnp.int32) < length
    scores = jnp.where(valid[None, None, :], scores, -1e+30)
    probability = low(jax.nn.softmax(scores, axis=-1))
    context = jnp.einsum('hqk,khd->qhd', probability, value_block, precision=highest).reshape(L, D)
    context = low(low_back(context))
    branch = low_back(jnp.dot(context, weight_mix, precision=highest) + bias_mix)
    hidden = layer_norm(sequence + branch, gain_first, shift_first)
    preact = low_back(jnp.dot(low(hidden), weight_up, precision=highest) + bias_up)
    activated = low(jax.nn.gelu(preact, approximate=False))
    feed_out = low_back(jnp.dot(activated, weight_down, precision=highest) + bias_down)
    return layer_norm(hidden + feed_out, gain_second, shift_second)

def reference(tokens, lengths, order, weight_in, bias_in, weight_mix, bias_mix, gain_first, shift_first, weight_up, bias_up, weight_down, bias_down, gain_second, shift_second, cotangent):
    count = MB * SEQS
    group = math.gcd(count, max(1, 4096 // L))
    floats = tuple((array.astype(jnp.float32) for array in (weight_in, bias_in, weight_mix, bias_mix, gain_first, shift_first, weight_up, bias_up, weight_down, bias_down, gain_second, shift_second)))
    batch_index = jnp.arange(MB, dtype=jnp.int32)[:, None]
    picks = order.astype(jnp.int32)
    spans = lengths[batch_index, picks].reshape(count // group, group).astype(jnp.int32)

    def whole_layer(inputs, *params):
        dealt = inputs[batch_index, picks]
        blocks = dealt.reshape(count // group, group, L, D)

        def run_block(packed):
            return jax.vmap(lambda single, span: encode(single, span, params))(packed[0], packed[1])
        outputs = lax.map(jax.checkpoint(run_block), (blocks, spans))
        return outputs.reshape(MB, SEQS, L, D)
    result, pullback = jax.vjp(whole_layer, tokens.astype(jnp.float32), *floats)
    grads = pullback(cotangent.astype(jnp.float32))
    return (result.astype(jnp.bfloat16), grads[0].astype(jnp.bfloat16), grads[1], grads[2], grads[3], grads[4], grads[5], grads[6], grads[7], grads[8], grads[9], grads[10], grads[11], grads[12])
```

```python
import functools

import jax
import jax.numpy as jnp
from jax import lax
from jax.experimental import pallas as pl
from jax.experimental.pallas import tpu as pltpu
from jax.sharding import PartitionSpec as P

MESH = pl.DeviceIdType.MESH

HD = 64


epsilon = 1e-12


def matmul(left, right):
    return jnp.dot(left, right, preferred_element_type=jnp.float32)


def rows_product(left, right):
    return lax.dot_general(
        left, right, (((0,), (0,)), ((), ())), preferred_element_type=jnp.float32
    )


def right_transposed(left, right):
    return lax.dot_general(
        left, right, (((1,), (1,)), ((), ())), preferred_element_type=jnp.float32
    )


def split_heads(block, heads):
    return block.reshape(block.shape[0], heads, -1).transpose(1, 0, 2)


def join_heads(block):
    return block.transpose(1, 0, 2).reshape(block.shape[1], -1)


def norm_forward(summed, norm_gain, norm_shift):
    row_mean = jnp.mean(summed, -1, keepdims=True)
    centered = summed - row_mean
    reciprocal = lax.rsqrt(jnp.mean(centered * centered, -1, keepdims=True) + epsilon)
    normed = centered * reciprocal
    return (normed * norm_gain + norm_shift, normed, reciprocal)


def norm_backward(upstream, normed, reciprocal, norm_gain):
    scaled = upstream * norm_gain
    summed_grad = reciprocal * (
        scaled
        - jnp.mean(scaled, -1, keepdims=True)
        - normed * jnp.mean(scaled * normed, -1, keepdims=True)
    )
    return (summed_grad, jnp.sum(upstream * normed, 0), jnp.sum(upstream, 0))


def head_scores(head_query, head_keys, valid):
    scores = right_transposed(head_query, head_keys) * 0.125
    return jnp.where(valid[None, :], scores, -1e30)


def attend_forward(packed, valid):
    head_query, head_keys, head_values = packed
    scores = head_scores(head_query, head_keys, valid)
    row_max = jnp.max(scores, -1, keepdims=True)
    weights_raw = jnp.exp(scores - row_max)
    row_sum = jnp.sum(weights_raw, -1, keepdims=True)
    probability = weights_raw / row_sum
    context = matmul(probability.astype(jnp.bfloat16), head_values)
    return (context, (row_max + jnp.log(row_sum))[:, 0])


def attend_backward(packed, valid):
    head_query, head_keys, head_values, context_grad, log_total = packed
    scores = head_scores(head_query, head_keys, valid)
    probability = jnp.exp(scores - log_total[:, None])
    low_prob = probability.astype(jnp.bfloat16)
    prob_grad = right_transposed(context_grad, head_values)
    value_grad = rows_product(low_prob, context_grad)
    shifted = prob_grad - jnp.sum(probability * prob_grad, -1, keepdims=True)
    score_grad = (probability * shifted).astype(jnp.bfloat16)
    query_grad = matmul(score_grad, head_keys) * 0.125
    key_grad = rows_product(score_grad, head_query) * 0.125
    return (query_grad, key_grad, value_grad)


def forward(weights, sequence, length):
    (
        weight_in,
        bias_in,
        weight_mix,
        bias_mix,
        gain_first,
        shift_first,
        weight_up,
        bias_up,
        weight_down,
        bias_down,
        gain_second,
        shift_second,
    ) = weights
    width = sequence.shape[1]
    heads = width // HD
    valid = jnp.arange(sequence.shape[0], dtype=jnp.int32) < length
    bias_full = jnp.concatenate(
        [
            bias_in[:width].astype(jnp.float32),
            jnp.zeros((width,), jnp.float32),
            bias_in[width:].astype(jnp.float32),
        ]
    )
    projected = (matmul(sequence, weight_in) + bias_full).astype(jnp.bfloat16)
    queries = split_heads(projected[:, :width], heads)
    key_heads = split_heads(projected[:, width : 2 * width], heads)
    value_heads = split_heads(projected[:, 2 * width :], heads)
    context, log_total = lax.map(
        lambda packed: attend_forward(packed, valid), (queries, key_heads, value_heads)
    )
    context_low = join_heads(context).astype(jnp.bfloat16)
    branch = matmul(context_low, weight_mix) + bias_mix.astype(jnp.float32)
    hidden, normed_first, recip_first = norm_forward(
        sequence.astype(jnp.float32) + branch,
        gain_first.astype(jnp.float32),
        shift_first.astype(jnp.float32),
    )
    hidden_low = hidden.astype(jnp.bfloat16)
    preact = matmul(hidden_low, weight_up) + bias_up.astype(jnp.float32)
    activated = jax.nn.gelu(preact, approximate=False).astype(jnp.bfloat16)
    feed_out = matmul(activated, weight_down) + bias_down.astype(jnp.float32)
    result, normed_second, recip_second = norm_forward(
        hidden + feed_out, gain_second.astype(jnp.float32), shift_second.astype(jnp.float32)
    )
    stored = (
        valid,
        queries,
        key_heads,
        value_heads,
        log_total,
        context_low,
        normed_first,
        recip_first,
        hidden_low,
        preact,
        activated,
        normed_second,
        recip_second,
    )
    return (result.astype(jnp.bfloat16), stored)


def backward(weights, sequence, upstream_low, stored):
    (
        weight_in,
        bias_in,
        weight_mix,
        bias_mix,
        gain_first,
        shift_first,
        weight_up,
        bias_up,
        weight_down,
        bias_down,
        gain_second,
        shift_second,
    ) = weights
    (
        valid,
        queries,
        key_heads,
        value_heads,
        log_total,
        context_low,
        normed_first,
        recip_first,
        hidden_low,
        preact,
        activated,
        normed_second,
        recip_second,
    ) = stored
    width = sequence.shape[1]
    heads = width // HD
    upstream = upstream_low.astype(jnp.float32)
    second_grad, gain_second_grad, shift_second_grad = norm_backward(
        upstream, normed_second, recip_second, gain_second.astype(jnp.float32)
    )
    feed_grad = second_grad.astype(jnp.bfloat16)
    bias_down_grad = jnp.sum(feed_grad.astype(jnp.float32), 0)
    weight_down_grad = rows_product(activated, feed_grad)
    act_grad = right_transposed(feed_grad, weight_down)
    slope = (
        0.5 * (1.0 + jax.scipy.special.erf(preact * 0.7071067811865476))
        + preact * jnp.exp(-0.5 * preact * preact) * 0.3989422804014327
    )
    preact_grad = (act_grad * slope).astype(jnp.bfloat16)
    bias_up_grad = jnp.sum(preact_grad.astype(jnp.float32), 0)
    weight_up_grad = rows_product(hidden_low, preact_grad)
    hidden_grad = second_grad + right_transposed(preact_grad, weight_up)
    first_grad, gain_first_grad, shift_first_grad = norm_backward(
        hidden_grad, normed_first, recip_first, gain_first.astype(jnp.float32)
    )
    branch_grad = first_grad.astype(jnp.bfloat16)
    bias_mix_grad = jnp.sum(branch_grad.astype(jnp.float32), 0)
    weight_mix_grad = rows_product(context_low, branch_grad)
    context_grad = right_transposed(branch_grad, weight_mix).astype(jnp.bfloat16)
    query_grad, key_grad, value_grad = lax.map(
        lambda packed: attend_backward(packed, valid),
        (queries, key_heads, value_heads, split_heads(context_grad, heads), log_total),
    )
    projected_grad = jnp.concatenate(
        [join_heads(query_grad), join_heads(key_grad), join_heads(value_grad)], -1
    ).astype(jnp.bfloat16)
    column_sums = jnp.sum(projected_grad.astype(jnp.float32), 0)
    bias_in_grad = jnp.concatenate([column_sums[:width], column_sums[2 * width :]])
    weight_in_grad = rows_product(sequence, projected_grad)
    input_grad = (first_grad + right_transposed(projected_grad, weight_in)).astype(jnp.bfloat16)
    gradients = (
        weight_in_grad,
        bias_in_grad,
        weight_mix_grad,
        bias_mix_grad,
        gain_first_grad,
        shift_first_grad,
        weight_up_grad,
        bias_up_grad,
        weight_down_grad,
        bias_down_grad,
        gain_second_grad,
        shift_second_grad,
    )
    return (input_grad, gradients)


def permuted(blocks, picks):
    chosen = (picks[:, None] == jnp.arange(picks.shape[0])[None, :]).astype(blocks.dtype)
    flat = blocks.reshape(blocks.shape[0], -1)
    return matmul(chosen, flat).astype(blocks.dtype).reshape(blocks.shape)


def inverse_of(picks):
    slots = jnp.arange(picks.shape[0], dtype=jnp.int32)
    return jnp.sum(jnp.where(picks[:, None] == slots[None, :], slots[:, None], 0), 0)


def fetch_weights(shards):
    return (
        lax.all_gather(shards[0], "dp", axis=0, tiled=True),
        lax.all_gather(shards[1], "dp", axis=0, tiled=True),
        lax.all_gather(shards[2], "dp", axis=0, tiled=True),
        lax.all_gather(shards[3], "dp", axis=0, tiled=True),
        lax.all_gather(shards[4], "dp", axis=0, tiled=True),
        lax.all_gather(shards[5], "dp", axis=0, tiled=True),
        lax.all_gather(shards[6], "dp", axis=0, tiled=True),
        lax.all_gather(shards[7], "dp", axis=0, tiled=True),
        lax.all_gather(shards[8], "dp", axis=0, tiled=True),
        lax.all_gather(shards[9], "dp", axis=0, tiled=True),
        lax.all_gather(shards[10], "dp", axis=0, tiled=True),
        lax.all_gather(shards[11], "dp", axis=0, tiled=True),
    )


def add_trees(first, second):
    if first is None:
        return second
    return jax.tree.map(lambda left, right: left + right, first, second)


def portable(
    tokens,
    lengths,
    order,
    weight_in,
    bias_in,
    weight_mix,
    bias_mix,
    gain_first,
    shift_first,
    weight_up,
    bias_up,
    weight_down,
    bias_down,
    gain_second,
    shift_second,
    cotangent,
):
    shards = (
        weight_in,
        bias_in,
        weight_mix,
        bias_mix,
        gain_first,
        shift_first,
        weight_up,
        bias_up,
        weight_down,
        bias_down,
        gain_second,
        shift_second,
    )
    device = lax.axis_index("dp")
    totals = None
    outputs_list = []
    grads_list = []
    for batch in range(tokens.shape[0]):
        current = fetch_weights(shards)
        picks = order[batch]
        dealt_tokens = permuted(tokens[batch], picks)
        sequence, upstream = (
            lax.all_to_all(dealt_tokens, "dp", split_axis=0, concat_axis=1, tiled=True),
            lax.all_to_all(cotangent[batch], "dp", split_axis=0, concat_axis=1, tiled=True),
        )
        length = jnp.sum(jnp.where(jnp.arange(picks.shape[0]) == picks[device], lengths[batch], 0))
        result, stored = forward(current, sequence[0], length)
        behind = (
            lax.all_gather(shards[0], "dp", axis=0, tiled=True),
            lax.all_gather(shards[1], "dp", axis=0, tiled=True),
            lax.all_gather(shards[2], "dp", axis=0, tiled=True),
            lax.all_gather(shards[3], "dp", axis=0, tiled=True),
            lax.all_gather(shards[4], "dp", axis=0, tiled=True),
            lax.all_gather(shards[5], "dp", axis=0, tiled=True),
            lax.all_gather(shards[6], "dp", axis=0, tiled=True),
            lax.all_gather(shards[7], "dp", axis=0, tiled=True),
            lax.all_gather(shards[8], "dp", axis=0, tiled=True),
            lax.all_gather(shards[9], "dp", axis=0, tiled=True),
            lax.all_gather(shards[10], "dp", axis=0, tiled=True),
            lax.all_gather(shards[11], "dp", axis=0, tiled=True),
        )
        input_grad, gradients = backward(behind, sequence[0], upstream[0], stored)
        back_out, back_grad = (
            lax.all_to_all(result[None], "dp", split_axis=1, concat_axis=0, tiled=True),
            lax.all_to_all(input_grad[None], "dp", split_axis=1, concat_axis=0, tiled=True),
        )
        restored = permuted(back_grad, inverse_of(picks))
        outputs_list.append(back_out)
        grads_list.append(restored)
        totals = add_trees(totals, gradients)
    totals = (
        lax.psum_scatter(totals[0], "dp", scatter_dimension=0, tiled=True),
        lax.psum_scatter(totals[1], "dp", scatter_dimension=0, tiled=True),
        lax.psum_scatter(totals[2], "dp", scatter_dimension=0, tiled=True),
        lax.psum_scatter(totals[3], "dp", scatter_dimension=0, tiled=True),
        lax.psum_scatter(totals[4], "dp", scatter_dimension=0, tiled=True),
        lax.psum_scatter(totals[5], "dp", scatter_dimension=0, tiled=True),
        lax.psum_scatter(totals[6], "dp", scatter_dimension=0, tiled=True),
        lax.psum_scatter(totals[7], "dp", scatter_dimension=0, tiled=True),
        lax.psum_scatter(totals[8], "dp", scatter_dimension=0, tiled=True),
        lax.psum_scatter(totals[9], "dp", scatter_dimension=0, tiled=True),
        lax.psum_scatter(totals[10], "dp", scatter_dimension=0, tiled=True),
        lax.psum_scatter(totals[11], "dp", scatter_dimension=0, tiled=True),
    )
    return (
        jnp.stack(outputs_list),
        jnp.stack(grads_list),
        totals[0],
        totals[1],
        totals[2],
        totals[3],
        totals[4],
        totals[5],
        totals[6],
        totals[7],
        totals[8],
        totals[9],
        totals[10],
        totals[11],
    )


COUNT = 32


def meet_all(me):
    barrier = pltpu.get_barrier_semaphore()

    def greet(step, carry):
        pl.semaphore_signal(
            barrier, inc=1, device_id=(lax.rem(me + step, COUNT),), device_id_type=MESH
        )
        return carry

    lax.fori_loop(1, COUNT, greet, 0)
    pl.semaphore_wait(barrier, COUNT - 1)


def remote(source, target, send_sem, recv_sem, device):
    return pltpu.make_async_remote_copy(
        src_ref=source,
        dst_ref=target,
        send_sem=send_sem,
        recv_sem=recv_sem,
        device_id=(device,),
        device_id_type=MESH,
    )


def collect_kernel(
    backward_order,
    tokens,
    cotangent,
    shard_in,
    shard_mix,
    shard_up,
    shard_down,
    shard_small,
    sequence,
    upstream,
    full_in,
    full_mix,
    full_up,
    full_down,
    full_small,
    dealt,
    send_sems,
    block_sems,
    exchange_sems,
    own_sems,
):
    me = lax.axis_index("dp")
    core, column, row, layer = me % 2, (me // 2) % 2, (me // 4) % 2, me // 8
    sibling = me + 1 - 2 * core
    across_row = me + 4 * (1 - 2 * row)
    across_column = me + 2 * (1 - 2 * column)
    second = (1 - core) * across_row + core * across_column
    third = (1 - core) * across_column + core * across_row
    lines = [((layer + step) % 4) * 8 + me % 8 for step in range(4)]
    shards = (shard_in, shard_mix, shard_up, shard_down, shard_small)
    fulls = (full_in, full_mix, full_up, full_down, full_small)
    kinds = range(len(fulls))

    own = [
        pltpu.make_async_copy(shards[kind], fulls[kind].at[me], own_sems.at[kind])
        for kind in kinds
    ] + [
        pltpu.make_async_copy(tokens.at[:, me], sequence.at[:, me], own_sems.at[len(fulls)])
    ]
    for copy in own:
        copy.start()
    for pair in range(2):
        for seat in range(COUNT):
            dealt[pair, seat] = cotangent[pair, backward_order[pair, seat]]
    own.append(
        pltpu.make_async_copy(dealt.at[:, me], upstream.at[:, me], own_sems.at[len(fulls) + 1])
    )
    own[-1].start()
    meet_all(me)

    def exchange(source, target, which):
        def go(step, carry):
            device = lax.rem(me + step, COUNT)
            remote(
                source.at[:, device],
                target.at[:, me],
                send_sems.at[which],
                exchange_sems.at[which],
                device,
            ).start()
            return carry

        lax.fori_loop(1, COUNT, go, 0)

    def exchanged(source, target, which):
        others = pl.ds(0, COUNT - 1)
        copy = remote(
            source.at[:, others], target.at[:, others], send_sems.at[which], exchange_sems.at[which], me
        )
        copy.wait_recv()
        copy.wait_send()

    def send(kind, source, block, device):
        remote(
            source,
            fulls[kind].at[block],
            send_sems.at[2 + kind],
            block_sems.at[kind, block],
            device,
        ).start()

    def receive(kind, block):
        here = fulls[kind].at[block]
        remote(here, here, send_sems.at[2 + kind], block_sems.at[kind, block], me).wait_recv()

    def forward(kind, block, devices):
        receive(kind, block)
        for device in devices:
            send(kind, fulls[kind].at[block], block, device)

    def from_lines(kind):
        for step in (1, 2, 3):
            forward(kind, lines[step], (second, third, sibling))

    def from_second(kind):
        for step in range(4):
            forward(kind, lines[step] + second - me, (third, sibling))

    def from_third(kind):
        for step in range(4):
            for offset in (0, second - me):
                forward(kind, lines[step] + third - me + offset, (sibling,))

    exchange(tokens, sequence, 0)
    for kind in kinds:
        for device in lines[1:] + [second, third, sibling]:
            send(kind, shards[kind], me, device)
    exchange(dealt, upstream, 1)
    for tick in range(len(fulls) + 2):
        for late, stage in enumerate((from_lines, from_second, from_third)):
            if 0 <= tick - late < len(fulls):
                stage(tick - late)
    for kind in kinds:
        for step in range(4):
            for there in (0, second - me):
                for further in (0, third - me):
                    receive(kind, lines[step] + sibling - me + there + further)
    exchanged(tokens, sequence, 0)
    exchanged(dealt, upstream, 1)
    for kind in kinds:
        here = fulls[kind].at[pl.ds(0, COUNT - 1)]
        remote(here, here, send_sems.at[2 + kind], block_sems.at[kind, 0], me).wait_send()
    for copy in own:
        copy.wait()


def collect(backward_order, tokens, cotangent, shards):
    anywhere = pl.BlockSpec(memory_space=pl.ANY)
    return pl.pallas_call(
        collect_kernel,
        out_shape=[jax.ShapeDtypeStruct(tokens.shape, tokens.dtype)] * 2
        + [jax.ShapeDtypeStruct((COUNT,) + shard.shape, shard.dtype) for shard in shards],
        in_specs=[
            pl.BlockSpec(memory_space=pltpu.SMEM),
            anywhere,
            pl.BlockSpec(memory_space=pltpu.VMEM),
        ]
        + [anywhere] * len(shards),
        out_specs=[anywhere] * (2 + len(shards)),
        scratch_shapes=[
            pltpu.VMEM(tokens.shape, tokens.dtype),
            pltpu.SemaphoreType.DMA((2 + len(shards),)),
            pltpu.SemaphoreType.DMA((len(shards), COUNT)),
            pltpu.SemaphoreType.DMA((2,)),
            pltpu.SemaphoreType.DMA((2 + len(shards),)),
        ],
        compiler_params=pltpu.CompilerParams(
            collective_id=0, has_side_effects=True, vmem_limit_bytes=40 << 20
        ),
        name="collect",
    )(backward_order, tokens, cotangent, *shards)


SMALL = (1, 3, 4, 5, 7, 9, 10, 11)
LARGE = (0, 2, 6, 8)


def local(tokens, lengths, order, *rest):
    shards, cotangent = rest[:12], rest[12]
    if lax.axis_size("dp") != COUNT or tokens.shape[2] % 8:
        return portable(tokens, lengths, order, *rest)
    device = lax.axis_index("dp")
    small = jnp.concatenate(
        [jnp.pad(shards[i].astype(jnp.float32), (0, 128 - shards[i].shape[0]))[None] for i in SMALL]
    )
    backward_order = jnp.stack([inverse_of(order[batch]) for batch in range(order.shape[0])])
    sequence, upstream, *full = collect(
        backward_order, tokens, cotangent, [shards[i] for i in LARGE] + [small]
    )
    weights = [None] * 12
    for place, i in enumerate(LARGE):
        weights[i] = full[place].reshape(-1, full[place].shape[-1])
    for place, i in enumerate(SMALL):
        weights[i] = full[4][:, place, : shards[i].shape[0]].reshape(-1).astype(jnp.bfloat16)
    totals = None
    outputs_list = []
    grads_list = []
    for batch in range(tokens.shape[0]):
        picks = order[batch]
        length = lengths[batch][device]
        mine = sequence[batch].reshape(-1, sequence.shape[-1])
        result, stored = forward(weights, mine, length)
        input_grad, gradients = backward(
            weights, mine, upstream[batch].reshape(mine.shape), stored
        )
        back_out, back_grad = (
            lax.all_to_all(result[None], "dp", split_axis=1, concat_axis=0, tiled=True),
            lax.all_to_all(input_grad[None], "dp", split_axis=1, concat_axis=0, tiled=True),
        )
        outputs_list.append(permuted(back_out, picks))
        grads_list.append(back_grad)
        totals = add_trees(totals, gradients)
    totals = [
        lax.psum_scatter(total, "dp", scatter_dimension=0, tiled=True) for total in totals
    ]
    return (jnp.stack(outputs_list), jnp.stack(grads_list), *totals)


def solution(mesh):
    return jax.shard_map(
        local,
        mesh=mesh,
        in_specs=(
            P(None, None, "dp", None),
            P(),
            P(),
            P("dp", None),
            P("dp"),
            P("dp", None),
            P("dp"),
            P("dp"),
            P("dp"),
            P("dp", None),
            P("dp"),
            P("dp", None),
            P("dp"),
            P("dp"),
            P("dp"),
            P(None, None, "dp", None),
        ),
        out_specs=(
            P(None, None, "dp", None),
            P(None, None, "dp", None),
            P("dp", None),
            P("dp"),
            P("dp", None),
            P("dp"),
            P("dp"),
            P("dp"),
            P("dp", None),
            P("dp"),
            P("dp", None),
            P("dp"),
            P("dp"),
            P("dp"),
        ),
        check_vma=False,
    )
```

```python
import functools

import jax
import jax.numpy as jnp
from jax import lax
from jax.experimental import pallas as pl
from jax.experimental.pallas import tpu as pltpu
from jax.sharding import PartitionSpec as P

MESH = pl.DeviceIdType.MESH

HD = 64


epsilon = 1e-12


def matmul(left, right):
    return jnp.dot(left, right, preferred_element_type=jnp.float32)


def rows_product(left, right):
    return lax.dot_general(
        left, right, (((0,), (0,)), ((), ())), preferred_element_type=jnp.float32
    )


def right_transposed(left, right):
    return lax.dot_general(
        left, right, (((1,), (1,)), ((), ())), preferred_element_type=jnp.float32
    )


def split_heads(block, heads):
    return block.reshape(block.shape[0], heads, -1).transpose(1, 0, 2)


def join_heads(block):
    return block.transpose(1, 0, 2).reshape(block.shape[1], -1)


def norm_forward(summed, norm_gain, norm_shift):
    row_mean = jnp.mean(summed, -1, keepdims=True)
    centered = summed - row_mean
    reciprocal = lax.rsqrt(jnp.mean(centered * centered, -1, keepdims=True) + epsilon)
    normed = centered * reciprocal
    return (normed * norm_gain + norm_shift, normed, reciprocal)


def norm_backward(upstream, normed, reciprocal, norm_gain):
    scaled = upstream * norm_gain
    summed_grad = reciprocal * (
        scaled
        - jnp.mean(scaled, -1, keepdims=True)
        - normed * jnp.mean(scaled * normed, -1, keepdims=True)
    )
    return (summed_grad, jnp.sum(upstream * normed, 0), jnp.sum(upstream, 0))


def head_scores(head_query, head_keys, valid):
    scores = right_transposed(head_query, head_keys) * 0.125
    return jnp.where(valid[None, :], scores, -1e30)


def attend_forward(packed, valid):
    head_query, head_keys, head_values = packed
    scores = head_scores(head_query, head_keys, valid)
    row_max = jnp.max(scores, -1, keepdims=True)
    weights_raw = jnp.exp(scores - row_max)
    row_sum = jnp.sum(weights_raw, -1, keepdims=True)
    probability = weights_raw / row_sum
    context = matmul(probability.astype(jnp.bfloat16), head_values)
    return (context, (row_max + jnp.log(row_sum))[:, 0])


def attend_backward(packed, valid):
    head_query, head_keys, head_values, context_grad, log_total = packed
    scores = head_scores(head_query, head_keys, valid)
    probability = jnp.exp(scores - log_total[:, None])
    low_prob = probability.astype(jnp.bfloat16)
    prob_grad = right_transposed(context_grad, head_values)
    value_grad = rows_product(low_prob, context_grad)
    shifted = prob_grad - jnp.sum(probability * prob_grad, -1, keepdims=True)
    score_grad = (probability * shifted).astype(jnp.bfloat16)
    query_grad = matmul(score_grad, head_keys) * 0.125
    key_grad = rows_product(score_grad, head_query) * 0.125
    return (query_grad, key_grad, value_grad)


def forward(weights, sequence, length):
    (
        weight_in,
        bias_in,
        weight_mix,
        bias_mix,
        gain_first,
        shift_first,
        weight_up,
        bias_up,
        weight_down,
        bias_down,
        gain_second,
        shift_second,
    ) = weights
    width = sequence.shape[1]
    heads = width // HD
    valid = jnp.arange(sequence.shape[0], dtype=jnp.int32) < length
    bias_full = jnp.concatenate(
        [
            bias_in[:width].astype(jnp.float32),
            jnp.zeros((width,), jnp.float32),
            bias_in[width:].astype(jnp.float32),
        ]
    )
    projected = (matmul(sequence, weight_in) + bias_full).astype(jnp.bfloat16)
    queries = split_heads(projected[:, :width], heads)
    key_heads = split_heads(projected[:, width : 2 * width], heads)
    value_heads = split_heads(projected[:, 2 * width :], heads)
    context, log_total = lax.map(
        lambda packed: attend_forward(packed, valid), (queries, key_heads, value_heads)
    )
    context_low = join_heads(context).astype(jnp.bfloat16)
    branch = matmul(context_low, weight_mix) + bias_mix.astype(jnp.float32)
    hidden, normed_first, recip_first = norm_forward(
        sequence.astype(jnp.float32) + branch,
        gain_first.astype(jnp.float32),
        shift_first.astype(jnp.float32),
    )
    hidden_low = hidden.astype(jnp.bfloat16)
    preact = matmul(hidden_low, weight_up) + bias_up.astype(jnp.float32)
    activated = jax.nn.gelu(preact, approximate=False).astype(jnp.bfloat16)
    feed_out = matmul(activated, weight_down) + bias_down.astype(jnp.float32)
    result, normed_second, recip_second = norm_forward(
        hidden + feed_out, gain_second.astype(jnp.float32), shift_second.astype(jnp.float32)
    )
    stored = (
        valid,
        queries,
        key_heads,
        value_heads,
        log_total,
        context_low,
        normed_first,
        recip_first,
        hidden_low,
        preact,
        activated,
        normed_second,
        recip_second,
    )
    return (result.astype(jnp.bfloat16), stored)


def backward(weights, sequence, upstream_low, stored):
    (
        weight_in,
        bias_in,
        weight_mix,
        bias_mix,
        gain_first,
        shift_first,
        weight_up,
        bias_up,
        weight_down,
        bias_down,
        gain_second,
        shift_second,
    ) = weights
    (
        valid,
        queries,
        key_heads,
        value_heads,
        log_total,
        context_low,
        normed_first,
        recip_first,
        hidden_low,
        preact,
        activated,
        normed_second,
        recip_second,
    ) = stored
    width = sequence.shape[1]
    heads = width // HD
    upstream = upstream_low.astype(jnp.float32)
    second_grad, gain_second_grad, shift_second_grad = norm_backward(
        upstream, normed_second, recip_second, gain_second.astype(jnp.float32)
    )
    feed_grad = second_grad.astype(jnp.bfloat16)
    bias_down_grad = jnp.sum(feed_grad.astype(jnp.float32), 0)
    weight_down_grad = rows_product(activated, feed_grad)
    act_grad = right_transposed(feed_grad, weight_down)
    slope = (
        0.5 * (1.0 + jax.scipy.special.erf(preact * 0.7071067811865476))
        + preact * jnp.exp(-0.5 * preact * preact) * 0.3989422804014327
    )
    preact_grad = (act_grad * slope).astype(jnp.bfloat16)
    bias_up_grad = jnp.sum(preact_grad.astype(jnp.float32), 0)
    weight_up_grad = rows_product(hidden_low, preact_grad)
    hidden_grad = second_grad + right_transposed(preact_grad, weight_up)
    first_grad, gain_first_grad, shift_first_grad = norm_backward(
        hidden_grad, normed_first, recip_first, gain_first.astype(jnp.float32)
    )
    branch_grad = first_grad.astype(jnp.bfloat16)
    bias_mix_grad = jnp.sum(branch_grad.astype(jnp.float32), 0)
    weight_mix_grad = rows_product(context_low, branch_grad)
    context_grad = right_transposed(branch_grad, weight_mix).astype(jnp.bfloat16)
    query_grad, key_grad, value_grad = lax.map(
        lambda packed: attend_backward(packed, valid),
        (queries, key_heads, value_heads, split_heads(context_grad, heads), log_total),
    )
    projected_grad = jnp.concatenate(
        [join_heads(query_grad), join_heads(key_grad), join_heads(value_grad)], -1
    ).astype(jnp.bfloat16)
    column_sums = jnp.sum(projected_grad.astype(jnp.float32), 0)
    bias_in_grad = jnp.concatenate([column_sums[:width], column_sums[2 * width :]])
    weight_in_grad = rows_product(sequence, projected_grad)
    input_grad = (first_grad + right_transposed(projected_grad, weight_in)).astype(jnp.bfloat16)
    gradients = (
        weight_in_grad,
        bias_in_grad,
        weight_mix_grad,
        bias_mix_grad,
        gain_first_grad,
        shift_first_grad,
        weight_up_grad,
        bias_up_grad,
        weight_down_grad,
        bias_down_grad,
        gain_second_grad,
        shift_second_grad,
    )
    return (input_grad, gradients)


def permuted(blocks, picks):
    chosen = (picks[:, None] == jnp.arange(picks.shape[0])[None, :]).astype(blocks.dtype)
    flat = blocks.reshape(blocks.shape[0], -1)
    return matmul(chosen, flat).astype(blocks.dtype).reshape(blocks.shape)


def inverse_of(picks):
    slots = jnp.arange(picks.shape[0], dtype=jnp.int32)
    return jnp.sum(jnp.where(picks[:, None] == slots[None, :], slots[:, None], 0), 0)


def fetch_weights(shards):
    return (
        lax.all_gather(shards[0], "dp", axis=0, tiled=True),
        lax.all_gather(shards[1], "dp", axis=0, tiled=True),
        lax.all_gather(shards[2], "dp", axis=0, tiled=True),
        lax.all_gather(shards[3], "dp", axis=0, tiled=True),
        lax.all_gather(shards[4], "dp", axis=0, tiled=True),
        lax.all_gather(shards[5], "dp", axis=0, tiled=True),
        lax.all_gather(shards[6], "dp", axis=0, tiled=True),
        lax.all_gather(shards[7], "dp", axis=0, tiled=True),
        lax.all_gather(shards[8], "dp", axis=0, tiled=True),
        lax.all_gather(shards[9], "dp", axis=0, tiled=True),
        lax.all_gather(shards[10], "dp", axis=0, tiled=True),
        lax.all_gather(shards[11], "dp", axis=0, tiled=True),
    )


def add_trees(first, second):
    if first is None:
        return second
    return jax.tree.map(lambda left, right: left + right, first, second)


def portable(
    tokens,
    lengths,
    order,
    weight_in,
    bias_in,
    weight_mix,
    bias_mix,
    gain_first,
    shift_first,
    weight_up,
    bias_up,
    weight_down,
    bias_down,
    gain_second,
    shift_second,
    cotangent,
):
    shards = (
        weight_in,
        bias_in,
        weight_mix,
        bias_mix,
        gain_first,
        shift_first,
        weight_up,
        bias_up,
        weight_down,
        bias_down,
        gain_second,
        shift_second,
    )
    device = lax.axis_index("dp")
    totals = None
    outputs_list = []
    grads_list = []
    for batch in range(tokens.shape[0]):
        current = fetch_weights(shards)
        picks = order[batch]
        dealt_tokens = permuted(tokens[batch], picks)
        sequence, upstream = (
            lax.all_to_all(dealt_tokens, "dp", split_axis=0, concat_axis=1, tiled=True),
            lax.all_to_all(cotangent[batch], "dp", split_axis=0, concat_axis=1, tiled=True),
        )
        length = jnp.sum(jnp.where(jnp.arange(picks.shape[0]) == picks[device], lengths[batch], 0))
        result, stored = forward(current, sequence[0], length)
        behind = (
            lax.all_gather(shards[0], "dp", axis=0, tiled=True),
            lax.all_gather(shards[1], "dp", axis=0, tiled=True),
            lax.all_gather(shards[2], "dp", axis=0, tiled=True),
            lax.all_gather(shards[3], "dp", axis=0, tiled=True),
            lax.all_gather(shards[4], "dp", axis=0, tiled=True),
            lax.all_gather(shards[5], "dp", axis=0, tiled=True),
            lax.all_gather(shards[6], "dp", axis=0, tiled=True),
            lax.all_gather(shards[7], "dp", axis=0, tiled=True),
            lax.all_gather(shards[8], "dp", axis=0, tiled=True),
            lax.all_gather(shards[9], "dp", axis=0, tiled=True),
            lax.all_gather(shards[10], "dp", axis=0, tiled=True),
            lax.all_gather(shards[11], "dp", axis=0, tiled=True),
        )
        input_grad, gradients = backward(behind, sequence[0], upstream[0], stored)
        back_out, back_grad = (
            lax.all_to_all(result[None], "dp", split_axis=1, concat_axis=0, tiled=True),
            lax.all_to_all(input_grad[None], "dp", split_axis=1, concat_axis=0, tiled=True),
        )
        restored = permuted(back_grad, inverse_of(picks))
        outputs_list.append(back_out)
        grads_list.append(restored)
        totals = add_trees(totals, gradients)
    totals = (
        lax.psum_scatter(totals[0], "dp", scatter_dimension=0, tiled=True),
        lax.psum_scatter(totals[1], "dp", scatter_dimension=0, tiled=True),
        lax.psum_scatter(totals[2], "dp", scatter_dimension=0, tiled=True),
        lax.psum_scatter(totals[3], "dp", scatter_dimension=0, tiled=True),
        lax.psum_scatter(totals[4], "dp", scatter_dimension=0, tiled=True),
        lax.psum_scatter(totals[5], "dp", scatter_dimension=0, tiled=True),
        lax.psum_scatter(totals[6], "dp", scatter_dimension=0, tiled=True),
        lax.psum_scatter(totals[7], "dp", scatter_dimension=0, tiled=True),
        lax.psum_scatter(totals[8], "dp", scatter_dimension=0, tiled=True),
        lax.psum_scatter(totals[9], "dp", scatter_dimension=0, tiled=True),
        lax.psum_scatter(totals[10], "dp", scatter_dimension=0, tiled=True),
        lax.psum_scatter(totals[11], "dp", scatter_dimension=0, tiled=True),
    )
    return (
        jnp.stack(outputs_list),
        jnp.stack(grads_list),
        totals[0],
        totals[1],
        totals[2],
        totals[3],
        totals[4],
        totals[5],
        totals[6],
        totals[7],
        totals[8],
        totals[9],
        totals[10],
        totals[11],
    )


COUNT = 32


def meet_all(me):
    barrier = pltpu.get_barrier_semaphore()

    def greet(step, carry):
        pl.semaphore_signal(
            barrier, inc=1, device_id=(lax.rem(me + step, COUNT),), device_id_type=MESH
        )
        return carry

    lax.fori_loop(1, COUNT, greet, 0)
    pl.semaphore_wait(barrier, COUNT - 1)


def remote(source, target, send_sem, recv_sem, device):
    return pltpu.make_async_remote_copy(
        src_ref=source,
        dst_ref=target,
        send_sem=send_sem,
        recv_sem=recv_sem,
        device_id=(device,),
        device_id_type=MESH,
    )


def collect_kernel(
    backward_order,
    tokens,
    cotangent,
    shard_in,
    shard_mix,
    shard_up,
    shard_down,
    shard_small,
    sequence,
    upstream,
    full_in,
    full_mix,
    full_up,
    full_down,
    full_small,
    dealt,
    send_sems,
    block_sems,
    exchange_sems,
    own_sems,
):
    me = lax.axis_index("dp")
    core, column, row, layer = me % 2, (me // 2) % 2, (me // 4) % 2, me // 8
    sibling = me + 1 - 2 * core
    across_row = me + 4 * (1 - 2 * row)
    across_column = me + 2 * (1 - 2 * column)
    second = (1 - core) * across_row + core * across_column
    third = (1 - core) * across_column + core * across_row
    lines = [((layer + step) % 4) * 8 + me % 8 for step in range(4)]
    shards = (shard_in, shard_mix, shard_up, shard_down, shard_small)
    fulls = (full_in, full_mix, full_up, full_down, full_small)
    kinds = range(len(fulls))

    own = [
        pltpu.make_async_copy(shards[kind], fulls[kind].at[me], own_sems.at[kind])
        for kind in kinds
    ] + [
        pltpu.make_async_copy(tokens.at[:, me], sequence.at[:, me], own_sems.at[len(fulls)])
    ]
    for copy in own:
        copy.start()
    for pair in range(2):
        for seat in range(COUNT):
            dealt[pair, seat] = cotangent[pair, backward_order[pair, seat]]
    own.append(
        pltpu.make_async_copy(dealt.at[:, me], upstream.at[:, me], own_sems.at[len(fulls) + 1])
    )
    own[-1].start()
    meet_all(me)

    def exchange(source, target, which):
        def go(step, carry):
            device = lax.rem(me + step, COUNT)
            remote(
                source.at[:, device],
                target.at[:, me],
                send_sems.at[which],
                exchange_sems.at[which],
                device,
            ).start()
            return carry

        lax.fori_loop(1, COUNT, go, 0)

    def exchanged(source, target, which):
        others = pl.ds(0, COUNT - 1)
        copy = remote(
            source.at[:, others], target.at[:, others], send_sems.at[which], exchange_sems.at[which], me
        )
        copy.wait_recv()
        copy.wait_send()

    def send(kind, source, block, device):
        remote(
            source,
            fulls[kind].at[block],
            send_sems.at[2 + kind],
            block_sems.at[kind, block],
            device,
        ).start()

    def receive(kind, block):
        here = fulls[kind].at[block]
        remote(here, here, send_sems.at[2 + kind], block_sems.at[kind, block], me).wait_recv()

    def forward(kind, block, devices):
        receive(kind, block)
        for device in devices:
            send(kind, fulls[kind].at[block], block, device)

    def from_lines(kind):
        for step in (1, 2, 3):
            forward(kind, lines[step], (second, third, sibling))

    def from_second(kind):
        for step in range(4):
            forward(kind, lines[step] + second - me, (third, sibling))

    def from_third(kind):
        for step in range(4):
            for offset in (0, second - me):
                forward(kind, lines[step] + third - me + offset, (sibling,))

    exchange(tokens, sequence, 0)
    for kind in kinds:
        for device in lines[1:] + [second, third, sibling]:
            send(kind, shards[kind], me, device)
    exchange(dealt, upstream, 1)
    for tick in range(len(fulls) + 2):
        for late, stage in enumerate((from_lines, from_second, from_third)):
            if 0 <= tick - late < len(fulls):
                stage(tick - late)
    for kind in kinds:
        for step in range(4):
            for there in (0, second - me):
                for further in (0, third - me):
                    receive(kind, lines[step] + sibling - me + there + further)
    exchanged(tokens, sequence, 0)
    exchanged(dealt, upstream, 1)
    for kind in kinds:
        here = fulls[kind].at[pl.ds(0, COUNT - 1)]
        remote(here, here, send_sems.at[2 + kind], block_sems.at[kind, 0], me).wait_send()
    for copy in own:
        copy.wait()


def collect(backward_order, tokens, cotangent, shards):
    anywhere = pl.BlockSpec(memory_space=pl.ANY)
    return pl.pallas_call(
        collect_kernel,
        out_shape=[jax.ShapeDtypeStruct(tokens.shape, tokens.dtype)] * 2
        + [jax.ShapeDtypeStruct((COUNT,) + shard.shape, shard.dtype) for shard in shards],
        in_specs=[
            pl.BlockSpec(memory_space=pltpu.SMEM),
            anywhere,
            pl.BlockSpec(memory_space=pltpu.VMEM),
        ]
        + [anywhere] * len(shards),
        out_specs=[anywhere] * (2 + len(shards)),
        scratch_shapes=[
            pltpu.VMEM(tokens.shape, tokens.dtype),
            pltpu.SemaphoreType.DMA((2 + len(shards),)),
            pltpu.SemaphoreType.DMA((len(shards), COUNT)),
            pltpu.SemaphoreType.DMA((2,)),
            pltpu.SemaphoreType.DMA((2 + len(shards),)),
        ],
        compiler_params=pltpu.CompilerParams(
            collective_id=0, has_side_effects=True, vmem_limit_bytes=40 << 20
        ),
        name="collect",
    )(backward_order, tokens, cotangent, *shards)


WIDTHS = (48, 24, 24, 24, 96, 24, 24, 24)
BIAS_IN, BIAS_MIX, GAIN_FIRST, SHIFT_FIRST, BIAS_UP, BIAS_DOWN, GAIN_SECOND, SHIFT_SECOND = range(8)
TILE = 256
PAIR = 128


def contract(left, right, left_dim, right_dim):
    return lax.dot_general(
        left,
        right,
        (((left_dim,), (right_dim,)), ((), ())),
        preferred_element_type=jnp.float32,
    )


def owners(width):
    lane = lax.broadcasted_iota(jnp.int32, (COUNT, COUNT * width), 1)
    owner = (lane * (-(-(1 << 20) // width))) >> 20
    device = lax.broadcasted_iota(jnp.int32, (COUNT, COUNT * width), 0)
    return owner == device


def places(width):
    lane = lax.broadcasted_iota(jnp.int32, (PAIR, COUNT * width), 1)
    owner = (lane * (-(-(1 << 20) // width))) >> 20
    entry = lax.broadcasted_iota(jnp.int32, (PAIR, COUNT * width), 0)
    return jnp.where(lane - owner * width == entry, 1.0, 0.0).astype(jnp.bfloat16)


def columns(tile, size=TILE):
    return pl.ds(pl.multiple_of(tile * size, size), size)


class Layer:
    def __init__(self, refs):
        self.__dict__.update(refs)
        self.rows, self.width = self.normed.shape
        self.hidden_width = self.slope.shape[1]

    def spread_small(self):
        for place, width in enumerate(WIDTHS):
            given = self.small[:, place, :].astype(jnp.bfloat16)
            spread = contract(given, places(width), 1, 0)
            row = jnp.sum(jnp.where(owners(width), spread, 0.0), 0, keepdims=True)
            if place == BIAS_IN:
                self.bias_row[:, : self.width] = row[:, : self.width]
                self.bias_row[:, self.width : 2 * self.width] = jnp.zeros_like(row[:, : self.width])
                self.bias_row[:, 2 * self.width :] = row[:, self.width :]
            elif place == BIAS_UP:
                self.up_row[...] = row
            else:
                self.vectors[place : place + 1, :] = row

    def vector(self, place):
        return self.vectors[place : place + 1, :]

    def project(self, tile):
        here = columns(tile)
        value = jnp.dot(
            self.sequence[...], self.weight_in[:, here], preferred_element_type=jnp.float32
        )
        value = (value + self.bias_row[:, here]).astype(jnp.bfloat16)
        scale = jnp.where(tile < self.width // TILE, 0.125, 1.0).astype(jnp.bfloat16)
        self.packed[:, here] = value * scale

    def heads_of(self, step):
        pairs = self.width // PAIR
        batch, pair = step // pairs, step % pairs
        rows = pl.ds(pl.multiple_of(batch * TILE, TILE), TILE)
        return batch, pair, rows

    def block(self, part, rows, pair):
        offset = pl.multiple_of(part * self.width + pair * PAIR, PAIR)
        return self.packed[rows, pl.ds(offset, PAIR)]

    def half(self, value, head):
        lane = lax.broadcasted_iota(jnp.int32, value.shape, 1)
        keep = lane < PAIR // 2 if head == 0 else lane >= PAIR // 2
        return jnp.where(keep, value, jnp.zeros_like(value))

    def attend(self, step):
        batch, pair, rows = self.heads_of(step)
        queries, key_block, value_block = (self.block(part, rows, pair) for part in range(3))
        length = self.lengths[batch]
        lane = lax.broadcasted_iota(jnp.int32, (1, TILE), 1)
        blocked = jnp.where(lane < length, 0.0, -1e30)
        context = []
        for head in range(2):
            scores = contract(self.half(queries, head), key_block, 1, 1) + blocked
            weights = jnp.exp(scores - jnp.max(scores, -1, keepdims=True))
            total = jnp.sum(weights, -1, keepdims=True)
            low = (weights * (1.0 / total)).astype(jnp.bfloat16)
            self.chances[2 * step + head] = low
            context.append(jnp.dot(low, value_block, preferred_element_type=jnp.float32))
        lane = lax.broadcasted_iota(jnp.int32, context[0].shape, 1)
        joined = jnp.where(lane < PAIR // 2, context[0], context[1])
        self.context[rows, columns(pair, PAIR)] = joined.astype(jnp.bfloat16)

    def mix(self, part):
        rows = columns(part)
        branch = jnp.dot(
            self.context[rows, :], self.weight_mix[...], preferred_element_type=jnp.float32
        )
        summed = self.sequence[rows, :].astype(jnp.float32) + (branch + self.vector(BIAS_MIX))
        centered = summed - jnp.mean(summed, -1, keepdims=True)
        factor = lax.rsqrt(jnp.mean(centered * centered, -1, keepdims=True) + epsilon)
        normed = centered * factor
        hidden = normed * self.vector(GAIN_FIRST) + self.vector(SHIFT_FIRST)
        self.normed[rows, :] = normed
        self.factor[rows, :] = factor
        self.hidden_low[rows, :] = hidden.astype(jnp.bfloat16)

    def up(self, tile):
        here = columns(tile)
        value = jnp.dot(
            self.hidden_low[...], self.weight_up[:, here], preferred_element_type=jnp.float32
        )
        value = value + self.up_row[:, here]
        below = 0.5 * (1.0 + lax.erf(value * 0.7071067811865476))
        density = jnp.exp(-0.5 * value * value) * 0.3989422804014327
        self.active[:, here] = (value * below).astype(jnp.bfloat16)
        self.slope[:, here] = (below + value * density).astype(self.slope.dtype)

    def down(self, tile):
        here = columns(tile)
        self.upper[:, here] = jnp.dot(
            self.active[...], self.weight_down[:, here], preferred_element_type=jnp.float32
        )

    def finish(self, part, size=128):
        rows = columns(part, size)
        hidden = self.normed[rows, :] * self.vector(GAIN_FIRST) + self.vector(SHIFT_FIRST)
        summed = hidden + (self.upper[rows, :] + self.vector(BIAS_DOWN))
        centered = summed - jnp.mean(summed, -1, keepdims=True)
        factor = lax.rsqrt(jnp.mean(centered * centered, -1, keepdims=True) + epsilon)
        normed = centered * factor
        gain = self.vector(GAIN_SECOND)
        self.result[rows, :] = (normed * gain + self.vector(SHIFT_SECOND)).astype(jnp.bfloat16)
        upstream = self.upstream[rows, :].astype(jnp.float32)
        grad = self.norm_backward(upstream, normed, factor, gain, GAIN_SECOND, SHIFT_SECOND)
        low = grad.astype(jnp.bfloat16)
        self.upper[rows, :] = grad
        self.feed_grad[rows, :] = low
        self.add_term(BIAS_DOWN, low.astype(jnp.float32))

    def add_term(self, place, value):
        self.terms[place : place + 1, :] += jnp.sum(value, 0, keepdims=True)

    def norm_backward(self, upstream, normed, factor, gain, gain_place, shift_place):
        self.add_term(gain_place, upstream * normed)
        self.add_term(shift_place, upstream)
        scaled = upstream * gain
        return factor * (
            scaled
            - jnp.mean(scaled, -1, keepdims=True)
            - normed * jnp.mean(scaled * normed, -1, keepdims=True)
        )

    def down_weight_grad(self, tile):
        here = columns(tile)
        self.down_grad[here, :] = contract(
            self.active[:, here], self.feed_grad[...], 0, 0
        ).astype(jnp.bfloat16)

    def active_backward(self, tile):
        here = columns(tile)
        grad = contract(self.feed_grad[...], self.weight_down[here, :], 1, 1)
        low = (grad * self.slope[:, here].astype(jnp.float32)).astype(jnp.bfloat16)
        self.preact_grad[:, here] = low
        self.up_terms[:, here] = jnp.sum(low.astype(jnp.float32), 0, keepdims=True)

    def up_weight_grad(self, tile):
        here = columns(tile)
        self.up_grad[:, here] = contract(
            self.hidden_low[...], self.preact_grad[:, here], 0, 0
        ).astype(jnp.bfloat16)

    def hidden_backward(self, tile):
        here = columns(tile)
        self.upper[:, here] += contract(self.preact_grad[...], self.weight_up[here, :], 1, 1)

    def first_backward(self, part, size=128):
        rows = columns(part, size)
        grad = self.norm_backward(
            self.upper[rows, :],
            self.normed[rows, :],
            self.factor[rows, :],
            self.vector(GAIN_FIRST),
            GAIN_FIRST,
            SHIFT_FIRST,
        )
        low = grad.astype(jnp.bfloat16)
        self.upper[rows, :] = grad
        self.feed_grad[rows, :] = low
        self.add_term(BIAS_MIX, low.astype(jnp.float32))

    def mix_weight_grad(self, tile):
        here = columns(tile)
        self.mix_grad[:, here] = contract(
            self.context[...], self.feed_grad[:, here], 0, 0
        ).astype(jnp.bfloat16)

    def mix_backward(self, tile):
        here = columns(tile)
        self.context_grad[:, here] = contract(
            self.feed_grad[...], self.weight_mix[here, :], 1, 1
        ).astype(jnp.bfloat16)

    def attend_backward(self, step):
        batch, pair, rows = self.heads_of(step)
        queries, key_block, value_block = (self.block(part, rows, pair) for part in range(3))
        grads = self.context_grad[rows, columns(pair, PAIR)]
        query_grad = key_grad = value_grad = 0.0
        for head in range(2):
            low = self.chances[2 * step + head]
            chance = low.astype(jnp.float32)
            mine = self.half(grads, head)
            chance_grad = contract(mine, value_block, 1, 1)
            moved = chance_grad - jnp.sum(chance * chance_grad, -1, keepdims=True)
            score_grad = (chance * moved).astype(jnp.bfloat16)
            value_grad += contract(low, mine, 0, 0)
            query_grad += jnp.dot(
                score_grad, self.half(key_block, head), preferred_element_type=jnp.float32
            )
            key_grad += contract(score_grad, self.half(queries, head), 0, 0)
        for part, grad in enumerate((query_grad * 0.125, key_grad, value_grad)):
            offset = pl.multiple_of(part * self.width + pair * PAIR, PAIR)
            self.packed[rows, pl.ds(offset, PAIR)] = grad.astype(jnp.bfloat16)

    def in_weight_grad(self, tile):
        here = columns(tile)
        grads = self.packed[:, here]
        self.in_grad[:, here] = contract(self.sequence[...], grads, 0, 0).astype(jnp.bfloat16)
        self.in_terms[:, here] = jnp.sum(grads.astype(jnp.float32), 0, keepdims=True)

    def input_backward(self, tile):
        here = columns(tile)
        grad = self.upper[:, here] + contract(self.packed[...], self.weight_in[here, :], 1, 1)
        self.input_grad[:, here] = grad.astype(jnp.bfloat16)

    def gather_terms(self):
        for place, width in enumerate(WIDTHS):
            if place == BIAS_IN:
                row = jnp.concatenate(
                    [self.in_terms[:, : self.width], self.in_terms[:, 2 * self.width :]], -1
                )
            elif place == BIAS_UP:
                row = self.up_terms[...]
            else:
                row = self.terms[place : place + 1, :]
            high = row.astype(jnp.bfloat16)
            rest = row - high.astype(jnp.float32)
            middle = rest.astype(jnp.bfloat16)
            low = (rest - middle.astype(jnp.float32)).astype(jnp.bfloat16)
            keep, spots = owners(width), places(width)
            self.small_grad[:, place, :] = sum(
                contract(jnp.where(keep, part.astype(jnp.float32), 0.0).astype(jnp.bfloat16), spots, 1, 1)
                for part in (high, middle, low)
            )


def steps(count, body):
    lax.fori_loop(0, count, lambda step, carry: (body(step), carry)[1], 0)


def layer_kernel(names, *refs):
    layer = Layer(dict(zip(names, refs)))
    tiles, wide = layer.width // TILE, layer.hidden_width // TILE
    pairs = 2 * (layer.width // PAIR)
    layer.terms[...] = jnp.zeros_like(layer.terms)
    layer.spread_small()
    steps(3 * tiles, layer.project)
    steps(pairs, layer.attend)
    steps(layer.rows // TILE, layer.mix)
    steps(wide, layer.up)
    steps(tiles, layer.down)
    steps(layer.rows // 128, layer.finish)
    steps(wide, layer.down_weight_grad)
    steps(wide, layer.active_backward)
    steps(wide, layer.up_weight_grad)
    steps(tiles, layer.hidden_backward)
    steps(layer.rows // 128, layer.first_backward)
    steps(tiles, layer.mix_weight_grad)
    steps(tiles, layer.mix_backward)
    steps(pairs, layer.attend_backward)
    steps(3 * tiles, layer.in_weight_grad)
    steps(tiles, layer.input_backward)
    layer.gather_terms()


def scratch_of(rows, width, hidden_width):
    low, full = jnp.bfloat16, jnp.float32
    return {
        "bias_row": ((1, 3 * width), full),
        "up_row": ((1, hidden_width), full),
        "vectors": ((8, width), full),
        "terms": ((8, width), full),
        "up_terms": ((1, hidden_width), full),
        "in_terms": ((1, 3 * width), full),
        "packed": ((rows, 3 * width), low),
        "chances": ((2 * rows // TILE * width // PAIR, TILE, TILE), low),
        "context": ((rows, width), low),
        "normed": ((rows, width), full),
        "factor": ((rows, 1), full),
        "hidden_low": ((rows, width), low),
        "active": ((rows, hidden_width), low),
        "slope": ((rows, hidden_width), full),
        "upper": ((rows, width), full),
        "feed_grad": ((rows, width), low),
        "preact_grad": ((rows, hidden_width), low),
        "context_grad": ((rows, width), low),
    }


def compute(lengths, sequence, upstream, weight_in, weight_mix, weight_up, weight_down, small):
    rows, width = sequence.shape
    hidden_width = weight_up.shape[1]
    low = jnp.bfloat16
    outs = {
        "result": ((rows, width), low),
        "input_grad": ((rows, width), low),
        "in_grad": (weight_in.shape, low),
        "mix_grad": (weight_mix.shape, low),
        "up_grad": (weight_up.shape, low),
        "down_grad": (weight_down.shape, low),
        "small_grad": (small.shape, jnp.float32),
    }
    scratch = scratch_of(rows, width, hidden_width)
    names = (
        ["lengths", "sequence", "upstream", "weight_in", "weight_mix", "weight_up", "weight_down", "small"]
        + list(outs)
        + list(scratch)
    )
    inside = pl.BlockSpec(memory_space=pltpu.VMEM)
    return pl.pallas_call(
        functools.partial(layer_kernel, names),
        out_shape=[jax.ShapeDtypeStruct(*out) for out in outs.values()],
        in_specs=[pl.BlockSpec(memory_space=pltpu.SMEM)] + [inside] * 7,
        out_specs=[inside] * len(outs),
        scratch_shapes=[pltpu.VMEM(*part) for part in scratch.values()],
        compiler_params=pltpu.CompilerParams(vmem_limit_bytes=62 << 20),
        name="layer",
    )(lengths, sequence, upstream, weight_in, weight_mix, weight_up, weight_down, small)


class Spot:
    def __init__(self):
        self.me = me = lax.axis_index("dp")
        core, column, row, layer = me % 2, (me // 2) % 2, (me // 4) % 2, me // 8
        self.sibling = me + 1 - 2 * core
        across_row = me + 4 * (1 - 2 * row)
        across_column = me + 2 * (1 - 2 * column)
        self.second = (1 - core) * across_row + core * across_column
        self.third = (1 - core) * across_column + core * across_row
        self.lines = [((layer + step) % 4) * 8 + me % 8 for step in range(4)]

    def blocks(self, *partners):
        offsets = [0]
        for partner in partners:
            offsets = offsets + [offset + partner - self.me for offset in offsets]
        return [line + offset for line in self.lines for offset in offsets]


def everyone(me, body):
    lax.fori_loop(1, COUNT, lambda step, carry: (body(lax.rem(me + step, COUNT)), carry)[1], 0)


class Reduction:
    def __init__(self, spot, partial, landing, total, send_sem, land_sems):
        self.spot, self.partial, self.landing, self.total = spot, partial, landing, total
        self.send_sem, self.land_sems = send_sem, land_sems

    def ship(self, stage, blocks, device):
        for place, block in enumerate(blocks):
            remote(
                self.partial.at[block],
                self.landing[stage].at[place],
                self.send_sem,
                self.land_sems.at[stage],
                device,
            ).start()

    def arrive(self, stage):
        here = self.landing[stage]
        remote(here, here, self.send_sem, self.land_sems.at[stage], self.spot.me).wait_recv()

    def add(self, stage, blocks):
        for place, block in enumerate(blocks):
            self.partial[block] = self.partial[block] + self.landing[stage][place]

    def begin(self):
        spot = self.spot
        theirs = [b + spot.sibling - spot.me for b in spot.blocks(spot.third, spot.second)]
        self.ship(0, theirs, spot.sibling)

    def across_third(self):
        spot = self.spot
        self.arrive(0)
        self.add(0, spot.blocks(spot.second, spot.third))
        theirs = [b + spot.third - spot.me for b in spot.blocks(spot.second)]
        self.ship(1, theirs, spot.third)

    def across_second(self):
        spot = self.spot
        self.arrive(1)
        self.add(1, spot.blocks(spot.second))
        theirs = [b + spot.second - spot.me for b in spot.blocks()]
        self.ship(2, theirs, spot.second)

    def along(self):
        spot = self.spot
        self.arrive(2)
        self.add(2, spot.blocks())
        for step in (1, 2, 3):
            remote(
                self.partial.at[spot.lines[step]],
                self.landing[3].at[3 - step],
                self.send_sem,
                self.land_sems.at[3],
                spot.lines[step],
            ).start()

    def end(self):
        self.arrive(3)
        total = self.partial[self.spot.me].astype(jnp.float32)
        for step in range(3):
            total = total + self.landing[3][step].astype(jnp.float32)
        self.total[...] = total

    def drain(self):
        here = self.partial.at[pl.ds(0, COUNT - 1)]
        remote(here, here, self.send_sem, self.land_sems.at[0], self.spot.me).wait_send()


STAGES = (16, 8, 4, 3)


def scatter_kernel(
    order,
    result,
    input_grad,
    small_grad,
    down_grad,
    up_grad,
    mix_grad,
    in_grad,
    layer_out,
    tokens_grad,
    small_total,
    down_total,
    up_total,
    mix_total,
    in_total,
    returned,
    small_landing,
    *rest,
):
    landings, (send_sems, land_sems, exchange_sems, own_sems) = rest[:16], rest[16:]
    spot = Spot()
    me = spot.me
    own = [
        pltpu.make_async_copy(result.at[:, me], returned.at[:, me], own_sems.at[0]),
        pltpu.make_async_copy(input_grad.at[:, me], tokens_grad.at[:, me], own_sems.at[1]),
        pltpu.make_async_copy(small_grad.at[me], small_landing.at[me], own_sems.at[2]),
    ]
    for copy in own:
        copy.start()
    meet_all(me)
    reductions = [
        Reduction(
            spot,
            partial,
            landings[4 * kind : 4 * kind + 4],
            total,
            send_sems.at[3 + kind],
            land_sems.at[kind],
        )
        for kind, (partial, total) in enumerate(
            (
                (down_grad, down_total),
                (up_grad, up_total),
                (mix_grad, mix_total),
                (in_grad, in_total),
            )
        )
    ]

    def give(source, target, which):
        everyone(
            me,
            lambda device: remote(
                source.at[:, device],
                target.at[:, me],
                send_sems.at[which],
                exchange_sems.at[which],
                device,
            ).start(),
        )

    def given(source, target, which):
        others = pl.ds(0, COUNT - 1)
        copy = remote(
            source.at[:, others], target.at[:, others], send_sems.at[which], exchange_sems.at[which], me
        )
        copy.wait_recv()
        copy.wait_send()

    reductions[0].begin()
    give(result, returned, 0)
    for reduction in reductions[1:]:
        reduction.begin()
    give(input_grad, tokens_grad, 1)
    everyone(
        me,
        lambda device: remote(
            small_grad.at[device],
            small_landing.at[me],
            send_sems.at[2],
            exchange_sems.at[2],
            device,
        ).start(),
    )
    for tick in range(len(reductions) + 3):
        for late, stage in enumerate(
            (Reduction.across_third, Reduction.across_second, Reduction.along, Reduction.end)
        ):
            if 0 <= tick - late < len(reductions):
                stage(reductions[tick - late])
    own[0].wait()
    given(result, returned, 0)
    for batch in range(2):
        for seat in range(COUNT):
            layer_out[batch, seat] = returned[batch, order[batch, seat]]
    others = pl.ds(0, COUNT - 1)
    copy = remote(
        small_grad.at[others], small_landing.at[others], send_sems.at[2], exchange_sems.at[2], me
    )
    copy.wait_recv()
    copy.wait_send()
    own[2].wait()
    small_total[...] = jnp.sum(small_landing[...], 0)
    for reduction in reductions:
        reduction.drain()
    given(input_grad, tokens_grad, 1)
    own[1].wait()


def scatter(order, result, input_grad, small_grad, partials):
    anywhere = pl.BlockSpec(memory_space=pl.ANY)
    inside = pl.BlockSpec(memory_space=pltpu.VMEM)
    low, full = jnp.bfloat16, jnp.float32
    return pl.pallas_call(
        scatter_kernel,
        out_shape=[jax.ShapeDtypeStruct(result.shape, low)] * 2
        + [jax.ShapeDtypeStruct(small_grad.shape[1:], full)]
        + [jax.ShapeDtypeStruct(partial.shape[1:], full) for partial in partials],
        in_specs=[pl.BlockSpec(memory_space=pltpu.SMEM)] + [inside] * 7,
        out_specs=[inside, anywhere] + [inside] * 5,
        scratch_shapes=[
            pltpu.VMEM(result.shape, low),
            pltpu.VMEM(small_grad.shape, full),
        ]
        + [
            pltpu.VMEM((stage,) + partial.shape[1:], low)
            for partial in partials
            for stage in STAGES
        ]
        + [
            pltpu.SemaphoreType.DMA((7,)),
            pltpu.SemaphoreType.DMA((4, 4)),
            pltpu.SemaphoreType.DMA((3,)),
            pltpu.SemaphoreType.DMA((3,)),
        ],
        compiler_params=pltpu.CompilerParams(
            collective_id=1, has_side_effects=True, vmem_limit_bytes=60 << 20
        ),
        name="scatter",
    )(order, result, input_grad, small_grad, *partials)


SMALL = (1, 3, 4, 5, 7, 9, 10, 11)
LARGE = (0, 2, 6, 8)


def local(tokens, lengths, order, *rest):
    shards, cotangent = rest[:12], rest[12]
    if lax.axis_size("dp") != COUNT or tokens.shape[2] % 8:
        return portable(tokens, lengths, order, *rest)
    device = lax.axis_index("dp")
    small = jnp.concatenate(
        [jnp.pad(shards[i].astype(jnp.float32), (0, 128 - shards[i].shape[0]))[None] for i in SMALL]
    )
    backward_order = jnp.stack([inverse_of(order[batch]) for batch in range(order.shape[0])])
    sequence, upstream, *full = collect(
        backward_order, tokens, cotangent, [shards[i] for i in LARGE] + [small]
    )
    width = tokens.shape[-1]
    result, input_grad, in_grad, mix_grad, up_grad, down_grad, small_grad = compute(
        lax.dynamic_index_in_dim(lengths, device, 1, keepdims=False),
        sequence.reshape(-1, width),
        upstream.reshape(-1, width),
        *[part.reshape(-1, part.shape[-1]) for part in full[:4]],
        full[4],
    )
    layer_out, tokens_grad, small_total, *totals = scatter(
        order,
        result.reshape(tokens.shape),
        input_grad.reshape(tokens.shape),
        small_grad,
        [
            part.reshape(COUNT, -1, part.shape[-1])
            for part in (down_grad, up_grad, mix_grad, in_grad)
        ],
    )
    outputs = [None] * 12
    for i, total in zip((8, 6, 2, 0), totals):
        outputs[i] = total
    for place, i in enumerate(SMALL):
        outputs[i] = small_total[place, : shards[i].shape[0]]
    return (layer_out, tokens_grad, *outputs)


def solution(mesh):
    return jax.shard_map(
        local,
        mesh=mesh,
        in_specs=(
            P(None, None, "dp", None),
            P(),
            P(),
            P("dp", None),
            P("dp"),
            P("dp", None),
            P("dp"),
            P("dp"),
            P("dp"),
            P("dp", None),
            P("dp"),
            P("dp", None),
            P("dp"),
            P("dp"),
            P("dp"),
            P(None, None, "dp", None),
        ),
        out_specs=(
            P(None, None, "dp", None),
            P(None, None, "dp", None),
            P("dp", None),
            P("dp"),
            P("dp", None),
            P("dp"),
            P("dp"),
            P("dp"),
            P("dp", None),
            P("dp"),
            P("dp", None),
            P("dp"),
            P("dp"),
            P("dp"),
        ),
        check_vma=False,
    )
```

```python
import functools
import types

import jax
import jax.numpy as jnp
from jax import lax
from jax.experimental import pallas as pl
from jax.experimental.pallas import tpu as pltpu
from jax.sharding import PartitionSpec as P

MESH = pl.DeviceIdType.MESH

HD = 64


epsilon = 1e-12


def matmul(left, right):
    return jnp.dot(left, right, preferred_element_type=jnp.float32)


def rows_product(left, right):
    return lax.dot_general(
        left, right, (((0,), (0,)), ((), ())), preferred_element_type=jnp.float32
    )


def right_transposed(left, right):
    return lax.dot_general(
        left, right, (((1,), (1,)), ((), ())), preferred_element_type=jnp.float32
    )


def split_heads(block, heads):
    return block.reshape(block.shape[0], heads, -1).transpose(1, 0, 2)


def join_heads(block):
    return block.transpose(1, 0, 2).reshape(block.shape[1], -1)


def norm_forward(summed, norm_gain, norm_shift):
    row_mean = jnp.mean(summed, -1, keepdims=True)
    centered = summed - row_mean
    reciprocal = lax.rsqrt(jnp.mean(centered * centered, -1, keepdims=True) + epsilon)
    normed = centered * reciprocal
    return (normed * norm_gain + norm_shift, normed, reciprocal)


def norm_backward(upstream, normed, reciprocal, norm_gain):
    scaled = upstream * norm_gain
    summed_grad = reciprocal * (
        scaled
        - jnp.mean(scaled, -1, keepdims=True)
        - normed * jnp.mean(scaled * normed, -1, keepdims=True)
    )
    return (summed_grad, jnp.sum(upstream * normed, 0), jnp.sum(upstream, 0))


def head_scores(head_query, head_keys, valid):
    scores = right_transposed(head_query, head_keys) * 0.125
    return jnp.where(valid[None, :], scores, -1e30)


def attend_forward(packed, valid):
    head_query, head_keys, head_values = packed
    scores = head_scores(head_query, head_keys, valid)
    row_max = jnp.max(scores, -1, keepdims=True)
    weights_raw = jnp.exp(scores - row_max)
    row_sum = jnp.sum(weights_raw, -1, keepdims=True)
    probability = weights_raw / row_sum
    context = matmul(probability.astype(jnp.bfloat16), head_values)
    return (context, (row_max + jnp.log(row_sum))[:, 0])


def attend_backward(packed, valid):
    head_query, head_keys, head_values, context_grad, log_total = packed
    scores = head_scores(head_query, head_keys, valid)
    probability = jnp.exp(scores - log_total[:, None])
    low_prob = probability.astype(jnp.bfloat16)
    prob_grad = right_transposed(context_grad, head_values)
    value_grad = rows_product(low_prob, context_grad)
    shifted = prob_grad - jnp.sum(probability * prob_grad, -1, keepdims=True)
    score_grad = (probability * shifted).astype(jnp.bfloat16)
    query_grad = matmul(score_grad, head_keys) * 0.125
    key_grad = rows_product(score_grad, head_query) * 0.125
    return (query_grad, key_grad, value_grad)


def forward(weights, sequence, length):
    (
        weight_in,
        bias_in,
        weight_mix,
        bias_mix,
        gain_first,
        shift_first,
        weight_up,
        bias_up,
        weight_down,
        bias_down,
        gain_second,
        shift_second,
    ) = weights
    width = sequence.shape[1]
    heads = width // HD
    valid = jnp.arange(sequence.shape[0], dtype=jnp.int32) < length
    bias_full = jnp.concatenate(
        [
            bias_in[:width].astype(jnp.float32),
            jnp.zeros((width,), jnp.float32),
            bias_in[width:].astype(jnp.float32),
        ]
    )
    projected = (matmul(sequence, weight_in) + bias_full).astype(jnp.bfloat16)
    queries = split_heads(projected[:, :width], heads)
    key_heads = split_heads(projected[:, width : 2 * width], heads)
    value_heads = split_heads(projected[:, 2 * width :], heads)
    context, log_total = lax.map(
        lambda packed: attend_forward(packed, valid), (queries, key_heads, value_heads)
    )
    context_low = join_heads(context).astype(jnp.bfloat16)
    branch = matmul(context_low, weight_mix) + bias_mix.astype(jnp.float32)
    hidden, normed_first, recip_first = norm_forward(
        sequence.astype(jnp.float32) + branch,
        gain_first.astype(jnp.float32),
        shift_first.astype(jnp.float32),
    )
    hidden_low = hidden.astype(jnp.bfloat16)
    preact = matmul(hidden_low, weight_up) + bias_up.astype(jnp.float32)
    activated = jax.nn.gelu(preact, approximate=False).astype(jnp.bfloat16)
    feed_out = matmul(activated, weight_down) + bias_down.astype(jnp.float32)
    result, normed_second, recip_second = norm_forward(
        hidden + feed_out, gain_second.astype(jnp.float32), shift_second.astype(jnp.float32)
    )
    stored = (
        valid,
        queries,
        key_heads,
        value_heads,
        log_total,
        context_low,
        normed_first,
        recip_first,
        hidden_low,
        preact,
        activated,
        normed_second,
        recip_second,
    )
    return (result.astype(jnp.bfloat16), stored)


def backward(weights, sequence, upstream_low, stored):
    (
        weight_in,
        bias_in,
        weight_mix,
        bias_mix,
        gain_first,
        shift_first,
        weight_up,
        bias_up,
        weight_down,
        bias_down,
        gain_second,
        shift_second,
    ) = weights
    (
        valid,
        queries,
        key_heads,
        value_heads,
        log_total,
        context_low,
        normed_first,
        recip_first,
        hidden_low,
        preact,
        activated,
        normed_second,
        recip_second,
    ) = stored
    width = sequence.shape[1]
    heads = width // HD
    upstream = upstream_low.astype(jnp.float32)
    second_grad, gain_second_grad, shift_second_grad = norm_backward(
        upstream, normed_second, recip_second, gain_second.astype(jnp.float32)
    )
    feed_grad = second_grad.astype(jnp.bfloat16)
    bias_down_grad = jnp.sum(feed_grad.astype(jnp.float32), 0)
    weight_down_grad = rows_product(activated, feed_grad)
    act_grad = right_transposed(feed_grad, weight_down)
    slope = (
        0.5 * (1.0 + jax.scipy.special.erf(preact * 0.7071067811865476))
        + preact * jnp.exp(-0.5 * preact * preact) * 0.3989422804014327
    )
    preact_grad = (act_grad * slope).astype(jnp.bfloat16)
    bias_up_grad = jnp.sum(preact_grad.astype(jnp.float32), 0)
    weight_up_grad = rows_product(hidden_low, preact_grad)
    hidden_grad = second_grad + right_transposed(preact_grad, weight_up)
    first_grad, gain_first_grad, shift_first_grad = norm_backward(
        hidden_grad, normed_first, recip_first, gain_first.astype(jnp.float32)
    )
    branch_grad = first_grad.astype(jnp.bfloat16)
    bias_mix_grad = jnp.sum(branch_grad.astype(jnp.float32), 0)
    weight_mix_grad = rows_product(context_low, branch_grad)
    context_grad = right_transposed(branch_grad, weight_mix).astype(jnp.bfloat16)
    query_grad, key_grad, value_grad = lax.map(
        lambda packed: attend_backward(packed, valid),
        (queries, key_heads, value_heads, split_heads(context_grad, heads), log_total),
    )
    projected_grad = jnp.concatenate(
        [join_heads(query_grad), join_heads(key_grad), join_heads(value_grad)], -1
    ).astype(jnp.bfloat16)
    column_sums = jnp.sum(projected_grad.astype(jnp.float32), 0)
    bias_in_grad = jnp.concatenate([column_sums[:width], column_sums[2 * width :]])
    weight_in_grad = rows_product(sequence, projected_grad)
    input_grad = (first_grad + right_transposed(projected_grad, weight_in)).astype(jnp.bfloat16)
    gradients = (
        weight_in_grad,
        bias_in_grad,
        weight_mix_grad,
        bias_mix_grad,
        gain_first_grad,
        shift_first_grad,
        weight_up_grad,
        bias_up_grad,
        weight_down_grad,
        bias_down_grad,
        gain_second_grad,
        shift_second_grad,
    )
    return (input_grad, gradients)


def permuted(blocks, picks):
    chosen = (picks[:, None] == jnp.arange(picks.shape[0])[None, :]).astype(blocks.dtype)
    flat = blocks.reshape(blocks.shape[0], -1)
    return matmul(chosen, flat).astype(blocks.dtype).reshape(blocks.shape)


def inverse_of(picks):
    slots = jnp.arange(picks.shape[0], dtype=jnp.int32)
    return jnp.sum(jnp.where(picks[:, None] == slots[None, :], slots[:, None], 0), 0)


def fetch_weights(shards):
    return (
        lax.all_gather(shards[0], "dp", axis=0, tiled=True),
        lax.all_gather(shards[1], "dp", axis=0, tiled=True),
        lax.all_gather(shards[2], "dp", axis=0, tiled=True),
        lax.all_gather(shards[3], "dp", axis=0, tiled=True),
        lax.all_gather(shards[4], "dp", axis=0, tiled=True),
        lax.all_gather(shards[5], "dp", axis=0, tiled=True),
        lax.all_gather(shards[6], "dp", axis=0, tiled=True),
        lax.all_gather(shards[7], "dp", axis=0, tiled=True),
        lax.all_gather(shards[8], "dp", axis=0, tiled=True),
        lax.all_gather(shards[9], "dp", axis=0, tiled=True),
        lax.all_gather(shards[10], "dp", axis=0, tiled=True),
        lax.all_gather(shards[11], "dp", axis=0, tiled=True),
    )


def add_trees(first, second):
    if first is None:
        return second
    return jax.tree.map(lambda left, right: left + right, first, second)


def portable(
    tokens,
    lengths,
    order,
    weight_in,
    bias_in,
    weight_mix,
    bias_mix,
    gain_first,
    shift_first,
    weight_up,
    bias_up,
    weight_down,
    bias_down,
    gain_second,
    shift_second,
    cotangent,
):
    shards = (
        weight_in,
        bias_in,
        weight_mix,
        bias_mix,
        gain_first,
        shift_first,
        weight_up,
        bias_up,
        weight_down,
        bias_down,
        gain_second,
        shift_second,
    )
    device = lax.axis_index("dp")
    totals = None
    outputs_list = []
    grads_list = []
    for batch in range(tokens.shape[0]):
        current = fetch_weights(shards)
        picks = order[batch]
        dealt_tokens = permuted(tokens[batch], picks)
        sequence, upstream = (
            lax.all_to_all(dealt_tokens, "dp", split_axis=0, concat_axis=1, tiled=True),
            lax.all_to_all(cotangent[batch], "dp", split_axis=0, concat_axis=1, tiled=True),
        )
        length = jnp.sum(jnp.where(jnp.arange(picks.shape[0]) == picks[device], lengths[batch], 0))
        result, stored = forward(current, sequence[0], length)
        behind = (
            lax.all_gather(shards[0], "dp", axis=0, tiled=True),
            lax.all_gather(shards[1], "dp", axis=0, tiled=True),
            lax.all_gather(shards[2], "dp", axis=0, tiled=True),
            lax.all_gather(shards[3], "dp", axis=0, tiled=True),
            lax.all_gather(shards[4], "dp", axis=0, tiled=True),
            lax.all_gather(shards[5], "dp", axis=0, tiled=True),
            lax.all_gather(shards[6], "dp", axis=0, tiled=True),
            lax.all_gather(shards[7], "dp", axis=0, tiled=True),
            lax.all_gather(shards[8], "dp", axis=0, tiled=True),
            lax.all_gather(shards[9], "dp", axis=0, tiled=True),
            lax.all_gather(shards[10], "dp", axis=0, tiled=True),
            lax.all_gather(shards[11], "dp", axis=0, tiled=True),
        )
        input_grad, gradients = backward(behind, sequence[0], upstream[0], stored)
        back_out, back_grad = (
            lax.all_to_all(result[None], "dp", split_axis=1, concat_axis=0, tiled=True),
            lax.all_to_all(input_grad[None], "dp", split_axis=1, concat_axis=0, tiled=True),
        )
        restored = permuted(back_grad, inverse_of(picks))
        outputs_list.append(back_out)
        grads_list.append(restored)
        totals = add_trees(totals, gradients)
    totals = (
        lax.psum_scatter(totals[0], "dp", scatter_dimension=0, tiled=True),
        lax.psum_scatter(totals[1], "dp", scatter_dimension=0, tiled=True),
        lax.psum_scatter(totals[2], "dp", scatter_dimension=0, tiled=True),
        lax.psum_scatter(totals[3], "dp", scatter_dimension=0, tiled=True),
        lax.psum_scatter(totals[4], "dp", scatter_dimension=0, tiled=True),
        lax.psum_scatter(totals[5], "dp", scatter_dimension=0, tiled=True),
        lax.psum_scatter(totals[6], "dp", scatter_dimension=0, tiled=True),
        lax.psum_scatter(totals[7], "dp", scatter_dimension=0, tiled=True),
        lax.psum_scatter(totals[8], "dp", scatter_dimension=0, tiled=True),
        lax.psum_scatter(totals[9], "dp", scatter_dimension=0, tiled=True),
        lax.psum_scatter(totals[10], "dp", scatter_dimension=0, tiled=True),
        lax.psum_scatter(totals[11], "dp", scatter_dimension=0, tiled=True),
    )
    return (
        jnp.stack(outputs_list),
        jnp.stack(grads_list),
        totals[0],
        totals[1],
        totals[2],
        totals[3],
        totals[4],
        totals[5],
        totals[6],
        totals[7],
        totals[8],
        totals[9],
        totals[10],
        totals[11],
    )


COUNT = 32
ROWS, LAYERS = 8, 4


def meet_all(me):
    barrier = pltpu.get_barrier_semaphore()

    def greet(step, carry):
        pl.semaphore_signal(
            barrier, inc=1, device_id=(lax.rem(me + step, COUNT),), device_id_type=MESH
        )
        return carry

    lax.fori_loop(1, COUNT, greet, 0)
    pl.semaphore_wait(barrier, COUNT - 1)


def remote(source, target, send_sem, recv_sem, device):
    return pltpu.make_async_remote_copy(
        src_ref=source,
        dst_ref=target,
        send_sem=send_sem,
        recv_sem=recv_sem,
        device_id=(device,),
        device_id_type=MESH,
    )


WIDTHS = (48, 24, 24, 24, 96, 24, 24, 24)
BIAS_IN, BIAS_MIX, GAIN_FIRST, SHIFT_FIRST, BIAS_UP, BIAS_DOWN, GAIN_SECOND, SHIFT_SECOND = range(8)
TILE = 256
PAIR = 128


def contract(left, right, left_dim, right_dim):
    return lax.dot_general(
        left,
        right,
        (((left_dim,), (right_dim,)), ((), ())),
        preferred_element_type=jnp.float32,
    )


def owners(width):
    lane = lax.broadcasted_iota(jnp.int32, (COUNT, COUNT * width), 1)
    owner = (lane * (-(-(1 << 20) // width))) >> 20
    device = lax.broadcasted_iota(jnp.int32, (COUNT, COUNT * width), 0)
    return owner == device


def places(width):
    lane = lax.broadcasted_iota(jnp.int32, (PAIR, COUNT * width), 1)
    owner = (lane * (-(-(1 << 20) // width))) >> 20
    entry = lax.broadcasted_iota(jnp.int32, (PAIR, COUNT * width), 0)
    return jnp.where(lane - owner * width == entry, 1.0, 0.0).astype(jnp.bfloat16)


def columns(tile, size=TILE):
    return pl.ds(pl.multiple_of(tile * size, size), size)


def flat(value):
    return value.reshape(-1, value.shape[-1])


def take_rows(ref, start, stop):
    layers, seats, groups, small, _ = ref.shape
    pieces = []
    while start < stop:
        layer, rest = divmod(start // small, seats * groups)
        seat, group = divmod(rest, groups)
        whole = min((stop - start) // (small * groups), seats - seat)
        if group == 0 and whole:
            pieces.append(flat(ref[layer, seat : seat + whole]))
            start += whole * groups * small
        else:
            end = min(groups, group + (stop - start) // small)
            pieces.append(flat(ref[layer, seat, group:end]))
            start += (end - group) * small
    return jnp.concatenate(pieces, 0)


class Layer:
    def __init__(self, refs):
        self.__dict__.update(refs)
        self.rows, self.width = self.normed.shape
        self.hidden_width = self.slope.shape[1]

    def spread_small(self):
        for place, width in enumerate(WIDTHS):
            given = self.small[:, place, :].astype(jnp.bfloat16)
            spread = contract(given, places(width), 1, 0)
            row = jnp.sum(jnp.where(owners(width), spread, 0.0), 0, keepdims=True)
            if place == BIAS_IN:
                self.bias_row[:, : self.width] = row[:, : self.width]
                self.bias_row[:, self.width : 2 * self.width] = jnp.zeros_like(row[:, : self.width])
                self.bias_row[:, 2 * self.width :] = row[:, self.width :]
            elif place == BIAS_UP:
                self.up_row[...] = row
            else:
                self.vectors[place : place + 1, :] = row

    def vector(self, place):
        return self.vectors[place : place + 1, :]

    def project(self, tile):
        here = columns(tile)
        value = jnp.dot(
            flat(self.sequence[...]),
            flat(self.weight_in[:, :, :, :, here]),
            preferred_element_type=jnp.float32
        )
        value = (value + self.bias_row[:, here]).astype(jnp.bfloat16)
        scale = jnp.where(tile < self.width // TILE, 0.125, 1.0).astype(jnp.bfloat16)
        self.packed[:, here] = value * scale

    def heads_of(self, step):
        pairs = self.width // PAIR
        batch, pair = step // pairs, step % pairs
        rows = pl.ds(pl.multiple_of(batch * TILE, TILE), TILE)
        return batch, pair, rows

    def block(self, part, rows, pair):
        offset = pl.multiple_of(part * self.width + pair * PAIR, PAIR)
        return self.packed[rows, pl.ds(offset, PAIR)]

    def half(self, value, head):
        lane = lax.broadcasted_iota(jnp.int32, value.shape, 1)
        keep = lane < PAIR // 2 if head == 0 else lane >= PAIR // 2
        return jnp.where(keep, value, jnp.zeros_like(value))

    def attend(self, step):
        batch, pair, rows = self.heads_of(step)
        queries, key_block, value_block = (self.block(part, rows, pair) for part in range(3))
        length = jnp.where(batch == 0, self.lengths[0], self.lengths[1])
        lane = lax.broadcasted_iota(jnp.int32, (1, TILE), 1)
        blocked = jnp.where(lane < length, 0.0, -1e30)
        context = []
        for head in range(2):
            scores = contract(self.half(queries, head), key_block, 1, 1) + blocked
            weights = jnp.exp(scores - jnp.max(scores, -1, keepdims=True))
            total = jnp.sum(weights, -1, keepdims=True)
            low = (weights * (1.0 / total)).astype(jnp.bfloat16)
            self.chances[2 * step + head] = low
            context.append(jnp.dot(low, value_block, preferred_element_type=jnp.float32))
        lane = lax.broadcasted_iota(jnp.int32, context[0].shape, 1)
        joined = jnp.where(lane < PAIR // 2, context[0], context[1])
        self.context[rows, columns(pair, PAIR)] = joined.astype(jnp.bfloat16)

    def mix(self, part):
        rows = columns(part)
        branch = jnp.dot(
            self.context[rows, :], flat(self.weight_mix[...]), preferred_element_type=jnp.float32
        )
        summed = flat(self.sequence[part]).astype(jnp.float32) + (branch + self.vector(BIAS_MIX))
        centered = summed - jnp.mean(summed, -1, keepdims=True)
        factor = lax.rsqrt(jnp.mean(centered * centered, -1, keepdims=True) + epsilon)
        normed = centered * factor
        hidden = normed * self.vector(GAIN_FIRST) + self.vector(SHIFT_FIRST)
        self.normed[rows, :] = normed
        self.factor[rows, :] = factor
        self.hidden_low[rows, :] = hidden.astype(jnp.bfloat16)

    def up(self, tile):
        here = columns(tile)
        value = jnp.dot(
            self.hidden_low[...], flat(self.weight_up[:, :, :, :, here]), preferred_element_type=jnp.float32
        )
        value = value + self.up_row[:, here]
        below = 0.5 * (1.0 + lax.erf(value * 0.7071067811865476))
        density = jnp.exp(-0.5 * value * value) * 0.3989422804014327
        self.active[:, here] = (value * below).astype(jnp.bfloat16)
        self.slope[:, here] = (below + value * density).astype(self.slope.dtype)

    def down(self, tile):
        here = columns(tile)
        self.upper[:, here] = jnp.dot(
            self.active[...], flat(self.weight_down[:, :, :, :, here]), preferred_element_type=jnp.float32
        )

    def finish(self, part, size=128):
        rows = columns(part, size)
        hidden = self.normed[rows, :] * self.vector(GAIN_FIRST) + self.vector(SHIFT_FIRST)
        summed = hidden + (self.upper[rows, :] + self.vector(BIAS_DOWN))
        centered = summed - jnp.mean(summed, -1, keepdims=True)
        factor = lax.rsqrt(jnp.mean(centered * centered, -1, keepdims=True) + epsilon)
        normed = centered * factor
        gain = self.vector(GAIN_SECOND)
        low = (normed * gain + self.vector(SHIFT_SECOND)).astype(jnp.bfloat16)
        parts, seats = TILE // size, size // 8
        batch, span = part // parts, pl.ds((part % parts) * seats, seats)
        self.result[batch, span] = low.reshape(seats, 8, self.width)
        upstream = flat(self.upstream[batch, span]).astype(jnp.float32)
        grad = self.norm_backward(upstream, normed, factor, gain, GAIN_SECOND, SHIFT_SECOND)
        low = grad.astype(jnp.bfloat16)
        self.upper[rows, :] = grad
        self.feed_grad[rows, :] = low
        self.add_term(BIAS_DOWN, low.astype(jnp.float32))

    def add_term(self, place, value):
        self.terms[place : place + 1, :] += jnp.sum(value, 0, keepdims=True)

    def norm_backward(self, upstream, normed, factor, gain, gain_place, shift_place):
        self.add_term(gain_place, upstream * normed)
        self.add_term(shift_place, upstream)
        scaled = upstream * gain
        return factor * (
            scaled
            - jnp.mean(scaled, -1, keepdims=True)
            - normed * jnp.mean(scaled * normed, -1, keepdims=True)
        )

    def down_weight_grad(self, layer):
        span = self.hidden_width // LAYERS
        made = [
            contract(self.active[:, columns(layer * (span // TILE) + i)], self.feed_grad[...], 0, 0)
            for i in range(span // TILE)
        ]
        made = jnp.concatenate([part.astype(jnp.bfloat16) for part in made], 0)
        self.down_grad[layer] = made.reshape(self.down_grad.shape[1:])

    def active_backward(self, layer):
        span = self.hidden_width // LAYERS
        weight = flat(self.weight_down[layer])
        for i in range(span // TILE):
            here = columns(layer * (span // TILE) + i)
            grad = contract(self.feed_grad[...], weight[i * TILE : (i + 1) * TILE], 1, 1)
            low = (grad * self.slope[:, here].astype(jnp.float32)).astype(jnp.bfloat16)
            self.preact_grad[:, here] = low
            self.up_terms[:, here] = jnp.sum(low.astype(jnp.float32), 0, keepdims=True)

    def up_weight_grad(self, tile):
        here = columns(tile)
        grad = contract(self.hidden_low[...], self.preact_grad[:, here], 0, 0)
        self.keep_columns(self.up_grad, here, grad)

    def hidden_backward(self, tile):
        here = columns(tile)
        weight = take_rows(self.weight_up, tile * TILE, (tile + 1) * TILE)
        self.upper[:, here] += contract(self.preact_grad[...], weight, 1, 1)

    def first_backward(self, part, size=128):
        rows = columns(part, size)
        grad = self.norm_backward(
            self.upper[rows, :],
            self.normed[rows, :],
            self.factor[rows, :],
            self.vector(GAIN_FIRST),
            GAIN_FIRST,
            SHIFT_FIRST,
        )
        low = grad.astype(jnp.bfloat16)
        self.upper[rows, :] = grad
        self.feed_grad[rows, :] = low
        self.add_term(BIAS_MIX, low.astype(jnp.float32))

    def mix_weight_grad(self, tile):
        here = columns(tile)
        grad = contract(self.context[...], self.feed_grad[:, here], 0, 0)
        self.keep_columns(self.mix_grad, here, grad)

    def mix_backward(self, tile):
        here = columns(tile)
        weight = take_rows(self.weight_mix, tile * TILE, (tile + 1) * TILE)
        self.context_grad[:, here] = contract(self.feed_grad[...], weight, 1, 1).astype(
            jnp.bfloat16
        )

    def attend_backward(self, step):
        batch, pair, rows = self.heads_of(step)
        queries, key_block, value_block = (self.block(part, rows, pair) for part in range(3))
        grads = self.context_grad[rows, columns(pair, PAIR)]
        query_grad = key_grad = value_grad = 0.0
        for head in range(2):
            low = self.chances[2 * step + head]
            chance = low.astype(jnp.float32)
            mine = self.half(grads, head)
            chance_grad = contract(mine, value_block, 1, 1)
            moved = chance_grad - jnp.sum(chance * chance_grad, -1, keepdims=True)
            score_grad = (chance * moved).astype(jnp.bfloat16)
            value_grad += contract(low, mine, 0, 0)
            query_grad += jnp.dot(
                score_grad, self.half(key_block, head), preferred_element_type=jnp.float32
            )
            key_grad += contract(score_grad, self.half(queries, head), 0, 0)
        for part, grad in enumerate((query_grad * 0.125, key_grad, value_grad)):
            offset = pl.multiple_of(part * self.width + pair * PAIR, PAIR)
            self.packed[rows, pl.ds(offset, PAIR)] = grad.astype(jnp.bfloat16)

    def in_weight_grad(self, tile):
        here = columns(tile)
        grads = self.packed[:, here]
        self.keep_columns(self.in_grad, here, contract(flat(self.sequence[...]), grads, 0, 0))
        self.in_terms[:, here] = jnp.sum(grads.astype(jnp.float32), 0, keepdims=True)

    def input_backward(self, tile):
        here = columns(tile)
        weight = take_rows(self.weight_in, tile * TILE, (tile + 1) * TILE)
        grad = self.upper[:, here] + contract(self.packed[...], weight, 1, 1)
        shape = self.input_grad.shape[:3] + (TILE,)
        self.input_grad[:, :, :, here] = grad.astype(jnp.bfloat16).reshape(shape)

    def keep_columns(self, ref, here, grad):
        ref[:, :, :, :, here] = grad.astype(jnp.bfloat16).reshape(ref.shape[:4] + (TILE,))

    def gather_terms(self):
        for place, width in enumerate(WIDTHS):
            if place == BIAS_IN:
                row = jnp.concatenate(
                    [self.in_terms[:, : self.width], self.in_terms[:, 2 * self.width :]], -1
                )
            elif place == BIAS_UP:
                row = self.up_terms[...]
            else:
                row = self.terms[place : place + 1, :]
            high = row.astype(jnp.bfloat16)
            rest = row - high.astype(jnp.float32)
            middle = rest.astype(jnp.bfloat16)
            low = (rest - middle.astype(jnp.float32)).astype(jnp.bfloat16)
            keep, spots = owners(width), places(width)
            self.small_grad[:, place, :] = sum(
                contract(jnp.where(keep, part.astype(jnp.float32), 0.0).astype(jnp.bfloat16), spots, 1, 1)
                for part in (high, middle, low)
            )


def scratch_of(rows, width, hidden_width):
    low, full = jnp.bfloat16, jnp.float32
    return dict(
        bias_row=pltpu.VMEM((1, 3 * width), full),
        up_row=pltpu.VMEM((1, hidden_width), full),
        vectors=pltpu.VMEM((8, width), full),
        terms=pltpu.VMEM((8, width), full),
        up_terms=pltpu.VMEM((1, hidden_width), full),
        in_terms=pltpu.VMEM((1, 3 * width), full),
        packed=pltpu.VMEM((rows, 3 * width), low),
        chances=pltpu.VMEM((2 * rows // TILE * width // PAIR, TILE, TILE), low),
        context=pltpu.VMEM((rows, width), low),
        normed=pltpu.VMEM((rows, width), full),
        factor=pltpu.VMEM((rows, 1), full),
        hidden_low=pltpu.VMEM((rows, width), low),
        active=pltpu.VMEM((rows, hidden_width), low),
        slope=pltpu.VMEM((rows, hidden_width), low),
        upper=pltpu.VMEM((rows, width), full),
        feed_grad=pltpu.VMEM((rows, width), low),
    )


class Spot:
    def __init__(self):
        self.me = me = lax.axis_index("dp")
        core, column, row = me % 2, (me // 2) % 2, (me // 4) % 2
        self.layer, self.seat = me // 8, me % 8
        self.to_sibling = 1 - 2 * core
        across_row = 4 * (1 - 2 * row)
        across_column = 2 * (1 - 2 * column)
        self.to_second = (1 - core) * across_row + core * across_column
        self.to_third = (1 - core) * across_column + core * across_row
        self.sibling = me + self.to_sibling
        self.second = me + self.to_second
        self.third = me + self.to_third
        self.above = [lax.rem(self.layer + step, LAYERS) for step in (1, 2, 3)]


class Chunk:
    def __init__(self, kind, groups, cols):
        self.kind, self.groups, self.cols = kind, groups, cols

    def line(self, refs, seat):
        return refs[self.kind].at[:, seat, self.groups, :, self.cols]

    def block(self, refs, layer, seat):
        return refs[self.kind].at[layer, seat, self.groups, :, self.cols]

    def bulk(self, refs, layers, lines):
        return refs[self.kind].at[pl.ds(0, layers), pl.ds(0, lines), self.groups, :, self.cols]


def chunks_of(shapes):
    made = []
    for kind, (groups, _, width) in enumerate(shapes):
        if kind < 3:
            size = shapes[1][2]
            for start in range(0, width, size):
                made.append(Chunk(kind, pl.ds(0, groups), pl.ds(start, size)))
        else:
            size = shapes[0][0]
            for start in range(0, groups, size):
                made.append(Chunk(kind, pl.ds(start, size), pl.ds(0, width)))
    return made


class Traffic:
    def __init__(self, spot, refs):
        self.spot = spot
        self.__dict__.update(refs)
        self.chunks = chunks_of([tuple(shard.shape) for shard in self.shards])


    def own(self, k):
        chunk, spot = self.chunks[k], self.spot
        source = self.shards[chunk.kind].at[chunk.groups, :, chunk.cols]
        target = chunk.block(self.full, spot.layer, spot.seat)
        for layer in spot.above:
            remote(
                source, target, self.sent.at[k], self.along_in.at[k], layer * ROWS + spot.seat
            ).start()

    def line_out(self, k, seat, device, sem):
        line = self.chunks[k].line(self.full, seat)
        remote(line, line, self.sent.at[k], sem, device).start()

    def wait_lines(self, k, sem, count=1):
        chunk = self.chunks[k]
        here = chunk.bulk(self.full, 3 if count == 3 else LAYERS, 1 if count == 3 else count)
        return remote(here, here, self.sent.at[k], sem, self.spot.me)

    def from_line(self, k):
        spot = self.spot
        self.wait_lines(k, self.along_in.at[k], 3).wait_recv()
        self.line_out(k, spot.seat, spot.second, self.second_in.at[k])
        self.line_out(k, spot.seat, spot.third, self.third_in.at[k, 0])
        self.line_out(k, spot.seat, spot.sibling, self.sibling_in.at[k])

    def from_second(self, k):
        spot = self.spot
        self.wait_lines(k, self.second_in.at[k]).wait_recv()
        seat = spot.seat + spot.to_second
        self.line_out(k, seat, spot.third, self.third_in.at[k, 1])
        self.line_out(k, seat, spot.sibling, self.sibling_in.at[k])

    def from_third(self, k, which):
        spot = self.spot
        self.wait_lines(k, self.third_in.at[k, which]).wait_recv()
        seat = spot.seat + spot.to_third + which * spot.to_second
        self.line_out(k, seat, spot.sibling, self.sibling_in.at[k])

    def complete(self, k):
        self.wait_lines(k, self.sibling_in.at[k], 4).wait_recv()

    def own_sent(self, k):
        self.wait_lines(k, self.sent.at[k], 7).wait_send()
        self.wait_lines(k, self.sent.at[k], 3).wait_send()


    def exchange(self, source, target, which, first=0, last=COUNT - 1):
        me = self.spot.me

        def go(step, carry):
            device = lax.rem(me + lax.rem(step * 5, COUNT), COUNT)
            remote(
                source.at[:, device],
                target.at[:, me],
                self.given.at[which],
                self.taken.at[which],
                device,
            ).start()
            return carry

        lax.fori_loop(1 + first, 1 + last, go, 0)

    def exchanged(self, target, which):
        here = target.at[:, pl.ds(0, COUNT - 1)]
        return remote(
            here,
            here,
            self.given.at[which],
            self.taken.at[which],
            self.spot.me,
        )

    def exchange_small(self, source, target, which):
        me = self.spot.me

        def go(step, carry):
            device = lax.rem(me + step, COUNT)
            remote(
                source if which == 4 else source.at[device],
                target.at[me],
                self.given.at[which],
                self.taken.at[which],
                device,
            ).start()
            return carry

        lax.fori_loop(1, COUNT, go, 0)

    def exchanged_small(self, target, which):
        here = target.at[pl.ds(0, COUNT - 1)]
        return remote(here, here, self.given.at[which], self.taken.at[which], self.spot.me)


    def move(self, k, seat, landing, device, sem):
        remote(
            self.chunks[k].line(self.partial, seat), landing, self.shed.at[k], sem, device
        ).start()

    def landing(self, k, landings, slot):
        chunk = self.chunks[k]
        return landings[chunk.kind].at[slot, :, chunk.groups, :, chunk.cols]

    def landed(self, k, landings, sem):
        chunk = self.chunks[k]
        here = landings[chunk.kind].at[:, :, chunk.groups, :, chunk.cols]
        remote(here, here, self.shed.at[k], sem, self.spot.me).wait_recv()

    def take_in(self, k, seat, landings, slot):
        chunk = self.chunks[k]
        line, here = chunk.line(self.partial, seat), self.landing(k, landings, slot)
        line[...] = line[...] + here[...]

    def begin(self, k):
        spot = self.spot
        for slot in range(4):
            seat = 2 * slot + (spot.seat + 1) % 2
            self.move(
                k, seat, self.landing(k, self.land_first, slot), spot.sibling, self.first_in.at[k]
            )

    def to_third(self, k):
        spot = self.spot
        self.landed(k, self.land_first, self.first_in.at[k])
        for slot in range(4):
            self.take_in(k, 2 * slot + spot.seat % 2, self.land_first, slot)
        for slot in range(2):
            seat = spot.seat + spot.to_third + slot * spot.to_second
            self.move(
                k, seat, self.landing(k, self.land_third, slot), spot.third, self.across_in.at[k]
            )

    def to_second(self, k):
        spot = self.spot
        self.landed(k, self.land_third, self.across_in.at[k])
        for slot in range(2):
            self.take_in(k, spot.seat + slot * spot.to_second, self.land_third, slot)
        seat = spot.seat + spot.to_second
        self.move(k, seat, self.landing(k, self.land_second, 0), spot.second, self.over_in.at[k])

    def to_owner(self, k):
        chunk, spot = self.chunks[k], self.spot
        self.landed(k, self.land_second, self.over_in.at[k])
        self.take_in(k, spot.seat, self.land_second, 0)
        target = self.sums[chunk.kind].at[spot.layer, chunk.groups, :, chunk.cols]
        for layer in spot.above:
            remote(
                chunk.block(self.partial, layer, spot.seat),
                target,
                self.shed.at[k],
                self.owner_in.at[k],
                layer * ROWS + spot.seat,
            ).start()
        self.keep(k).start()

    def keep(self, k):
        chunk, spot = self.chunks[k], self.spot
        return pltpu.make_async_copy(
            chunk.block(self.partial, spot.layer, spot.seat),
            self.sums[chunk.kind].at[spot.layer, chunk.groups, :, chunk.cols],
            self.kept.at[k],
        )

    def settle(self, k):
        chunk = self.chunks[k]
        here = self.sums[chunk.kind].at[pl.ds(0, 3), chunk.groups, :, chunk.cols]
        remote(here, here, self.shed.at[k], self.owner_in.at[k], self.spot.me).wait_recv()
        self.keep(k).wait()
        for count in (7, 3):
            there = chunk.bulk(self.partial, 3 if count == 3 else LAYERS, 1 if count == 3 else count)
            remote(there, there, self.shed.at[k], self.owner_in.at[k], self.spot.me).wait_send()


def interleave(count, body, steps=()):
    assert len(steps) <= count

    def one(index, carry):
        body(index)
        for place, thunks in enumerate(steps):
            if thunks:

                @pl.when(index == place)
                def _():
                    for thunk in thunks:
                        thunk()

        return carry

    lax.fori_loop(0, count, one, 0)


def unroll(count, body, steps):
    for index in range(count):
        body(index)
        for thunk in steps[index]:
            thunk()


def spread(thunks, slots):
    return [
        thunks[len(thunks) * place // slots : len(thunks) * (place + 1) // slots]
        for place in range(slots)
    ]


LEAD = 3


def step_kernel(trees, *given):
    given, named = list(given), {}
    for tree in trees:
        named.update(jax.tree.unflatten(tree, given[: tree.num_leaves]))
        given = given[tree.num_leaves :]
    refs = types.SimpleNamespace(**named)
    spot = Spot()
    me = spot.me
    traffic = Traffic(spot, named)
    chunks = range(len(traffic.chunks))
    tokens, cotangent = refs.tokens, refs.cotangent
    sequence, upstream = refs.sequence, refs.upstream
    first_spare, second_spare = refs.first_spare, refs.second_spare

    locals_ = [
        pltpu.make_async_copy(
            traffic.shards[kind], traffic.full[kind].at[spot.layer, spot.seat], traffic.local.at[kind]
        )
        for kind in range(4)
    ] + [
        pltpu.make_async_copy(cotangent, first_spare, traffic.local.at[4]),
        pltpu.make_async_copy(tokens.at[:, me], sequence.at[:, me], traffic.local.at[5]),
        pltpu.make_async_copy(refs.small_own, refs.small.at[me], traffic.local.at[6]),
    ]
    for copy in locals_:
        copy.start()
    meet_all(me)

    def tokens_piece(first, last):
        return lambda: traffic.exchange(tokens, sequence, 0, first, last)

    def piece_of(source, target, which, first, last):
        return lambda: traffic.exchange(source, target, which, first, last)

    def do(method, *args):
        return lambda: method(*args)

    layer = Layer(named)
    layer.context_grad, layer.preact_grad = refs.hidden_low, refs.active
    layer.result, layer.input_grad = first_spare, second_spare
    layer.weight_in, layer.weight_mix, layer.weight_up, layer.weight_down = refs.full
    layer.in_grad, layer.mix_grad, layer.up_grad, layer.down_grad = refs.partial
    layer.lengths = [refs.lengths[batch, me] for batch in range(2)]
    tiles, wide = layer.width // TILE, layer.hidden_width // TILE
    pairs = 2 * (layer.width // PAIR)
    ins = 3
    ups = wide // tiles
    assert len(chunks) == ins + 1 + 2 * ups

    ticks = []
    token_cuts = [0, 8, 16, 24, COUNT - 1]
    for tick in range(-LEAD, len(chunks) + 2):
        here = []
        if 0 <= tick + LEAD < len(chunks):
            here.append(do(traffic.own, tick + LEAD))
        if -LEAD <= tick < 4 - LEAD:
            here.append(tokens_piece(token_cuts[tick + LEAD], token_cuts[tick + LEAD + 1]))
        if tick == -LEAD:
            here.append(do(traffic.exchange_small, refs.small_own, refs.small, 4))
        if 0 <= tick < len(chunks):
            here.append(do(traffic.from_line, tick))
        if 0 <= tick - 1 < len(chunks):
            here.append(do(traffic.from_second, tick - 1))
            here.append(do(traffic.from_third, tick - 1, 0))
        if 0 <= tick - 2 < len(chunks):
            here.append(do(traffic.from_third, tick - 2, 1))
        if tick >= 6:
            first = (tick - 6) * 4
            if first < COUNT - 1:
                here.append(
                    piece_of(second_spare, upstream, 1, first, min(first + 4, COUNT - 1))
                )
        ticks.append(here)
    flat = lambda first, last: [thunk for here in ticks[first + LEAD : last + LEAD] for thunk in here]

    for thunk in flat(-LEAD, 0):
        thunk()
    for copy in locals_:
        copy.wait()
    layer.terms[...] = jnp.zeros_like(layer.terms)
    for batch in range(2):
        for seat in range(COUNT):
            second_spare[batch, seat] = first_spare[batch, refs.backward_order[batch, seat]]
    own_upstream = pltpu.make_async_copy(
        second_spare.at[:, me], upstream.at[:, me], traffic.local.at[7]
    )
    own_upstream.start()
    for thunk in flat(0, 2):
        thunk()
    traffic.exchanged_small(refs.small, 4).wait_recv()
    layer.spread_small()
    for thunk in flat(2, ins + 2):
        thunk()
    traffic.exchanged(sequence, 0).wait_recv()
    for k in range(ins):
        traffic.complete(k)
    interleave(3 * tiles, layer.project, spread(flat(ins + 2, ins + 3), 3 * tiles))
    interleave(pairs, layer.attend, spread(flat(ins + 3, ins + 6), pairs))
    traffic.complete(ins)
    interleave(layer.rows // TILE, layer.mix)
    for thunk in flat(ins + 6, ins + ups + 3):
        thunk()
    for k in range(ins + 1, ins + 1 + ups):
        traffic.complete(k)
    interleave(wide, layer.up, spread(flat(ins + ups + 3, len(chunks) + 2), wide))
    for k in range(ins + 1 + ups, len(chunks)):
        traffic.complete(k)
    interleave(tiles, layer.down)
    own_upstream.wait()
    cotangents = traffic.exchanged(upstream, 1)
    cotangents.wait_recv()
    interleave(layer.rows // 128, layer.finish)

    keep_result = pltpu.make_async_copy(
        first_spare.at[:, me], refs.returned.at[:, me], traffic.local.at[0]
    )
    keep_result.start()
    pieces = [
        piece_of(first_spare, refs.returned, 2, first, min(first + 4, COUNT - 1))
        for first in range(0, COUNT - 1, 4)
    ]
    interleave(LAYERS, layer.down_weight_grad, spread(pieces, LAYERS))

    queue = list(range(ins + 1 + ups, len(chunks))) + list(range(ins + 1, ins + 1 + ups))
    queue += [ins] + list(range(ins))
    walk = []
    for tick in range(len(queue) + 2):
        for late, stage in enumerate((traffic.to_third, traffic.to_second, traffic.to_owner)):
            if 0 <= tick - late < len(queue):
                walk.append(do(stage, queue[tick - late]))

    def next_steps(count):
        taken, walk[:] = walk[:count], walk[count:]
        return taken

    def with_begin(steps, count, every, kinds):
        made = [list(step) for step in steps] + [[] for _ in range(count - len(steps))]
        for place, k in enumerate(kinds):
            made[(place + 1) * every - 1].insert(0, do(traffic.begin, k))
        return made

    for k in queue[:ups]:
        traffic.begin(k)
    interleave(LAYERS, layer.active_backward, spread(next_steps(3), LAYERS))
    interleave(
        wide,
        layer.up_weight_grad,
        with_begin(spread(next_steps(3), wide), wide, tiles, queue[ups : 2 * ups]),
    )
    unroll(tiles, layer.hidden_backward, spread(next_steps(2), tiles))
    interleave(layer.rows // 128, layer.first_backward, spread(next_steps(1), 1))
    interleave(
        tiles,
        layer.mix_weight_grad,
        with_begin(spread(next_steps(1), tiles), tiles, tiles, queue[2 * ups : 2 * ups + 1]),
    )
    unroll(tiles, layer.mix_backward, spread(next_steps(1), tiles))
    interleave(pairs, layer.attend_backward, spread(next_steps(5), pairs))
    interleave(
        3 * tiles,
        layer.in_weight_grad,
        with_begin(spread(next_steps(3), 3 * tiles), 3 * tiles, tiles, queue[2 * ups + 1 :]),
    )
    layer.gather_terms()
    traffic.exchange_small(refs.small_grad, refs.small_sums, 5)
    keep_small = pltpu.make_async_copy(
        refs.small_grad.at[me], refs.small_sums.at[me], traffic.local.at[1]
    )
    keep_small.start()
    cotangents.wait_send()
    unroll(tiles, layer.input_backward, spread(next_steps(1), tiles))
    keep_grad = pltpu.make_async_copy(
        second_spare.at[:, me], refs.tokens_grad.at[:, me], traffic.local.at[2]
    )
    keep_grad.start()
    left = next_steps(len(walk))
    cuts = list(range(0, COUNT - 1, 4))
    for place in range(max(len(left), len(cuts))):
        if place < len(cuts):
            piece_of(
                second_spare, refs.tokens_grad, 3, cuts[place], min(cuts[place] + 4, COUNT - 1)
            )()
        if place < len(left):
            left[place]()
    for k in queue:
        traffic.settle(k)
        traffic.own_sent(k)
    traffic.exchanged(sequence, 0).wait_send()
    for target, which in ((refs.returned, 2), (refs.tokens_grad, 3)):
        copy = traffic.exchanged(target, which)
        copy.wait_recv()
        copy.wait_send()
    traffic.exchanged_small(refs.small, 4).wait_send()
    small = traffic.exchanged_small(refs.small_sums, 5)
    small.wait_recv()
    small.wait_send()
    for copy in (keep_result, keep_small, keep_grad):
        copy.wait()


def encoder_step(lengths, backward_order, tokens, cotangent, shards, small_own):
    low, full = jnp.bfloat16, jnp.float32
    width, hidden_width = tokens.shape[-1], shards[2].shape[-1]
    rows = tokens.shape[0] * COUNT * tokens.shape[2]
    anywhere = pl.BlockSpec(memory_space=pl.ANY)
    inputs = dict(
        lengths=lengths,
        backward_order=backward_order,
        tokens=tokens,
        cotangent=cotangent,
        shards=shards,
        small_own=small_own,
    )
    shapes = [shard.shape for shard in shards]
    smalls = ((COUNT,) + small_own.shape, full)
    outputs = dict(
        returned=jax.ShapeDtypeStruct(tokens.shape, low),
        tokens_grad=jax.ShapeDtypeStruct(tokens.shape, low),
        sums=[jax.ShapeDtypeStruct((LAYERS,) + shape, low) for shape in shapes],
        small_sums=jax.ShapeDtypeStruct(*smalls),
    )
    sequences = pltpu.VMEM(tokens.shape, low)
    scratch = dict(
        full=[pltpu.VMEM((LAYERS, ROWS) + shape, low) for shape in shapes],
        partial=[pltpu.VMEM((LAYERS, ROWS) + shape, low) for shape in shapes],
        land_first=[pltpu.VMEM((4, LAYERS) + shape, low) for shape in shapes],
        land_third=[pltpu.VMEM((2, LAYERS) + shape, low) for shape in shapes],
        land_second=[pltpu.VMEM((1, LAYERS) + shape, low) for shape in shapes],
        sequence=sequences,
        upstream=sequences,
        first_spare=sequences,
        second_spare=sequences,
        small=pltpu.VMEM(*smalls),
        small_grad=pltpu.VMEM(*smalls),
        **scratch_of(rows, width, hidden_width),
    )
    count = len(chunks_of(shapes))
    each = pltpu.SemaphoreType.DMA((count,))
    sems = dict(
        local=pltpu.SemaphoreType.DMA((8,)),
        given=pltpu.SemaphoreType.DMA((6,)),
        taken=pltpu.SemaphoreType.DMA((6,)),
        third_in=pltpu.SemaphoreType.DMA((count, 2)),
        sent=each,
        along_in=each,
        second_in=each,
        sibling_in=each,
        shed=each,
        first_in=each,
        across_in=each,
        over_in=each,
        owner_in=each,
        kept=each,
    )
    smem = pl.BlockSpec(memory_space=pltpu.SMEM)
    given, given_tree = jax.tree.flatten(inputs)
    in_specs = [smem if leaf.dtype == jnp.int32 else anywhere for leaf in given]
    made, made_tree = jax.tree.flatten(outputs)
    held, held_tree = jax.tree.flatten({**scratch, **sems})
    results = pl.pallas_call(
        functools.partial(step_kernel, (given_tree, made_tree, held_tree)),
        out_shape=made,
        in_specs=in_specs,
        out_specs=[anywhere] * len(made),
        scratch_shapes=held,
        compiler_params=pltpu.CompilerParams(
            collective_id=0, has_side_effects=True, vmem_limit_bytes=VMEM_LIMIT
        ),
        name="encoder_step",
    )(*given)
    results = jax.tree.unflatten(made_tree, results)
    return types.SimpleNamespace(**results)


VMEM_LIMIT = 63 << 20


def finish_kernel(order, returned, moved, *refs):
    sums, small_sums, refs = refs[:4], refs[4], refs[5:]
    layer_out, tokens_grad, refs = refs[0], refs[1], refs[2:]
    totals, outs, (sem,) = refs[:4], refs[4:12], refs[12:]

    def deal(step, carry):
        batch, seat = step // COUNT, step % COUNT
        pltpu.make_async_copy(
            returned.at[batch, order[batch, seat]], layer_out.at[batch, seat], sem.at[0]
        ).start()
        return carry

    lax.fori_loop(0, 2 * COUNT, deal, 0)
    copy = pltpu.make_async_copy(moved, tokens_grad, sem.at[1])
    copy.start()
    for total, parts in zip(totals, sums):
        total[...] = sum(parts[layer].astype(jnp.float32) for layer in range(LAYERS))
    small = jnp.sum(small_sums[...], 0)
    for place, out in enumerate(outs):
        out[...] = small[place : place + 1, : out.shape[1]]
    copy.wait()
    pltpu.make_async_copy(returned, layer_out, sem.at[0]).wait()


def finish_step(order, returned, tokens_grad, sums, small_sums):
    anywhere = pl.BlockSpec(memory_space=pl.ANY)
    inside = pl.BlockSpec(memory_space=pltpu.VMEM)
    return pl.pallas_call(
        finish_kernel,
        out_shape=[jax.ShapeDtypeStruct(returned.shape, returned.dtype)] * 2
        + [jax.ShapeDtypeStruct(part.shape[1:], jnp.float32) for part in sums]
        + [jax.ShapeDtypeStruct((1, width), jnp.float32) for width in WIDTHS],
        in_specs=[pl.BlockSpec(memory_space=pltpu.SMEM)] + [anywhere] * 2 + [inside] * 5,
        out_specs=[anywhere] * 2 + [inside] * 12,
        scratch_shapes=[pltpu.SemaphoreType.DMA((2,))],
        name="finish_step",
    )(order, returned, tokens_grad, *sums, small_sums)


SMALL = (1, 3, 4, 5, 7, 9, 10, 11)
LARGE = (0, 2, 6, 8)


def local(tokens, lengths, order, *rest):
    shards, cotangent = rest[:12], rest[12]
    if lax.axis_size("dp") != COUNT or tokens.shape[2] % 8:
        return portable(tokens, lengths, order, *rest)
    small = sum(
        lax.pad(
            shards[i].astype(jnp.float32)[None],
            jnp.float32(0),
            ((place, len(SMALL) - 1 - place, 0), (0, 128 - shards[i].shape[0], 0)),
        )
        for place, i in enumerate(SMALL)
    )
    slots = lax.broadcasted_iota(jnp.int32, order.shape + (COUNT,), 1)
    targets = lax.broadcasted_iota(jnp.int32, order.shape + (COUNT,), 2)
    backward_order = jnp.sum(jnp.where(order[:, :, None] == targets, slots, 0), 1)
    made = encoder_step(
        lengths,
        backward_order,
        tokens,
        cotangent,
        [shards[i].reshape(-1, 8, shards[i].shape[-1]) for i in LARGE],
        small,
    )
    layer_out, tokens_grad, *rest = finish_step(
        order, made.returned, made.tokens_grad, made.sums, made.small_sums
    )
    outputs = [None] * 12
    for i, total in zip(LARGE, rest[:4]):
        outputs[i] = total.reshape(-1, total.shape[-1])
    for i, total in zip(SMALL, rest[4:]):
        outputs[i] = total.reshape(-1)
    return (layer_out, tokens_grad, *outputs)


def solution(mesh):
    return jax.shard_map(
        local,
        mesh=mesh,
        in_specs=(
            P(None, None, "dp", None),
            P(),
            P(),
            P("dp", None),
            P("dp"),
            P("dp", None),
            P("dp"),
            P("dp"),
            P("dp"),
            P("dp", None),
            P("dp"),
            P("dp", None),
            P("dp"),
            P("dp"),
            P("dp"),
            P(None, None, "dp", None),
        ),
        out_specs=(
            P(None, None, "dp", None),
            P(None, None, "dp", None),
            P("dp", None),
            P("dp"),
            P("dp", None),
            P("dp"),
            P("dp"),
            P("dp"),
            P("dp", None),
            P("dp"),
            P("dp", None),
            P("dp"),
            P("dp"),
            P("dp"),
        ),
        check_vma=False,
    )
```

```python
import functools
import types

import jax
import jax.numpy as jnp
from jax import lax
from jax.experimental import pallas as pl
from jax.experimental.pallas import tpu as pltpu
from jax.sharding import PartitionSpec as P

MESH = pl.DeviceIdType.MESH

HD = 64


epsilon = 1e-12


def matmul(left, right):
    return jnp.dot(left, right, preferred_element_type=jnp.float32)


def rows_product(left, right):
    return lax.dot_general(
        left, right, (((0,), (0,)), ((), ())), preferred_element_type=jnp.float32
    )


def right_transposed(left, right):
    return lax.dot_general(
        left, right, (((1,), (1,)), ((), ())), preferred_element_type=jnp.float32
    )


def split_heads(block, heads):
    return block.reshape(block.shape[0], heads, -1).transpose(1, 0, 2)


def join_heads(block):
    return block.transpose(1, 0, 2).reshape(block.shape[1], -1)


def norm_forward(summed, norm_gain, norm_shift):
    row_mean = jnp.mean(summed, -1, keepdims=True)
    centered = summed - row_mean
    reciprocal = lax.rsqrt(jnp.mean(centered * centered, -1, keepdims=True) + epsilon)
    normed = centered * reciprocal
    return (normed * norm_gain + norm_shift, normed, reciprocal)


def norm_backward(upstream, normed, reciprocal, norm_gain):
    scaled = upstream * norm_gain
    summed_grad = reciprocal * (
        scaled
        - jnp.mean(scaled, -1, keepdims=True)
        - normed * jnp.mean(scaled * normed, -1, keepdims=True)
    )
    return (summed_grad, jnp.sum(upstream * normed, 0), jnp.sum(upstream, 0))


def head_scores(head_query, head_keys, valid):
    scores = right_transposed(head_query, head_keys) * 0.125
    return jnp.where(valid[None, :], scores, -1e30)


def attend_forward(packed, valid):
    head_query, head_keys, head_values = packed
    scores = head_scores(head_query, head_keys, valid)
    row_max = jnp.max(scores, -1, keepdims=True)
    weights_raw = jnp.exp(scores - row_max)
    row_sum = jnp.sum(weights_raw, -1, keepdims=True)
    probability = weights_raw / row_sum
    context = matmul(probability.astype(jnp.bfloat16), head_values)
    return (context, (row_max + jnp.log(row_sum))[:, 0])


def attend_backward(packed, valid):
    head_query, head_keys, head_values, context_grad, log_total = packed
    scores = head_scores(head_query, head_keys, valid)
    probability = jnp.exp(scores - log_total[:, None])
    low_prob = probability.astype(jnp.bfloat16)
    prob_grad = right_transposed(context_grad, head_values)
    value_grad = rows_product(low_prob, context_grad)
    shifted = prob_grad - jnp.sum(probability * prob_grad, -1, keepdims=True)
    score_grad = (probability * shifted).astype(jnp.bfloat16)
    query_grad = matmul(score_grad, head_keys) * 0.125
    key_grad = rows_product(score_grad, head_query) * 0.125
    return (query_grad, key_grad, value_grad)


def forward(weights, sequence, length):
    (
        weight_in,
        bias_in,
        weight_mix,
        bias_mix,
        gain_first,
        shift_first,
        weight_up,
        bias_up,
        weight_down,
        bias_down,
        gain_second,
        shift_second,
    ) = weights
    width = sequence.shape[1]
    heads = width // HD
    valid = jnp.arange(sequence.shape[0], dtype=jnp.int32) < length
    bias_full = jnp.concatenate(
        [
            bias_in[:width].astype(jnp.float32),
            jnp.zeros((width,), jnp.float32),
            bias_in[width:].astype(jnp.float32),
        ]
    )
    projected = (matmul(sequence, weight_in) + bias_full).astype(jnp.bfloat16)
    queries = split_heads(projected[:, :width], heads)
    key_heads = split_heads(projected[:, width : 2 * width], heads)
    value_heads = split_heads(projected[:, 2 * width :], heads)
    context, log_total = lax.map(
        lambda packed: attend_forward(packed, valid), (queries, key_heads, value_heads)
    )
    context_low = join_heads(context).astype(jnp.bfloat16)
    branch = matmul(context_low, weight_mix) + bias_mix.astype(jnp.float32)
    hidden, normed_first, recip_first = norm_forward(
        sequence.astype(jnp.float32) + branch,
        gain_first.astype(jnp.float32),
        shift_first.astype(jnp.float32),
    )
    hidden_low = hidden.astype(jnp.bfloat16)
    preact = matmul(hidden_low, weight_up) + bias_up.astype(jnp.float32)
    activated = jax.nn.gelu(preact, approximate=False).astype(jnp.bfloat16)
    feed_out = matmul(activated, weight_down) + bias_down.astype(jnp.float32)
    result, normed_second, recip_second = norm_forward(
        hidden + feed_out, gain_second.astype(jnp.float32), shift_second.astype(jnp.float32)
    )
    stored = (
        valid,
        queries,
        key_heads,
        value_heads,
        log_total,
        context_low,
        normed_first,
        recip_first,
        hidden_low,
        preact,
        activated,
        normed_second,
        recip_second,
    )
    return (result.astype(jnp.bfloat16), stored)


def backward(weights, sequence, upstream_low, stored):
    (
        weight_in,
        bias_in,
        weight_mix,
        bias_mix,
        gain_first,
        shift_first,
        weight_up,
        bias_up,
        weight_down,
        bias_down,
        gain_second,
        shift_second,
    ) = weights
    (
        valid,
        queries,
        key_heads,
        value_heads,
        log_total,
        context_low,
        normed_first,
        recip_first,
        hidden_low,
        preact,
        activated,
        normed_second,
        recip_second,
    ) = stored
    width = sequence.shape[1]
    heads = width // HD
    upstream = upstream_low.astype(jnp.float32)
    second_grad, gain_second_grad, shift_second_grad = norm_backward(
        upstream, normed_second, recip_second, gain_second.astype(jnp.float32)
    )
    feed_grad = second_grad.astype(jnp.bfloat16)
    bias_down_grad = jnp.sum(feed_grad.astype(jnp.float32), 0)
    weight_down_grad = rows_product(activated, feed_grad)
    act_grad = right_transposed(feed_grad, weight_down)
    slope = (
        0.5 * (1.0 + jax.scipy.special.erf(preact * 0.7071067811865476))
        + preact * jnp.exp(-0.5 * preact * preact) * 0.3989422804014327
    )
    preact_grad = (act_grad * slope).astype(jnp.bfloat16)
    bias_up_grad = jnp.sum(preact_grad.astype(jnp.float32), 0)
    weight_up_grad = rows_product(hidden_low, preact_grad)
    hidden_grad = second_grad + right_transposed(preact_grad, weight_up)
    first_grad, gain_first_grad, shift_first_grad = norm_backward(
        hidden_grad, normed_first, recip_first, gain_first.astype(jnp.float32)
    )
    branch_grad = first_grad.astype(jnp.bfloat16)
    bias_mix_grad = jnp.sum(branch_grad.astype(jnp.float32), 0)
    weight_mix_grad = rows_product(context_low, branch_grad)
    context_grad = right_transposed(branch_grad, weight_mix).astype(jnp.bfloat16)
    query_grad, key_grad, value_grad = lax.map(
        lambda packed: attend_backward(packed, valid),
        (queries, key_heads, value_heads, split_heads(context_grad, heads), log_total),
    )
    projected_grad = jnp.concatenate(
        [join_heads(query_grad), join_heads(key_grad), join_heads(value_grad)], -1
    ).astype(jnp.bfloat16)
    column_sums = jnp.sum(projected_grad.astype(jnp.float32), 0)
    bias_in_grad = jnp.concatenate([column_sums[:width], column_sums[2 * width :]])
    weight_in_grad = rows_product(sequence, projected_grad)
    input_grad = (first_grad + right_transposed(projected_grad, weight_in)).astype(jnp.bfloat16)
    gradients = (
        weight_in_grad,
        bias_in_grad,
        weight_mix_grad,
        bias_mix_grad,
        gain_first_grad,
        shift_first_grad,
        weight_up_grad,
        bias_up_grad,
        weight_down_grad,
        bias_down_grad,
        gain_second_grad,
        shift_second_grad,
    )
    return (input_grad, gradients)


def permuted(blocks, picks):
    chosen = (picks[:, None] == jnp.arange(picks.shape[0])[None, :]).astype(blocks.dtype)
    flat = blocks.reshape(blocks.shape[0], -1)
    return matmul(chosen, flat).astype(blocks.dtype).reshape(blocks.shape)


def inverse_of(picks):
    slots = jnp.arange(picks.shape[0], dtype=jnp.int32)
    return jnp.sum(jnp.where(picks[:, None] == slots[None, :], slots[:, None], 0), 0)


def fetch_weights(shards):
    return (
        lax.all_gather(shards[0], "dp", axis=0, tiled=True),
        lax.all_gather(shards[1], "dp", axis=0, tiled=True),
        lax.all_gather(shards[2], "dp", axis=0, tiled=True),
        lax.all_gather(shards[3], "dp", axis=0, tiled=True),
        lax.all_gather(shards[4], "dp", axis=0, tiled=True),
        lax.all_gather(shards[5], "dp", axis=0, tiled=True),
        lax.all_gather(shards[6], "dp", axis=0, tiled=True),
        lax.all_gather(shards[7], "dp", axis=0, tiled=True),
        lax.all_gather(shards[8], "dp", axis=0, tiled=True),
        lax.all_gather(shards[9], "dp", axis=0, tiled=True),
        lax.all_gather(shards[10], "dp", axis=0, tiled=True),
        lax.all_gather(shards[11], "dp", axis=0, tiled=True),
    )


def add_trees(first, second):
    if first is None:
        return second
    return jax.tree.map(lambda left, right: left + right, first, second)


def portable(
    tokens,
    lengths,
    order,
    weight_in,
    bias_in,
    weight_mix,
    bias_mix,
    gain_first,
    shift_first,
    weight_up,
    bias_up,
    weight_down,
    bias_down,
    gain_second,
    shift_second,
    cotangent,
):
    shards = (
        weight_in,
        bias_in,
        weight_mix,
        bias_mix,
        gain_first,
        shift_first,
        weight_up,
        bias_up,
        weight_down,
        bias_down,
        gain_second,
        shift_second,
    )
    device = lax.axis_index("dp")
    totals = None
    outputs_list = []
    grads_list = []
    for batch in range(tokens.shape[0]):
        current = fetch_weights(shards)
        picks = order[batch]
        dealt_tokens = permuted(tokens[batch], picks)
        sequence, upstream = (
            lax.all_to_all(dealt_tokens, "dp", split_axis=0, concat_axis=1, tiled=True),
            lax.all_to_all(cotangent[batch], "dp", split_axis=0, concat_axis=1, tiled=True),
        )
        length = jnp.sum(jnp.where(jnp.arange(picks.shape[0]) == picks[device], lengths[batch], 0))
        result, stored = forward(current, sequence[0], length)
        behind = (
            lax.all_gather(shards[0], "dp", axis=0, tiled=True),
            lax.all_gather(shards[1], "dp", axis=0, tiled=True),
            lax.all_gather(shards[2], "dp", axis=0, tiled=True),
            lax.all_gather(shards[3], "dp", axis=0, tiled=True),
            lax.all_gather(shards[4], "dp", axis=0, tiled=True),
            lax.all_gather(shards[5], "dp", axis=0, tiled=True),
            lax.all_gather(shards[6], "dp", axis=0, tiled=True),
            lax.all_gather(shards[7], "dp", axis=0, tiled=True),
            lax.all_gather(shards[8], "dp", axis=0, tiled=True),
            lax.all_gather(shards[9], "dp", axis=0, tiled=True),
            lax.all_gather(shards[10], "dp", axis=0, tiled=True),
            lax.all_gather(shards[11], "dp", axis=0, tiled=True),
        )
        input_grad, gradients = backward(behind, sequence[0], upstream[0], stored)
        back_out, back_grad = (
            lax.all_to_all(result[None], "dp", split_axis=1, concat_axis=0, tiled=True),
            lax.all_to_all(input_grad[None], "dp", split_axis=1, concat_axis=0, tiled=True),
        )
        restored = permuted(back_grad, inverse_of(picks))
        outputs_list.append(back_out)
        grads_list.append(restored)
        totals = add_trees(totals, gradients)
    totals = (
        lax.psum_scatter(totals[0], "dp", scatter_dimension=0, tiled=True),
        lax.psum_scatter(totals[1], "dp", scatter_dimension=0, tiled=True),
        lax.psum_scatter(totals[2], "dp", scatter_dimension=0, tiled=True),
        lax.psum_scatter(totals[3], "dp", scatter_dimension=0, tiled=True),
        lax.psum_scatter(totals[4], "dp", scatter_dimension=0, tiled=True),
        lax.psum_scatter(totals[5], "dp", scatter_dimension=0, tiled=True),
        lax.psum_scatter(totals[6], "dp", scatter_dimension=0, tiled=True),
        lax.psum_scatter(totals[7], "dp", scatter_dimension=0, tiled=True),
        lax.psum_scatter(totals[8], "dp", scatter_dimension=0, tiled=True),
        lax.psum_scatter(totals[9], "dp", scatter_dimension=0, tiled=True),
        lax.psum_scatter(totals[10], "dp", scatter_dimension=0, tiled=True),
        lax.psum_scatter(totals[11], "dp", scatter_dimension=0, tiled=True),
    )
    return (
        jnp.stack(outputs_list),
        jnp.stack(grads_list),
        totals[0],
        totals[1],
        totals[2],
        totals[3],
        totals[4],
        totals[5],
        totals[6],
        totals[7],
        totals[8],
        totals[9],
        totals[10],
        totals[11],
    )


COUNT = 32
ROWS, LAYERS = 8, 4


def meet_all(me):
    barrier = pltpu.get_barrier_semaphore()

    def greet(step, carry):
        pl.semaphore_signal(
            barrier, inc=1, device_id=(lax.rem(me + step, COUNT),), device_id_type=MESH
        )
        return carry

    lax.fori_loop(1, COUNT, greet, 0)
    pl.semaphore_wait(barrier, COUNT - 1)


def remote(source, target, send_sem, recv_sem, device):
    return pltpu.make_async_remote_copy(
        src_ref=source,
        dst_ref=target,
        send_sem=send_sem,
        recv_sem=recv_sem,
        device_id=(device,),
        device_id_type=MESH,
    )


WIDTHS = (48, 24, 24, 24, 96, 24, 24, 24)
BIAS_IN, BIAS_MIX, GAIN_FIRST, SHIFT_FIRST, BIAS_UP, BIAS_DOWN, GAIN_SECOND, SHIFT_SECOND = range(8)
TILE = 256
PAIR = 128


def contract(left, right, left_dim, right_dim):
    return lax.dot_general(
        left,
        right,
        (((left_dim,), (right_dim,)), ((), ())),
        preferred_element_type=jnp.float32,
    )


def owners(width):
    lane = lax.broadcasted_iota(jnp.int32, (COUNT, COUNT * width), 1)
    owner = (lane * (-(-(1 << 20) // width))) >> 20
    device = lax.broadcasted_iota(jnp.int32, (COUNT, COUNT * width), 0)
    return owner == device


def places(width):
    lane = lax.broadcasted_iota(jnp.int32, (PAIR, COUNT * width), 1)
    owner = (lane * (-(-(1 << 20) // width))) >> 20
    entry = lax.broadcasted_iota(jnp.int32, (PAIR, COUNT * width), 0)
    return jnp.where(lane - owner * width == entry, 1.0, 0.0).astype(jnp.bfloat16)


def columns(tile, size=TILE):
    return pl.ds(pl.multiple_of(tile * size, size), size)


def flat(value):
    return value.reshape(-1, value.shape[-1])


def take_rows(ref, start, stop):
    layers, seats, groups, small, _ = ref.shape
    pieces = []
    while start < stop:
        layer, rest = divmod(start // small, seats * groups)
        seat, group = divmod(rest, groups)
        whole = min((stop - start) // (small * groups), seats - seat)
        if group == 0 and whole:
            pieces.append(flat(ref[layer, seat : seat + whole]))
            start += whole * groups * small
        else:
            end = min(groups, group + (stop - start) // small)
            pieces.append(flat(ref[layer, seat, group:end]))
            start += (end - group) * small
    return jnp.concatenate(pieces, 0)


class Layer:
    def __init__(self, refs):
        self.__dict__.update(refs)
        self.rows, self.width = self.normed.shape
        self.hidden_width = self.slope.shape[1]

    def spread_small(self):
        for place, width in enumerate(WIDTHS):
            given = self.small[:, place, :].astype(jnp.bfloat16)
            spread = contract(given, places(width), 1, 0)
            row = jnp.sum(jnp.where(owners(width), spread, 0.0), 0, keepdims=True)
            if place == BIAS_IN:
                self.bias_row[:, : self.width] = row[:, : self.width]
                self.bias_row[:, self.width : 2 * self.width] = jnp.zeros_like(row[:, : self.width])
                self.bias_row[:, 2 * self.width :] = row[:, self.width :]
            elif place == BIAS_UP:
                self.up_row[...] = row
            else:
                self.vectors[place : place + 1, :] = row

    def vector(self, place):
        return self.vectors[place : place + 1, :]

    def project(self, tile):
        here = columns(tile)
        value = jnp.dot(
            flat(self.sequence[...]),
            flat(self.weight_in[:, :, :, :, here]),
            preferred_element_type=jnp.float32
        )
        value = (value + self.bias_row[:, here]).astype(jnp.bfloat16)
        scale = jnp.where(tile < self.width // TILE, 0.125, 1.0).astype(jnp.bfloat16)
        self.packed[:, here] = value * scale

    def heads_of(self, step):
        pairs = self.width // PAIR
        batch, pair = step // pairs, step % pairs
        rows = pl.ds(pl.multiple_of(batch * TILE, TILE), TILE)
        return batch, pair, rows

    def block(self, part, rows, pair):
        offset = pl.multiple_of(part * self.width + pair * PAIR, PAIR)
        return self.packed[rows, pl.ds(offset, PAIR)]

    def half(self, value, head):
        lane = lax.broadcasted_iota(jnp.int32, value.shape, 1)
        keep = lane < PAIR // 2 if head == 0 else lane >= PAIR // 2
        return jnp.where(keep, value, jnp.zeros_like(value))

    def attend(self, step):
        batch, pair, rows = self.heads_of(step)
        queries, key_block, value_block = (self.block(part, rows, pair) for part in range(3))
        length = jnp.where(batch == 0, self.lengths[0], self.lengths[1])
        lane = lax.broadcasted_iota(jnp.int32, (1, TILE), 1)
        blocked = jnp.where(lane < length, 0.0, -1e30)
        context = []
        for head in range(2):
            scores = contract(self.half(queries, head), key_block, 1, 1) + blocked
            weights = jnp.exp(scores - jnp.max(scores, -1, keepdims=True))
            total = jnp.sum(weights, -1, keepdims=True)
            low = (weights * (1.0 / total)).astype(jnp.bfloat16)
            self.chances[2 * step + head] = low
            context.append(jnp.dot(low, value_block, preferred_element_type=jnp.float32))
        lane = lax.broadcasted_iota(jnp.int32, context[0].shape, 1)
        joined = jnp.where(lane < PAIR // 2, context[0], context[1])
        self.context[rows, columns(pair, PAIR)] = joined.astype(jnp.bfloat16)

    def mix(self, part):
        rows = columns(part)
        branch = jnp.dot(
            self.context[rows, :], flat(self.weight_mix[...]), preferred_element_type=jnp.float32
        )
        summed = flat(self.sequence[part]).astype(jnp.float32) + (branch + self.vector(BIAS_MIX))
        centered = summed - jnp.mean(summed, -1, keepdims=True)
        factor = lax.rsqrt(jnp.mean(centered * centered, -1, keepdims=True) + epsilon)
        normed = centered * factor
        hidden = normed * self.vector(GAIN_FIRST) + self.vector(SHIFT_FIRST)
        self.normed[rows, :] = normed
        self.factor[rows, :] = factor
        self.hidden_low[rows, :] = hidden.astype(jnp.bfloat16)

    def up(self, tile):
        here = columns(tile)
        value = jnp.dot(
            self.hidden_low[...], flat(self.weight_up[:, :, :, :, here]), preferred_element_type=jnp.float32
        )
        value = value + self.up_row[:, here]
        below = 0.5 * (1.0 + lax.erf(value * 0.7071067811865476))
        density = jnp.exp(-0.5 * value * value) * 0.3989422804014327
        self.active[:, here] = (value * below).astype(jnp.bfloat16)
        self.slope[:, here] = (below + value * density).astype(self.slope.dtype)

    def down(self, tile):
        here = columns(tile)
        self.upper[:, here] = jnp.dot(
            self.active[...], flat(self.weight_down[:, :, :, :, here]), preferred_element_type=jnp.float32
        )

    def finish(self, part, size=128):
        rows = columns(part, size)
        hidden = self.normed[rows, :] * self.vector(GAIN_FIRST) + self.vector(SHIFT_FIRST)
        summed = hidden + (self.upper[rows, :] + self.vector(BIAS_DOWN))
        centered = summed - jnp.mean(summed, -1, keepdims=True)
        factor = lax.rsqrt(jnp.mean(centered * centered, -1, keepdims=True) + epsilon)
        normed = centered * factor
        gain = self.vector(GAIN_SECOND)
        low = (normed * gain + self.vector(SHIFT_SECOND)).astype(jnp.bfloat16)
        parts, seats = TILE // size, size // 8
        batch, span = part // parts, pl.ds((part % parts) * seats, seats)
        self.result[batch, span] = low.reshape(seats, 8, self.width)
        upstream = flat(self.upstream[batch, span]).astype(jnp.float32)
        grad = self.norm_backward(upstream, normed, factor, gain, GAIN_SECOND, SHIFT_SECOND)
        low = grad.astype(jnp.bfloat16)
        self.upper[rows, :] = grad
        self.feed_grad[rows, :] = low
        self.add_term(BIAS_DOWN, low.astype(jnp.float32))

    def add_term(self, place, value):
        self.terms[place : place + 1, :] += jnp.sum(value, 0, keepdims=True)

    def norm_backward(self, upstream, normed, factor, gain, gain_place, shift_place):
        self.add_term(gain_place, upstream * normed)
        self.add_term(shift_place, upstream)
        scaled = upstream * gain
        return factor * (
            scaled
            - jnp.mean(scaled, -1, keepdims=True)
            - normed * jnp.mean(scaled * normed, -1, keepdims=True)
        )

    def down_weight_grad(self, layer):
        span = self.hidden_width // LAYERS
        made = [
            contract(self.active[:, columns(layer * (span // TILE) + i)], self.feed_grad[...], 0, 0)
            for i in range(span // TILE)
        ]
        made = jnp.concatenate([part.astype(jnp.bfloat16) for part in made], 0)
        self.down_grad[layer] = made.reshape(self.down_grad.shape[1:])

    def active_backward(self, layer):
        span = self.hidden_width // LAYERS
        weight = flat(self.weight_down[layer])
        for i in range(span // TILE):
            here = columns(layer * (span // TILE) + i)
            grad = contract(self.feed_grad[...], weight[i * TILE : (i + 1) * TILE], 1, 1)
            low = (grad * self.slope[:, here].astype(jnp.float32)).astype(jnp.bfloat16)
            self.preact_grad[:, here] = low
            self.up_terms[:, here] = jnp.sum(low.astype(jnp.float32), 0, keepdims=True)

    def up_weight_grad(self, tile):
        here = columns(tile)
        grad = contract(self.hidden_low[...], self.preact_grad[:, here], 0, 0)
        self.keep_columns(self.up_grad, here, grad)

    def hidden_backward(self, tile):
        here = columns(tile)
        weight = take_rows(self.weight_up, tile * TILE, (tile + 1) * TILE)
        self.upper[:, here] += contract(self.preact_grad[...], weight, 1, 1)

    def first_backward(self, part, size=128):
        rows = columns(part, size)
        grad = self.norm_backward(
            self.upper[rows, :],
            self.normed[rows, :],
            self.factor[rows, :],
            self.vector(GAIN_FIRST),
            GAIN_FIRST,
            SHIFT_FIRST,
        )
        low = grad.astype(jnp.bfloat16)
        self.upper[rows, :] = grad
        self.feed_grad[rows, :] = low
        self.add_term(BIAS_MIX, low.astype(jnp.float32))

    def mix_weight_grad(self, tile):
        here = columns(tile)
        grad = contract(self.context[...], self.feed_grad[:, here], 0, 0)
        self.keep_columns(self.mix_grad, here, grad)

    def mix_backward(self, tile):
        here = columns(tile)
        weight = take_rows(self.weight_mix, tile * TILE, (tile + 1) * TILE)
        self.context_grad[:, here] = contract(self.feed_grad[...], weight, 1, 1).astype(
            jnp.bfloat16
        )

    def attend_backward(self, step):
        batch, pair, rows = self.heads_of(step)
        queries, key_block, value_block = (self.block(part, rows, pair) for part in range(3))
        grads = self.context_grad[rows, columns(pair, PAIR)]
        query_grad = key_grad = value_grad = 0.0
        for head in range(2):
            low = self.chances[2 * step + head]
            chance = low.astype(jnp.float32)
            mine = self.half(grads, head)
            chance_grad = contract(mine, value_block, 1, 1)
            moved = chance_grad - jnp.sum(chance * chance_grad, -1, keepdims=True)
            score_grad = (chance * moved).astype(jnp.bfloat16)
            value_grad += contract(low, mine, 0, 0)
            query_grad += jnp.dot(
                score_grad, self.half(key_block, head), preferred_element_type=jnp.float32
            )
            key_grad += contract(score_grad, self.half(queries, head), 0, 0)
        for part, grad in enumerate((query_grad * 0.125, key_grad, value_grad)):
            offset = pl.multiple_of(part * self.width + pair * PAIR, PAIR)
            self.packed[rows, pl.ds(offset, PAIR)] = grad.astype(jnp.bfloat16)

    def in_weight_grad(self, tile):
        here = columns(tile)
        grads = self.packed[:, here]
        self.keep_columns(self.in_grad, here, contract(flat(self.sequence[...]), grads, 0, 0))
        self.in_terms[:, here] = jnp.sum(grads.astype(jnp.float32), 0, keepdims=True)

    def input_backward(self, tile):
        here = columns(tile)
        weight = take_rows(self.weight_in, tile * TILE, (tile + 1) * TILE)
        grad = self.upper[:, here] + contract(self.packed[...], weight, 1, 1)
        shape = self.input_grad.shape[:3] + (TILE,)
        self.input_grad[:, :, :, here] = grad.astype(jnp.bfloat16).reshape(shape)

    def keep_columns(self, ref, here, grad):
        ref[:, :, :, :, here] = grad.astype(jnp.bfloat16).reshape(ref.shape[:4] + (TILE,))

    def gather_terms(self):
        for place, width in enumerate(WIDTHS):
            if place == BIAS_IN:
                row = jnp.concatenate(
                    [self.in_terms[:, : self.width], self.in_terms[:, 2 * self.width :]], -1
                )
            elif place == BIAS_UP:
                row = self.up_terms[...]
            else:
                row = self.terms[place : place + 1, :]
            high = row.astype(jnp.bfloat16)
            rest = row - high.astype(jnp.float32)
            middle = rest.astype(jnp.bfloat16)
            low = (rest - middle.astype(jnp.float32)).astype(jnp.bfloat16)
            keep, spots = owners(width), places(width)
            self.small_grad[:, place, :] = sum(
                contract(jnp.where(keep, part.astype(jnp.float32), 0.0).astype(jnp.bfloat16), spots, 1, 1)
                for part in (high, middle, low)
            )


def scratch_of(rows, width, hidden_width):
    low, full = jnp.bfloat16, jnp.float32
    return dict(
        bias_row=pltpu.VMEM((1, 3 * width), full),
        up_row=pltpu.VMEM((1, hidden_width), full),
        vectors=pltpu.VMEM((8, width), full),
        terms=pltpu.VMEM((8, width), full),
        up_terms=pltpu.VMEM((1, hidden_width), full),
        in_terms=pltpu.VMEM((1, 3 * width), full),
        packed=pltpu.VMEM((rows, 3 * width), low),
        chances=pltpu.VMEM((2 * rows // TILE * width // PAIR, TILE, TILE), low),
        context=pltpu.VMEM((rows, width), low),
        normed=pltpu.VMEM((rows, width), full),
        factor=pltpu.VMEM((rows, 1), full),
        hidden_low=pltpu.VMEM((rows, width), low),
        active=pltpu.VMEM((rows, hidden_width), low),
        slope=pltpu.VMEM((rows, hidden_width), low),
        upper=pltpu.VMEM((rows, width), full),
        feed_grad=pltpu.VMEM((rows, width), low),
    )


class Spot:
    def __init__(self):
        self.me = me = lax.axis_index("dp")
        core, column, row = me % 2, (me // 2) % 2, (me // 4) % 2
        self.layer, self.seat = me // 8, me % 8
        self.to_sibling = 1 - 2 * core
        across_row = 4 * (1 - 2 * row)
        across_column = 2 * (1 - 2 * column)
        self.to_second = (1 - core) * across_row + core * across_column
        self.to_third = (1 - core) * across_column + core * across_row
        self.sibling = me + self.to_sibling
        self.second = me + self.to_second
        self.third = me + self.to_third
        self.above = [lax.rem(self.layer + step, LAYERS) for step in (1, 2, 3)]


class Chunk:
    def __init__(self, kind, groups, cols):
        self.kind, self.groups, self.cols = kind, groups, cols

    def line(self, refs, seat):
        return refs[self.kind].at[:, seat, self.groups, :, self.cols]

    def block(self, refs, layer, seat):
        return refs[self.kind].at[layer, seat, self.groups, :, self.cols]

    def bulk(self, refs, layers, lines):
        return refs[self.kind].at[pl.ds(0, layers), pl.ds(0, lines), self.groups, :, self.cols]


def chunks_of(shapes):
    made = []
    for kind, (groups, _, width) in enumerate(shapes):
        if kind < 3:
            size = shapes[1][2]
            for start in range(0, width, size):
                made.append(Chunk(kind, pl.ds(0, groups), pl.ds(start, size)))
        else:
            size = shapes[0][0]
            for start in range(0, groups, size):
                made.append(Chunk(kind, pl.ds(start, size), pl.ds(0, width)))
    return made


class Traffic:
    def __init__(self, spot, refs):
        self.spot = spot
        self.__dict__.update(refs)
        self.chunks = chunks_of([tuple(shard.shape) for shard in self.shards])


    def own(self, k):
        chunk, spot = self.chunks[k], self.spot
        source = self.shards[chunk.kind].at[chunk.groups, :, chunk.cols]
        target = chunk.block(self.full, spot.layer, spot.seat)
        for layer in spot.above:
            remote(
                source, target, self.sent.at[k], self.along_in.at[k], layer * ROWS + spot.seat
            ).start()

    def line_out(self, k, seat, device, sem):
        line = self.chunks[k].line(self.full, seat)
        remote(line, line, self.sent.at[k], sem, device).start()

    def wait_lines(self, k, sem, count=1):
        chunk = self.chunks[k]
        here = chunk.bulk(self.full, 3 if count == 3 else LAYERS, 1 if count == 3 else count)
        return remote(here, here, self.sent.at[k], sem, self.spot.me)

    def from_line(self, k):
        spot = self.spot
        self.wait_lines(k, self.along_in.at[k], 3).wait_recv()
        self.line_out(k, spot.seat, spot.second, self.second_in.at[k])
        self.line_out(k, spot.seat, spot.third, self.third_in.at[k, 0])
        self.line_out(k, spot.seat, spot.sibling, self.sibling_in.at[k])

    def from_second(self, k):
        spot = self.spot
        self.wait_lines(k, self.second_in.at[k]).wait_recv()
        seat = spot.seat + spot.to_second
        self.line_out(k, seat, spot.third, self.third_in.at[k, 1])
        self.line_out(k, seat, spot.sibling, self.sibling_in.at[k])

    def from_third(self, k, which):
        spot = self.spot
        self.wait_lines(k, self.third_in.at[k, which]).wait_recv()
        seat = spot.seat + spot.to_third + which * spot.to_second
        self.line_out(k, seat, spot.sibling, self.sibling_in.at[k])

    def complete(self, k):
        self.wait_lines(k, self.sibling_in.at[k], 4).wait_recv()

    def own_sent(self, k):
        self.wait_lines(k, self.sent.at[k], 7).wait_send()
        self.wait_lines(k, self.sent.at[k], 3).wait_send()


    def exchange(self, source, target, which, first=0, last=COUNT - 1):
        me = self.spot.me

        def go(step, carry):
            device = lax.rem(me + lax.rem(step * 5, COUNT), COUNT)
            remote(
                source.at[:, device],
                target.at[:, me],
                self.given.at[which],
                self.taken.at[which],
                device,
            ).start()
            return carry

        lax.fori_loop(1 + first, 1 + last, go, 0)

    def exchanged(self, target, which):
        here = target.at[:, pl.ds(0, COUNT - 1)]
        return remote(
            here,
            here,
            self.given.at[which],
            self.taken.at[which],
            self.spot.me,
        )

    def exchange_small(self, source, target, which):
        me = self.spot.me

        def go(step, carry):
            device = lax.rem(me + step, COUNT)
            remote(
                source if which == 4 else source.at[device],
                target.at[me],
                self.given.at[which],
                self.taken.at[which],
                device,
            ).start()
            return carry

        lax.fori_loop(1, COUNT, go, 0)

    def exchanged_small(self, target, which):
        here = target.at[pl.ds(0, COUNT - 1)]
        return remote(here, here, self.given.at[which], self.taken.at[which], self.spot.me)


    def move(self, k, seat, landing, device, sem):
        remote(
            self.chunks[k].line(self.partial, seat), landing, self.shed.at[k], sem, device
        ).start()

    def landing(self, k, landings, slot):
        chunk = self.chunks[k]
        return landings[chunk.kind].at[slot, :, chunk.groups, :, chunk.cols]

    def landed(self, k, landings, sem):
        chunk = self.chunks[k]
        here = landings[chunk.kind].at[:, :, chunk.groups, :, chunk.cols]
        remote(here, here, self.shed.at[k], sem, self.spot.me).wait_recv()

    def take_in(self, k, seat, landings, slot):
        chunk = self.chunks[k]
        line, here = chunk.line(self.partial, seat), self.landing(k, landings, slot)
        line[...] = line[...] + here[...]

    def begin(self, k):
        spot = self.spot
        for slot in range(4):
            seat = 2 * slot + (spot.seat + 1) % 2
            self.move(
                k, seat, self.landing(k, self.land_first, slot), spot.sibling, self.first_in.at[k]
            )

    def to_third(self, k):
        spot = self.spot
        self.landed(k, self.land_first, self.first_in.at[k])
        for slot in range(4):
            self.take_in(k, 2 * slot + spot.seat % 2, self.land_first, slot)
        for slot in range(2):
            seat = spot.seat + spot.to_third + slot * spot.to_second
            self.move(
                k, seat, self.landing(k, self.land_third, slot), spot.third, self.across_in.at[k]
            )

    def to_second(self, k):
        spot = self.spot
        self.landed(k, self.land_third, self.across_in.at[k])
        for slot in range(2):
            self.take_in(k, spot.seat + slot * spot.to_second, self.land_third, slot)
        seat = spot.seat + spot.to_second
        self.move(k, seat, self.landing(k, self.land_second, 0), spot.second, self.over_in.at[k])

    def to_owner(self, k):
        chunk, spot = self.chunks[k], self.spot
        self.landed(k, self.land_second, self.over_in.at[k])
        self.take_in(k, spot.seat, self.land_second, 0)
        target = self.sums[chunk.kind].at[spot.layer, chunk.groups, :, chunk.cols]
        for layer in spot.above:
            remote(
                chunk.block(self.partial, layer, spot.seat),
                target,
                self.shed.at[k],
                self.owner_in.at[k],
                layer * ROWS + spot.seat,
            ).start()
        self.keep(k).start()

    def keep(self, k):
        chunk, spot = self.chunks[k], self.spot
        return pltpu.make_async_copy(
            chunk.block(self.partial, spot.layer, spot.seat),
            self.sums[chunk.kind].at[spot.layer, chunk.groups, :, chunk.cols],
            self.kept.at[k],
        )

    def settle(self, k):
        chunk = self.chunks[k]
        here = self.sums[chunk.kind].at[pl.ds(0, 3), chunk.groups, :, chunk.cols]
        remote(here, here, self.shed.at[k], self.owner_in.at[k], self.spot.me).wait_recv()
        self.keep(k).wait()
        for count in (7, 3):
            there = chunk.bulk(self.partial, 3 if count == 3 else LAYERS, 1 if count == 3 else count)
            remote(there, there, self.shed.at[k], self.owner_in.at[k], self.spot.me).wait_send()


def interleave(count, body, steps=()):
    assert len(steps) <= count

    def one(index, carry):
        body(index)
        for place, thunks in enumerate(steps):
            if thunks:

                @pl.when(index == place)
                def _():
                    for thunk in thunks:
                        thunk()

        return carry

    lax.fori_loop(0, count, one, 0)


def unroll(count, body, steps):
    for index in range(count):
        body(index)
        for thunk in steps[index]:
            thunk()


def spread(thunks, slots):
    return [
        thunks[len(thunks) * place // slots : len(thunks) * (place + 1) // slots]
        for place in range(slots)
    ]


LEAD, TOKENS_EACH, COTANGENT_FROM, COTANGENT_EACH = 1, 6, 5, 5


def step_kernel(trees, *given):
    given, named = list(given), {}
    for tree in trees:
        named.update(jax.tree.unflatten(tree, given[: tree.num_leaves]))
        given = given[tree.num_leaves :]
    refs = types.SimpleNamespace(**named)
    spot = Spot()
    me = spot.me
    traffic = Traffic(spot, named)
    chunks = range(len(traffic.chunks))
    tokens, cotangent = refs.tokens, refs.cotangent
    sequence, upstream = refs.sequence, refs.upstream
    first_spare, second_spare = refs.first_spare, refs.second_spare

    locals_ = [
        pltpu.make_async_copy(
            traffic.shards[kind], traffic.full[kind].at[spot.layer, spot.seat], traffic.local.at[kind]
        )
        for kind in range(4)
    ] + [
        pltpu.make_async_copy(cotangent, first_spare, traffic.local.at[4]),
        pltpu.make_async_copy(tokens.at[:, me], sequence.at[:, me], traffic.local.at[5]),
        pltpu.make_async_copy(refs.small_own, refs.small.at[me], traffic.local.at[6]),
    ]
    for copy in locals_:
        copy.start()
    meet_all(me)

    def piece_of(source, target, which, first, last):
        return lambda: traffic.exchange(source, target, which, first, last)

    def do(method, *args):
        return lambda: method(*args)

    layer = Layer(named)
    layer.context_grad, layer.preact_grad = refs.hidden_low, refs.active
    layer.result, layer.input_grad = first_spare, second_spare
    layer.weight_in, layer.weight_mix, layer.weight_up, layer.weight_down = refs.full
    layer.in_grad, layer.mix_grad, layer.up_grad, layer.down_grad = refs.partial
    layer.lengths = [refs.lengths[batch, me] for batch in range(2)]
    tiles, wide = layer.width // TILE, layer.hidden_width // TILE
    pairs = 2 * (layer.width // PAIR)
    ins = 3
    ups = wide // tiles
    assert len(chunks) == ins + 1 + 2 * ups

    ticks = []
    for tick in range(-LEAD, len(chunks) + 2):
        here = []
        if 0 <= tick + LEAD < len(chunks):
            here.append(do(traffic.own, tick + LEAD))
        first = (tick + LEAD) * TOKENS_EACH
        if first < COUNT - 1:
            last = min(first + TOKENS_EACH, COUNT - 1)
            here.append(piece_of(tokens, sequence, 0, first, last))
        if tick == -LEAD:
            here.append(do(traffic.exchange_small, refs.small_own, refs.small, 4))
        if 0 <= tick < len(chunks):
            here.append(do(traffic.from_line, tick))
        if 0 <= tick - 1 < len(chunks):
            here.append(do(traffic.from_second, tick - 1))
            here.append(do(traffic.from_third, tick - 1, 0))
        if 0 <= tick - 2 < len(chunks):
            here.append(do(traffic.from_third, tick - 2, 1))
        first = (tick - COTANGENT_FROM) * COTANGENT_EACH
        if 0 <= first < COUNT - 1:
            last = min(first + COTANGENT_EACH, COUNT - 1)
            here.append(piece_of(second_spare, upstream, 1, first, last))
        ticks.append(here)
    flat = lambda first, last: [thunk for here in ticks[first + LEAD : last + LEAD] for thunk in here]

    for thunk in flat(-LEAD, 0):
        thunk()
    for copy in locals_:
        copy.wait()
    layer.terms[...] = jnp.zeros_like(layer.terms)
    for batch in range(2):
        for seat in range(COUNT):
            second_spare[batch, seat] = first_spare[batch, refs.backward_order[batch, seat]]
    own_upstream = pltpu.make_async_copy(
        second_spare.at[:, me], upstream.at[:, me], traffic.local.at[7]
    )
    own_upstream.start()
    for thunk in flat(0, 2):
        thunk()
    traffic.exchanged_small(refs.small, 4).wait_recv()
    layer.spread_small()
    for thunk in flat(2, ins + 2):
        thunk()
    traffic.exchanged(sequence, 0).wait_recv()
    for k in range(ins):
        traffic.complete(k)
    interleave(3 * tiles, layer.project, spread(flat(ins + 2, ins + 3), 3 * tiles))
    interleave(pairs, layer.attend, spread(flat(ins + 3, ins + 6), pairs))
    traffic.complete(ins)
    interleave(layer.rows // TILE, layer.mix)
    for thunk in flat(ins + 6, ins + ups + 3):
        thunk()
    for k in range(ins + 1, ins + 1 + ups):
        traffic.complete(k)
    interleave(wide, layer.up, spread(flat(ins + ups + 3, len(chunks) + 2), wide))
    for k in range(ins + 1 + ups, len(chunks)):
        traffic.complete(k)
    interleave(tiles, layer.down)
    own_upstream.wait()
    cotangents = traffic.exchanged(upstream, 1)
    cotangents.wait_recv()
    interleave(layer.rows // 128, layer.finish)

    keep_result = pltpu.make_async_copy(
        first_spare.at[:, me], refs.returned.at[:, me], traffic.local.at[0]
    )
    keep_result.start()
    pieces = [
        piece_of(first_spare, refs.returned, 2, first, min(first + 4, COUNT - 1))
        for first in range(0, COUNT - 1, 4)
    ]
    interleave(LAYERS, layer.down_weight_grad, spread(pieces, LAYERS))

    queue = list(range(ins + 1 + ups, len(chunks))) + list(range(ins + 1, ins + 1 + ups))
    queue += [ins] + list(range(ins))
    walk = []
    for tick in range(len(queue) + 2):
        for late, stage in enumerate((traffic.to_third, traffic.to_second, traffic.to_owner)):
            if 0 <= tick - late < len(queue):
                walk.append(do(stage, queue[tick - late]))

    def next_steps(count):
        taken, walk[:] = walk[:count], walk[count:]
        return taken

    def with_begin(steps, count, every, kinds):
        made = [list(step) for step in steps] + [[] for _ in range(count - len(steps))]
        for place, k in enumerate(kinds):
            made[(place + 1) * every - 1].insert(0, do(traffic.begin, k))
        return made

    for k in queue[:ups]:
        traffic.begin(k)
    interleave(LAYERS, layer.active_backward, spread(next_steps(3), LAYERS))
    interleave(
        wide,
        layer.up_weight_grad,
        with_begin(spread(next_steps(3), wide), wide, tiles, queue[ups : 2 * ups]),
    )
    unroll(tiles, layer.hidden_backward, spread(next_steps(2), tiles))
    interleave(layer.rows // 128, layer.first_backward, spread(next_steps(1), 1))
    interleave(
        tiles,
        layer.mix_weight_grad,
        with_begin(spread(next_steps(1), tiles), tiles, tiles, queue[2 * ups : 2 * ups + 1]),
    )
    unroll(tiles, layer.mix_backward, spread(next_steps(1), tiles))
    interleave(pairs, layer.attend_backward, spread(next_steps(5), pairs))
    interleave(
        3 * tiles,
        layer.in_weight_grad,
        with_begin(spread(next_steps(3), 3 * tiles), 3 * tiles, tiles, queue[2 * ups + 1 :]),
    )
    layer.gather_terms()
    traffic.exchange_small(refs.small_grad, refs.small_sums, 5)
    keep_small = pltpu.make_async_copy(
        refs.small_grad.at[me], refs.small_sums.at[me], traffic.local.at[1]
    )
    keep_small.start()
    cotangents.wait_send()
    unroll(tiles, layer.input_backward, spread(next_steps(1), tiles))
    keep_grad = pltpu.make_async_copy(
        second_spare.at[:, me], refs.tokens_grad.at[:, me], traffic.local.at[2]
    )
    keep_grad.start()
    left = next_steps(len(walk))
    cuts = list(range(0, COUNT - 1, 4))
    for place in range(max(len(left), len(cuts))):
        if place < len(cuts):
            piece_of(
                second_spare, refs.tokens_grad, 3, cuts[place], min(cuts[place] + 4, COUNT - 1)
            )()
        if place < len(left):
            left[place]()
    for k in queue:
        traffic.settle(k)
        traffic.own_sent(k)
    traffic.exchanged(sequence, 0).wait_send()
    for target, which in ((refs.returned, 2), (refs.tokens_grad, 3)):
        copy = traffic.exchanged(target, which)
        copy.wait_recv()
        copy.wait_send()
    traffic.exchanged_small(refs.small, 4).wait_send()
    small = traffic.exchanged_small(refs.small_sums, 5)
    small.wait_recv()
    small.wait_send()
    for copy in (keep_result, keep_small, keep_grad):
        copy.wait()


def encoder_step(lengths, backward_order, tokens, cotangent, shards, small_own):
    low, full = jnp.bfloat16, jnp.float32
    width, hidden_width = tokens.shape[-1], shards[2].shape[-1]
    rows = tokens.shape[0] * COUNT * tokens.shape[2]
    anywhere = pl.BlockSpec(memory_space=pl.ANY)
    inputs = dict(
        lengths=lengths,
        backward_order=backward_order,
        tokens=tokens,
        cotangent=cotangent,
        shards=shards,
        small_own=small_own,
    )
    shapes = [shard.shape for shard in shards]
    smalls = ((COUNT,) + small_own.shape, full)
    outputs = dict(
        returned=jax.ShapeDtypeStruct(tokens.shape, low),
        tokens_grad=jax.ShapeDtypeStruct(tokens.shape, low),
        sums=[jax.ShapeDtypeStruct((LAYERS,) + shape, low) for shape in shapes],
        small_sums=jax.ShapeDtypeStruct(*smalls),
    )
    sequences = pltpu.VMEM(tokens.shape, low)
    scratch = dict(
        full=[pltpu.VMEM((LAYERS, ROWS) + shape, low) for shape in shapes],
        partial=[pltpu.VMEM((LAYERS, ROWS) + shape, low) for shape in shapes],
        land_first=[pltpu.VMEM((4, LAYERS) + shape, low) for shape in shapes],
        land_third=[pltpu.VMEM((2, LAYERS) + shape, low) for shape in shapes],
        land_second=[pltpu.VMEM((1, LAYERS) + shape, low) for shape in shapes],
        sequence=sequences,
        upstream=sequences,
        first_spare=sequences,
        second_spare=sequences,
        small=pltpu.VMEM(*smalls),
        small_grad=pltpu.VMEM(*smalls),
        **scratch_of(rows, width, hidden_width),
    )
    count = len(chunks_of(shapes))
    each = pltpu.SemaphoreType.DMA((count,))
    sems = dict(
        local=pltpu.SemaphoreType.DMA((8,)),
        given=pltpu.SemaphoreType.DMA((6,)),
        taken=pltpu.SemaphoreType.DMA((6,)),
        third_in=pltpu.SemaphoreType.DMA((count, 2)),
        sent=each,
        along_in=each,
        second_in=each,
        sibling_in=each,
        shed=each,
        first_in=each,
        across_in=each,
        over_in=each,
        owner_in=each,
        kept=each,
    )
    smem = pl.BlockSpec(memory_space=pltpu.SMEM)
    given, given_tree = jax.tree.flatten(inputs)
    in_specs = [smem if leaf.dtype == jnp.int32 else anywhere for leaf in given]
    made, made_tree = jax.tree.flatten(outputs)
    held, held_tree = jax.tree.flatten({**scratch, **sems})
    results = pl.pallas_call(
        functools.partial(step_kernel, (given_tree, made_tree, held_tree)),
        out_shape=made,
        in_specs=in_specs,
        out_specs=[anywhere] * len(made),
        scratch_shapes=held,
        compiler_params=pltpu.CompilerParams(
            collective_id=0, has_side_effects=True, vmem_limit_bytes=VMEM_LIMIT
        ),
        name="encoder_step",
    )(*given)
    results = jax.tree.unflatten(made_tree, results)
    return types.SimpleNamespace(**results)


VMEM_LIMIT = 63 << 20


def finish_kernel(order, *refs):
    sources, refs = refs[:7], refs[7:]
    layer_out, tokens_grad, refs = refs[0], refs[1], refs[2:]
    totals, outs, inner, sems = refs[:4], refs[4:12], refs[12:19], refs[19]
    copies = [
        pltpu.make_async_copy(source, target, sems.at[place])
        for place, (source, target) in enumerate(zip(sources, inner))
    ]
    for copy in copies:
        copy.start()
    copies[0].wait()
    for batch in range(2):
        for seat in range(COUNT):
            layer_out[batch, seat] = inner[0][batch, order[batch, seat]]
    copies[1].wait()
    tokens_grad[...] = inner[1][...]
    for total, parts, copy in zip(totals, inner[2:6], copies[2:6]):
        copy.wait()
        total[...] = sum(parts[layer].astype(jnp.float32) for layer in range(LAYERS))
    copies[6].wait()
    small = jnp.sum(inner[6][...], 0)
    for place, out in enumerate(outs):
        out[...] = small[place : place + 1, : out.shape[1]]


def finish_step(order, returned, tokens_grad, sums, small_sums):
    inside = pl.BlockSpec(memory_space=pltpu.VMEM)
    parts = [returned, tokens_grad, *sums, small_sums]
    return pl.pallas_call(
        finish_kernel,
        out_shape=[jax.ShapeDtypeStruct(returned.shape, returned.dtype)] * 2
        + [jax.ShapeDtypeStruct(part.shape[1:], jnp.float32) for part in sums]
        + [jax.ShapeDtypeStruct((1, width), jnp.float32) for width in WIDTHS],
        in_specs=[pl.BlockSpec(memory_space=pltpu.SMEM)]
        + [pl.BlockSpec(memory_space=pltpu.HBM)] * 7,
        out_specs=[inside] * 14,
        scratch_shapes=[pltpu.VMEM(part.shape, part.dtype) for part in parts]
        + [pltpu.SemaphoreType.DMA((7,))],
        compiler_params=pltpu.CompilerParams(vmem_limit_bytes=VMEM_LIMIT),
        name="finish_step",
    )(order, *parts)


SMALL = (1, 3, 4, 5, 7, 9, 10, 11)
LARGE = (0, 2, 6, 8)


def local(tokens, lengths, order, *rest):
    shards, cotangent = rest[:12], rest[12]
    if lax.axis_size("dp") != COUNT or tokens.shape[2] % 8:
        return portable(tokens, lengths, order, *rest)
    small = sum(
        lax.pad(
            shards[i].astype(jnp.float32)[None],
            jnp.float32(0),
            ((place, len(SMALL) - 1 - place, 0), (0, 128 - shards[i].shape[0], 0)),
        )
        for place, i in enumerate(SMALL)
    )
    slots = lax.broadcasted_iota(jnp.int32, order.shape + (COUNT,), 1)
    targets = lax.broadcasted_iota(jnp.int32, order.shape + (COUNT,), 2)
    backward_order = jnp.sum(jnp.where(order[:, :, None] == targets, slots, 0), 1)
    made = encoder_step(
        lengths,
        backward_order,
        tokens,
        cotangent,
        [shards[i].reshape(-1, 8, shards[i].shape[-1]) for i in LARGE],
        small,
    )
    layer_out, tokens_grad, *rest = finish_step(
        order, made.returned, made.tokens_grad, made.sums, made.small_sums
    )
    outputs = [None] * 12
    for i, total in zip(LARGE, rest[:4]):
        outputs[i] = total.reshape(-1, total.shape[-1])
    for i, total in zip(SMALL, rest[4:]):
        outputs[i] = total.reshape(-1)
    return (layer_out, tokens_grad, *outputs)


def solution(mesh):
    return jax.shard_map(
        local,
        mesh=mesh,
        in_specs=(
            P(None, None, "dp", None),
            P(),
            P(),
            P("dp", None),
            P("dp"),
            P("dp", None),
            P("dp"),
            P("dp"),
            P("dp"),
            P("dp", None),
            P("dp"),
            P("dp", None),
            P("dp"),
            P("dp"),
            P("dp"),
            P(None, None, "dp", None),
        ),
        out_specs=(
            P(None, None, "dp", None),
            P(None, None, "dp", None),
            P("dp", None),
            P("dp"),
            P("dp", None),
            P("dp"),
            P("dp"),
            P("dp"),
            P("dp", None),
            P("dp"),
            P("dp", None),
            P("dp"),
            P("dp"),
            P("dp"),
        ),
        check_vma=False,
    )
```

```python
import functools
import types

import jax
import jax.numpy as jnp
from jax import lax
from jax.experimental import pallas as pl
from jax.experimental.pallas import tpu as pltpu
from jax.sharding import PartitionSpec as P

MESH = pl.DeviceIdType.MESH

HD = 64


epsilon = 1e-12


def matmul(left, right):
    return jnp.dot(left, right, preferred_element_type=jnp.float32)


def rows_product(left, right):
    return lax.dot_general(
        left, right, (((0,), (0,)), ((), ())), preferred_element_type=jnp.float32
    )


def right_transposed(left, right):
    return lax.dot_general(
        left, right, (((1,), (1,)), ((), ())), preferred_element_type=jnp.float32
    )


def split_heads(block, heads):
    return block.reshape(block.shape[0], heads, -1).transpose(1, 0, 2)


def join_heads(block):
    return block.transpose(1, 0, 2).reshape(block.shape[1], -1)


def norm_forward(summed, norm_gain, norm_shift):
    row_mean = jnp.mean(summed, -1, keepdims=True)
    centered = summed - row_mean
    reciprocal = lax.rsqrt(jnp.mean(centered * centered, -1, keepdims=True) + epsilon)
    normed = centered * reciprocal
    return (normed * norm_gain + norm_shift, normed, reciprocal)


def norm_backward(upstream, normed, reciprocal, norm_gain):
    scaled = upstream * norm_gain
    summed_grad = reciprocal * (
        scaled
        - jnp.mean(scaled, -1, keepdims=True)
        - normed * jnp.mean(scaled * normed, -1, keepdims=True)
    )
    return (summed_grad, jnp.sum(upstream * normed, 0), jnp.sum(upstream, 0))


def head_scores(head_query, head_keys, valid):
    scores = right_transposed(head_query, head_keys) * 0.125
    return jnp.where(valid[None, :], scores, -1e30)


def attend_forward(packed, valid):
    head_query, head_keys, head_values = packed
    scores = head_scores(head_query, head_keys, valid)
    row_max = jnp.max(scores, -1, keepdims=True)
    weights_raw = jnp.exp(scores - row_max)
    row_sum = jnp.sum(weights_raw, -1, keepdims=True)
    probability = weights_raw / row_sum
    context = matmul(probability.astype(jnp.bfloat16), head_values)
    return (context, (row_max + jnp.log(row_sum))[:, 0])


def attend_backward(packed, valid):
    head_query, head_keys, head_values, context_grad, log_total = packed
    scores = head_scores(head_query, head_keys, valid)
    probability = jnp.exp(scores - log_total[:, None])
    low_prob = probability.astype(jnp.bfloat16)
    prob_grad = right_transposed(context_grad, head_values)
    value_grad = rows_product(low_prob, context_grad)
    shifted = prob_grad - jnp.sum(probability * prob_grad, -1, keepdims=True)
    score_grad = (probability * shifted).astype(jnp.bfloat16)
    query_grad = matmul(score_grad, head_keys) * 0.125
    key_grad = rows_product(score_grad, head_query) * 0.125
    return (query_grad, key_grad, value_grad)


def forward(weights, sequence, length):
    (
        weight_in,
        bias_in,
        weight_mix,
        bias_mix,
        gain_first,
        shift_first,
        weight_up,
        bias_up,
        weight_down,
        bias_down,
        gain_second,
        shift_second,
    ) = weights
    width = sequence.shape[1]
    heads = width // HD
    valid = jnp.arange(sequence.shape[0], dtype=jnp.int32) < length
    bias_full = jnp.concatenate(
        [
            bias_in[:width].astype(jnp.float32),
            jnp.zeros((width,), jnp.float32),
            bias_in[width:].astype(jnp.float32),
        ]
    )
    projected = (matmul(sequence, weight_in) + bias_full).astype(jnp.bfloat16)
    queries = split_heads(projected[:, :width], heads)
    key_heads = split_heads(projected[:, width : 2 * width], heads)
    value_heads = split_heads(projected[:, 2 * width :], heads)
    context, log_total = lax.map(
        lambda packed: attend_forward(packed, valid), (queries, key_heads, value_heads)
    )
    context_low = join_heads(context).astype(jnp.bfloat16)
    branch = matmul(context_low, weight_mix) + bias_mix.astype(jnp.float32)
    hidden, normed_first, recip_first = norm_forward(
        sequence.astype(jnp.float32) + branch,
        gain_first.astype(jnp.float32),
        shift_first.astype(jnp.float32),
    )
    hidden_low = hidden.astype(jnp.bfloat16)
    preact = matmul(hidden_low, weight_up) + bias_up.astype(jnp.float32)
    activated = jax.nn.gelu(preact, approximate=False).astype(jnp.bfloat16)
    feed_out = matmul(activated, weight_down) + bias_down.astype(jnp.float32)
    result, normed_second, recip_second = norm_forward(
        hidden + feed_out, gain_second.astype(jnp.float32), shift_second.astype(jnp.float32)
    )
    stored = (
        valid,
        queries,
        key_heads,
        value_heads,
        log_total,
        context_low,
        normed_first,
        recip_first,
        hidden_low,
        preact,
        activated,
        normed_second,
        recip_second,
    )
    return (result.astype(jnp.bfloat16), stored)


def backward(weights, sequence, upstream_low, stored):
    (
        weight_in,
        bias_in,
        weight_mix,
        bias_mix,
        gain_first,
        shift_first,
        weight_up,
        bias_up,
        weight_down,
        bias_down,
        gain_second,
        shift_second,
    ) = weights
    (
        valid,
        queries,
        key_heads,
        value_heads,
        log_total,
        context_low,
        normed_first,
        recip_first,
        hidden_low,
        preact,
        activated,
        normed_second,
        recip_second,
    ) = stored
    width = sequence.shape[1]
    heads = width // HD
    upstream = upstream_low.astype(jnp.float32)
    second_grad, gain_second_grad, shift_second_grad = norm_backward(
        upstream, normed_second, recip_second, gain_second.astype(jnp.float32)
    )
    feed_grad = second_grad.astype(jnp.bfloat16)
    bias_down_grad = jnp.sum(feed_grad.astype(jnp.float32), 0)
    weight_down_grad = rows_product(activated, feed_grad)
    act_grad = right_transposed(feed_grad, weight_down)
    slope = (
        0.5 * (1.0 + jax.scipy.special.erf(preact * 0.7071067811865476))
        + preact * jnp.exp(-0.5 * preact * preact) * 0.3989422804014327
    )
    preact_grad = (act_grad * slope).astype(jnp.bfloat16)
    bias_up_grad = jnp.sum(preact_grad.astype(jnp.float32), 0)
    weight_up_grad = rows_product(hidden_low, preact_grad)
    hidden_grad = second_grad + right_transposed(preact_grad, weight_up)
    first_grad, gain_first_grad, shift_first_grad = norm_backward(
        hidden_grad, normed_first, recip_first, gain_first.astype(jnp.float32)
    )
    branch_grad = first_grad.astype(jnp.bfloat16)
    bias_mix_grad = jnp.sum(branch_grad.astype(jnp.float32), 0)
    weight_mix_grad = rows_product(context_low, branch_grad)
    context_grad = right_transposed(branch_grad, weight_mix).astype(jnp.bfloat16)
    query_grad, key_grad, value_grad = lax.map(
        lambda packed: attend_backward(packed, valid),
        (queries, key_heads, value_heads, split_heads(context_grad, heads), log_total),
    )
    projected_grad = jnp.concatenate(
        [join_heads(query_grad), join_heads(key_grad), join_heads(value_grad)], -1
    ).astype(jnp.bfloat16)
    column_sums = jnp.sum(projected_grad.astype(jnp.float32), 0)
    bias_in_grad = jnp.concatenate([column_sums[:width], column_sums[2 * width :]])
    weight_in_grad = rows_product(sequence, projected_grad)
    input_grad = (first_grad + right_transposed(projected_grad, weight_in)).astype(jnp.bfloat16)
    gradients = (
        weight_in_grad,
        bias_in_grad,
        weight_mix_grad,
        bias_mix_grad,
        gain_first_grad,
        shift_first_grad,
        weight_up_grad,
        bias_up_grad,
        weight_down_grad,
        bias_down_grad,
        gain_second_grad,
        shift_second_grad,
    )
    return (input_grad, gradients)


def permuted(blocks, picks):
    chosen = (picks[:, None] == jnp.arange(picks.shape[0])[None, :]).astype(blocks.dtype)
    flat = blocks.reshape(blocks.shape[0], -1)
    return matmul(chosen, flat).astype(blocks.dtype).reshape(blocks.shape)


def inverse_of(picks):
    slots = jnp.arange(picks.shape[0], dtype=jnp.int32)
    return jnp.sum(jnp.where(picks[:, None] == slots[None, :], slots[:, None], 0), 0)


def fetch_weights(shards):
    return (
        lax.all_gather(shards[0], "dp", axis=0, tiled=True),
        lax.all_gather(shards[1], "dp", axis=0, tiled=True),
        lax.all_gather(shards[2], "dp", axis=0, tiled=True),
        lax.all_gather(shards[3], "dp", axis=0, tiled=True),
        lax.all_gather(shards[4], "dp", axis=0, tiled=True),
        lax.all_gather(shards[5], "dp", axis=0, tiled=True),
        lax.all_gather(shards[6], "dp", axis=0, tiled=True),
        lax.all_gather(shards[7], "dp", axis=0, tiled=True),
        lax.all_gather(shards[8], "dp", axis=0, tiled=True),
        lax.all_gather(shards[9], "dp", axis=0, tiled=True),
        lax.all_gather(shards[10], "dp", axis=0, tiled=True),
        lax.all_gather(shards[11], "dp", axis=0, tiled=True),
    )


def add_trees(first, second):
    if first is None:
        return second
    return jax.tree.map(lambda left, right: left + right, first, second)


def portable(
    tokens,
    lengths,
    order,
    weight_in,
    bias_in,
    weight_mix,
    bias_mix,
    gain_first,
    shift_first,
    weight_up,
    bias_up,
    weight_down,
    bias_down,
    gain_second,
    shift_second,
    cotangent,
):
    shards = (
        weight_in,
        bias_in,
        weight_mix,
        bias_mix,
        gain_first,
        shift_first,
        weight_up,
        bias_up,
        weight_down,
        bias_down,
        gain_second,
        shift_second,
    )
    device = lax.axis_index("dp")
    totals = None
    outputs_list = []
    grads_list = []
    for batch in range(tokens.shape[0]):
        current = fetch_weights(shards)
        picks = order[batch]
        dealt_tokens = permuted(tokens[batch], picks)
        sequence, upstream = (
            lax.all_to_all(dealt_tokens, "dp", split_axis=0, concat_axis=1, tiled=True),
            lax.all_to_all(cotangent[batch], "dp", split_axis=0, concat_axis=1, tiled=True),
        )
        length = jnp.sum(jnp.where(jnp.arange(picks.shape[0]) == picks[device], lengths[batch], 0))
        result, stored = forward(current, sequence[0], length)
        behind = (
            lax.all_gather(shards[0], "dp", axis=0, tiled=True),
            lax.all_gather(shards[1], "dp", axis=0, tiled=True),
            lax.all_gather(shards[2], "dp", axis=0, tiled=True),
            lax.all_gather(shards[3], "dp", axis=0, tiled=True),
            lax.all_gather(shards[4], "dp", axis=0, tiled=True),
            lax.all_gather(shards[5], "dp", axis=0, tiled=True),
            lax.all_gather(shards[6], "dp", axis=0, tiled=True),
            lax.all_gather(shards[7], "dp", axis=0, tiled=True),
            lax.all_gather(shards[8], "dp", axis=0, tiled=True),
            lax.all_gather(shards[9], "dp", axis=0, tiled=True),
            lax.all_gather(shards[10], "dp", axis=0, tiled=True),
            lax.all_gather(shards[11], "dp", axis=0, tiled=True),
        )
        input_grad, gradients = backward(behind, sequence[0], upstream[0], stored)
        back_out, back_grad = (
            lax.all_to_all(result[None], "dp", split_axis=1, concat_axis=0, tiled=True),
            lax.all_to_all(input_grad[None], "dp", split_axis=1, concat_axis=0, tiled=True),
        )
        restored = permuted(back_grad, inverse_of(picks))
        outputs_list.append(back_out)
        grads_list.append(restored)
        totals = add_trees(totals, gradients)
    totals = (
        lax.psum_scatter(totals[0], "dp", scatter_dimension=0, tiled=True),
        lax.psum_scatter(totals[1], "dp", scatter_dimension=0, tiled=True),
        lax.psum_scatter(totals[2], "dp", scatter_dimension=0, tiled=True),
        lax.psum_scatter(totals[3], "dp", scatter_dimension=0, tiled=True),
        lax.psum_scatter(totals[4], "dp", scatter_dimension=0, tiled=True),
        lax.psum_scatter(totals[5], "dp", scatter_dimension=0, tiled=True),
        lax.psum_scatter(totals[6], "dp", scatter_dimension=0, tiled=True),
        lax.psum_scatter(totals[7], "dp", scatter_dimension=0, tiled=True),
        lax.psum_scatter(totals[8], "dp", scatter_dimension=0, tiled=True),
        lax.psum_scatter(totals[9], "dp", scatter_dimension=0, tiled=True),
        lax.psum_scatter(totals[10], "dp", scatter_dimension=0, tiled=True),
        lax.psum_scatter(totals[11], "dp", scatter_dimension=0, tiled=True),
    )
    return (
        jnp.stack(outputs_list),
        jnp.stack(grads_list),
        totals[0],
        totals[1],
        totals[2],
        totals[3],
        totals[4],
        totals[5],
        totals[6],
        totals[7],
        totals[8],
        totals[9],
        totals[10],
        totals[11],
    )


COUNT = 32
ROWS, LAYERS = 8, 4


def meet_all(me):
    barrier = pltpu.get_barrier_semaphore()

    def greet(step, carry):
        pl.semaphore_signal(
            barrier, inc=1, device_id=(lax.rem(me + step, COUNT),), device_id_type=MESH
        )
        return carry

    lax.fori_loop(1, COUNT, greet, 0)
    pl.semaphore_wait(barrier, COUNT - 1)


def remote(source, target, send_sem, recv_sem, device):
    return pltpu.make_async_remote_copy(
        src_ref=source,
        dst_ref=target,
        send_sem=send_sem,
        recv_sem=recv_sem,
        device_id=(device,),
        device_id_type=MESH,
    )


WIDTHS = (48, 24, 24, 24, 96, 24, 24, 24)
BIAS_IN, BIAS_MIX, GAIN_FIRST, SHIFT_FIRST, BIAS_UP, BIAS_DOWN, GAIN_SECOND, SHIFT_SECOND = range(8)
TILE = 256
PAIR = 128


def contract(left, right, left_dim, right_dim):
    return lax.dot_general(
        left,
        right,
        (((left_dim,), (right_dim,)), ((), ())),
        preferred_element_type=jnp.float32,
    )


def owners(width):
    lane = lax.broadcasted_iota(jnp.int32, (COUNT, COUNT * width), 1)
    owner = (lane * (-(-(1 << 20) // width))) >> 20
    device = lax.broadcasted_iota(jnp.int32, (COUNT, COUNT * width), 0)
    return owner == device


def places(width):
    lane = lax.broadcasted_iota(jnp.int32, (PAIR, COUNT * width), 1)
    owner = (lane * (-(-(1 << 20) // width))) >> 20
    entry = lax.broadcasted_iota(jnp.int32, (PAIR, COUNT * width), 0)
    return jnp.where(lane - owner * width == entry, 1.0, 0.0).astype(jnp.bfloat16)


def columns(tile, size=TILE):
    return pl.ds(pl.multiple_of(tile * size, size), size)


def flat(value):
    return value.reshape(-1, value.shape[-1])


def take_rows(ref, start, stop):
    layers, seats, groups, small, _ = ref.shape
    pieces = []
    while start < stop:
        layer, rest = divmod(start // small, seats * groups)
        seat, group = divmod(rest, groups)
        whole = min((stop - start) // (small * groups), seats - seat)
        if group == 0 and whole:
            pieces.append(flat(ref[layer, seat : seat + whole]))
            start += whole * groups * small
        else:
            end = min(groups, group + (stop - start) // small)
            pieces.append(flat(ref[layer, seat, group:end]))
            start += (end - group) * small
    return jnp.concatenate(pieces, 0)


class Layer:
    def __init__(self, refs):
        self.__dict__.update(refs)
        self.rows, self.width = self.normed.shape
        self.hidden_width = self.slope.shape[1]

    def spread_small(self):
        for place, width in enumerate(WIDTHS):
            given = self.small[:, place, :].astype(jnp.bfloat16)
            spread = contract(given, places(width), 1, 0)
            row = jnp.sum(jnp.where(owners(width), spread, 0.0), 0, keepdims=True)
            if place == BIAS_IN:
                self.bias_row[:, : self.width] = row[:, : self.width]
                self.bias_row[:, self.width : 2 * self.width] = jnp.zeros_like(row[:, : self.width])
                self.bias_row[:, 2 * self.width :] = row[:, self.width :]
            elif place == BIAS_UP:
                self.up_row[...] = row
            else:
                self.vectors[place : place + 1, :] = row

    def vector(self, place):
        return self.vectors[place : place + 1, :]

    def project(self, tile):
        here = columns(tile)
        value = jnp.dot(
            flat(self.sequence[...]),
            flat(self.weight_in[:, :, :, :, here]),
            preferred_element_type=jnp.float32
        )
        value = (value + self.bias_row[:, here]).astype(jnp.bfloat16)
        scale = jnp.where(tile < self.width // TILE, 0.125, 1.0).astype(jnp.bfloat16)
        self.packed[:, here] = value * scale

    def heads_of(self, step):
        pairs = self.width // PAIR
        batch, pair = step // pairs, step % pairs
        rows = pl.ds(pl.multiple_of(batch * TILE, TILE), TILE)
        return batch, pair, rows

    def block(self, part, rows, pair):
        offset = pl.multiple_of(part * self.width + pair * PAIR, PAIR)
        return self.packed[rows, pl.ds(offset, PAIR)]

    def half(self, value, head):
        lane = lax.broadcasted_iota(jnp.int32, value.shape, 1)
        keep = lane < PAIR // 2 if head == 0 else lane >= PAIR // 2
        return jnp.where(keep, value, jnp.zeros_like(value))

    def attend(self, step):
        batch, pair, rows = self.heads_of(step)
        queries, key_block, value_block = (self.block(part, rows, pair) for part in range(3))
        length = jnp.where(batch == 0, self.lengths[0], self.lengths[1])
        lane = lax.broadcasted_iota(jnp.int32, (1, TILE), 1)
        blocked = jnp.where(lane < length, 0.0, -1e30)
        context = []
        for head in range(2):
            scores = contract(self.half(queries, head), key_block, 1, 1) + blocked
            weights = jnp.exp(scores - jnp.max(scores, -1, keepdims=True))
            total = jnp.sum(weights, -1, keepdims=True)
            low = (weights * (1.0 / total)).astype(jnp.bfloat16)
            self.chances[2 * step + head] = low
            context.append(jnp.dot(low, value_block, preferred_element_type=jnp.float32))
        lane = lax.broadcasted_iota(jnp.int32, context[0].shape, 1)
        joined = jnp.where(lane < PAIR // 2, context[0], context[1])
        self.context[rows, columns(pair, PAIR)] = joined.astype(jnp.bfloat16)

    def mix(self, part):
        rows = columns(part)
        branch = jnp.dot(
            self.context[rows, :], flat(self.weight_mix[...]), preferred_element_type=jnp.float32
        )
        summed = flat(self.sequence[part]).astype(jnp.float32) + (branch + self.vector(BIAS_MIX))
        centered = summed - jnp.mean(summed, -1, keepdims=True)
        factor = lax.rsqrt(jnp.mean(centered * centered, -1, keepdims=True) + epsilon)
        normed = centered * factor
        hidden = normed * self.vector(GAIN_FIRST) + self.vector(SHIFT_FIRST)
        self.normed[rows, :] = normed
        self.factor[rows, :] = factor
        self.hidden_low[rows, :] = hidden.astype(jnp.bfloat16)

    def up(self, tile):
        here = columns(tile)
        value = jnp.dot(
            self.hidden_low[...], flat(self.weight_up[:, :, :, :, here]), preferred_element_type=jnp.float32
        )
        value = value + self.up_row[:, here]
        below = 0.5 * (1.0 + lax.erf(value * 0.7071067811865476))
        density = jnp.exp(-0.5 * value * value) * 0.3989422804014327
        self.active[:, here] = (value * below).astype(jnp.bfloat16)
        self.slope[:, here] = (below + value * density).astype(self.slope.dtype)

    def down(self, tile):
        here = columns(tile)
        self.upper[:, here] = jnp.dot(
            self.active[...], flat(self.weight_down[:, :, :, :, here]), preferred_element_type=jnp.float32
        )

    def finish(self, part, size=128):
        rows = columns(part, size)
        hidden = self.normed[rows, :] * self.vector(GAIN_FIRST) + self.vector(SHIFT_FIRST)
        summed = hidden + (self.upper[rows, :] + self.vector(BIAS_DOWN))
        centered = summed - jnp.mean(summed, -1, keepdims=True)
        factor = lax.rsqrt(jnp.mean(centered * centered, -1, keepdims=True) + epsilon)
        normed = centered * factor
        gain = self.vector(GAIN_SECOND)
        low = (normed * gain + self.vector(SHIFT_SECOND)).astype(jnp.bfloat16)
        parts, seats = TILE // size, size // 8
        batch, span = part // parts, pl.ds((part % parts) * seats, seats)
        self.result[batch, span] = low.reshape(seats, 8, self.width)
        upstream = flat(self.upstream[batch, span]).astype(jnp.float32)
        grad = self.norm_backward(upstream, normed, factor, gain, GAIN_SECOND, SHIFT_SECOND)
        low = grad.astype(jnp.bfloat16)
        self.upper[rows, :] = grad
        self.feed_grad[rows, :] = low
        self.add_term(BIAS_DOWN, low.astype(jnp.float32))

    def add_term(self, place, value):
        self.terms[place : place + 1, :] += jnp.sum(value, 0, keepdims=True)

    def norm_backward(self, upstream, normed, factor, gain, gain_place, shift_place):
        self.add_term(gain_place, upstream * normed)
        self.add_term(shift_place, upstream)
        scaled = upstream * gain
        return factor * (
            scaled
            - jnp.mean(scaled, -1, keepdims=True)
            - normed * jnp.mean(scaled * normed, -1, keepdims=True)
        )

    def down_weight_grad(self, layer):
        span = self.hidden_width // LAYERS
        made = [
            contract(self.active[:, columns(layer * (span // TILE) + i)], self.feed_grad[...], 0, 0)
            for i in range(span // TILE)
        ]
        made = jnp.concatenate([part.astype(jnp.bfloat16) for part in made], 0)
        self.down_grad[layer] = made.reshape(self.down_grad.shape[1:])

    def active_backward(self, layer):
        span = self.hidden_width // LAYERS
        weight = flat(self.weight_down[layer])
        for i in range(span // TILE):
            here = columns(layer * (span // TILE) + i)
            grad = contract(self.feed_grad[...], weight[i * TILE : (i + 1) * TILE], 1, 1)
            low = (grad * self.slope[:, here].astype(jnp.float32)).astype(jnp.bfloat16)
            self.preact_grad[:, here] = low
            self.up_terms[:, here] = jnp.sum(low.astype(jnp.float32), 0, keepdims=True)

    def up_weight_grad(self, tile):
        here = columns(tile)
        grad = contract(self.hidden_low[...], self.preact_grad[:, here], 0, 0)
        self.keep_columns(self.up_grad, here, grad)

    def hidden_backward(self, tile):
        here = columns(tile)
        weight = take_rows(self.weight_up, tile * TILE, (tile + 1) * TILE)
        self.upper[:, here] += contract(self.preact_grad[...], weight, 1, 1)

    def first_backward(self, part, size=128):
        rows = columns(part, size)
        grad = self.norm_backward(
            self.upper[rows, :],
            self.normed[rows, :],
            self.factor[rows, :],
            self.vector(GAIN_FIRST),
            GAIN_FIRST,
            SHIFT_FIRST,
        )
        low = grad.astype(jnp.bfloat16)
        self.upper[rows, :] = grad
        self.feed_grad[rows, :] = low
        self.add_term(BIAS_MIX, low.astype(jnp.float32))

    def mix_weight_grad(self, tile):
        here = columns(tile)
        grad = contract(self.context[...], self.feed_grad[:, here], 0, 0)
        self.keep_columns(self.mix_grad, here, grad)

    def mix_backward(self, tile):
        here = columns(tile)
        weight = take_rows(self.weight_mix, tile * TILE, (tile + 1) * TILE)
        self.context_grad[:, here] = contract(self.feed_grad[...], weight, 1, 1).astype(
            jnp.bfloat16
        )

    def attend_backward(self, step):
        batch, pair, rows = self.heads_of(step)
        queries, key_block, value_block = (self.block(part, rows, pair) for part in range(3))
        grads = self.context_grad[rows, columns(pair, PAIR)]
        query_grad = key_grad = value_grad = 0.0
        for head in range(2):
            low = self.chances[2 * step + head]
            chance = low.astype(jnp.float32)
            mine = self.half(grads, head)
            chance_grad = contract(mine, value_block, 1, 1)
            moved = chance_grad - jnp.sum(chance * chance_grad, -1, keepdims=True)
            score_grad = (chance * moved).astype(jnp.bfloat16)
            value_grad += contract(low, mine, 0, 0)
            query_grad += jnp.dot(
                score_grad, self.half(key_block, head), preferred_element_type=jnp.float32
            )
            key_grad += contract(score_grad, self.half(queries, head), 0, 0)
        for part, grad in enumerate((query_grad * 0.125, key_grad, value_grad)):
            offset = pl.multiple_of(part * self.width + pair * PAIR, PAIR)
            self.packed[rows, pl.ds(offset, PAIR)] = grad.astype(jnp.bfloat16)

    def in_weight_grad(self, tile):
        here = columns(tile)
        grads = self.packed[:, here]
        self.keep_columns(self.in_grad, here, contract(flat(self.sequence[...]), grads, 0, 0))
        self.in_terms[:, here] = jnp.sum(grads.astype(jnp.float32), 0, keepdims=True)

    def input_backward(self, tile):
        here = columns(tile)
        weight = take_rows(self.weight_in, tile * TILE, (tile + 1) * TILE)
        grad = self.upper[:, here] + contract(self.packed[...], weight, 1, 1)
        shape = self.input_grad.shape[:3] + (TILE,)
        self.input_grad[:, :, :, here] = grad.astype(jnp.bfloat16).reshape(shape)

    def keep_columns(self, ref, here, grad):
        ref[:, :, :, :, here] = grad.astype(jnp.bfloat16).reshape(ref.shape[:4] + (TILE,))

    def gather_terms(self):
        for place, width in enumerate(WIDTHS):
            if place == BIAS_IN:
                row = jnp.concatenate(
                    [self.in_terms[:, : self.width], self.in_terms[:, 2 * self.width :]], -1
                )
            elif place == BIAS_UP:
                row = self.up_terms[...]
            else:
                row = self.terms[place : place + 1, :]
            high = row.astype(jnp.bfloat16)
            rest = row - high.astype(jnp.float32)
            middle = rest.astype(jnp.bfloat16)
            low = (rest - middle.astype(jnp.float32)).astype(jnp.bfloat16)
            keep, spots = owners(width), places(width)
            self.small_grad[:, place, :] = sum(
                contract(jnp.where(keep, part.astype(jnp.float32), 0.0).astype(jnp.bfloat16), spots, 1, 1)
                for part in (high, middle, low)
            )


def scratch_of(rows, width, hidden_width):
    low, full = jnp.bfloat16, jnp.float32
    return dict(
        bias_row=pltpu.VMEM((1, 3 * width), full),
        up_row=pltpu.VMEM((1, hidden_width), full),
        vectors=pltpu.VMEM((8, width), full),
        terms=pltpu.VMEM((8, width), full),
        up_terms=pltpu.VMEM((1, hidden_width), full),
        in_terms=pltpu.VMEM((1, 3 * width), full),
        packed=pltpu.VMEM((rows, 3 * width), low),
        chances=pltpu.VMEM((2 * rows // TILE * width // PAIR, TILE, TILE), low),
        context=pltpu.VMEM((rows, width), low),
        normed=pltpu.VMEM((rows, width), full),
        factor=pltpu.VMEM((rows, 1), full),
        hidden_low=pltpu.VMEM((rows, width), low),
        active=pltpu.VMEM((rows, hidden_width), low),
        slope=pltpu.VMEM((rows, hidden_width), low),
        upper=pltpu.VMEM((rows, width), full),
        feed_grad=pltpu.VMEM((rows, width), low),
    )


class Spot:
    def __init__(self):
        self.me = me = lax.axis_index("dp")
        core, column, row = me % 2, (me // 2) % 2, (me // 4) % 2
        self.layer, self.seat = me // 8, me % 8
        self.to_sibling = 1 - 2 * core
        across_row = 4 * (1 - 2 * row)
        across_column = 2 * (1 - 2 * column)
        self.to_second = (1 - core) * across_row + core * across_column
        self.to_third = (1 - core) * across_column + core * across_row
        self.sibling = me + self.to_sibling
        self.second = me + self.to_second
        self.third = me + self.to_third
        self.above = [lax.rem(self.layer + step, LAYERS) for step in (1, 2, 3)]


class Chunk:
    def __init__(self, kind, groups, cols):
        self.kind, self.groups, self.cols = kind, groups, cols

    def line(self, refs, seat):
        return refs[self.kind].at[:, seat, self.groups, :, self.cols]

    def block(self, refs, layer, seat):
        return refs[self.kind].at[layer, seat, self.groups, :, self.cols]

    def bulk(self, refs, layers, lines):
        return refs[self.kind].at[pl.ds(0, layers), pl.ds(0, lines), self.groups, :, self.cols]


def chunks_of(shapes):
    made = []
    for kind, (groups, _, width) in enumerate(shapes):
        if kind < 3:
            size = shapes[1][2]
            for start in range(0, width, size):
                made.append(Chunk(kind, pl.ds(0, groups), pl.ds(start, size)))
        else:
            size = shapes[0][0]
            for start in range(0, groups, size):
                made.append(Chunk(kind, pl.ds(start, size), pl.ds(0, width)))
    return made


class Traffic:
    def __init__(self, spot, refs):
        self.spot = spot
        self.__dict__.update(refs)
        self.chunks = chunks_of([tuple(shard.shape) for shard in self.shards])


    def own(self, k):
        chunk, spot = self.chunks[k], self.spot
        source = self.shards[chunk.kind].at[chunk.groups, :, chunk.cols]
        target = chunk.block(self.full, spot.layer, spot.seat)
        for layer in spot.above:
            remote(
                source, target, self.sent.at[k], self.along_in.at[k], layer * ROWS + spot.seat
            ).start()
        remote(source, target, self.sent.at[k], self.second_own.at[k], spot.second).start()
        remote(source, target, self.sent.at[k], self.third_own.at[k], spot.third).start()

    def line_out(self, k, seat, device, sem):
        line = self.chunks[k].line(self.full, seat)
        remote(line, line, self.sent.at[k], sem, device).start()

    def wait_lines(self, k, sem, count=1):
        chunk = self.chunks[k]
        layers = {0: 1, 3: 3}.get(count, LAYERS)
        here = chunk.bulk(self.full, layers, count if layers == LAYERS else 1)
        return remote(here, here, self.sent.at[k], sem, self.spot.me)

    def from_line(self, k):
        spot = self.spot
        self.wait_lines(k, self.along_in.at[k], 3).wait_recv()
        for layer in spot.above:
            block = self.chunks[k].block(self.full, layer, spot.seat)
            sent = self.sent.at[k]
            remote(block, block, sent, self.second_in.at[k], spot.second).start()
            remote(block, block, sent, self.third_in.at[k, 0], spot.third).start()
        self.line_out(k, spot.seat, spot.sibling, self.sibling_in.at[k])

    def from_second(self, k):
        spot = self.spot
        self.wait_lines(k, self.second_own.at[k], 0).wait_recv()
        self.wait_lines(k, self.second_in.at[k], 3).wait_recv()
        seat = spot.seat + spot.to_second
        self.line_out(k, seat, spot.third, self.third_in.at[k, 1])
        self.line_out(k, seat, spot.sibling, self.sibling_in.at[k])

    def from_third(self, k, which):
        spot = self.spot
        if which == 0:
            self.wait_lines(k, self.third_own.at[k], 0).wait_recv()
        self.wait_lines(k, self.third_in.at[k, which], 1 if which else 3).wait_recv()
        seat = spot.seat + spot.to_third + which * spot.to_second
        self.line_out(k, seat, spot.sibling, self.sibling_in.at[k])

    def complete(self, k):
        self.wait_lines(k, self.sibling_in.at[k], 4).wait_recv()

    def own_sent(self, k):
        self.wait_lines(k, self.sent.at[k], 7).wait_send()
        self.wait_lines(k, self.sent.at[k], 3).wait_send()


    def exchange(self, source, target, which, first=0, last=COUNT - 1):
        me = self.spot.me

        def go(step, carry):
            device = lax.rem(me + lax.rem(step * 5, COUNT), COUNT)
            remote(
                source.at[:, device],
                target.at[:, me],
                self.given.at[which],
                self.taken.at[which],
                device,
            ).start()
            return carry

        lax.fori_loop(1 + first, 1 + last, go, 0)

    def exchanged(self, target, which):
        here = target.at[:, pl.ds(0, COUNT - 1)]
        return remote(
            here,
            here,
            self.given.at[which],
            self.taken.at[which],
            self.spot.me,
        )

    def exchange_small(self, source, target, which):
        me = self.spot.me

        def go(step, carry):
            device = lax.rem(me + step, COUNT)
            remote(
                source if which == 4 else source.at[device],
                target.at[me],
                self.given.at[which],
                self.taken.at[which],
                device,
            ).start()
            return carry

        lax.fori_loop(1, COUNT, go, 0)

    def exchanged_small(self, target, which):
        here = target.at[pl.ds(0, COUNT - 1)]
        return remote(here, here, self.given.at[which], self.taken.at[which], self.spot.me)


    def move(self, k, seat, landing, device, sem):
        remote(
            self.chunks[k].line(self.partial, seat), landing, self.shed.at[k], sem, device
        ).start()

    def landing(self, k, landings, slot):
        chunk = self.chunks[k]
        return landings[chunk.kind].at[slot, :, chunk.groups, :, chunk.cols]

    def landed(self, k, landings, sem):
        chunk = self.chunks[k]
        here = landings[chunk.kind].at[:, :, chunk.groups, :, chunk.cols]
        remote(here, here, self.shed.at[k], sem, self.spot.me).wait_recv()

    def take_in(self, k, seat, landings, slot):
        chunk = self.chunks[k]
        line, here = chunk.line(self.partial, seat), self.landing(k, landings, slot)
        line[...] = line[...] + here[...]

    def begin(self, k):
        spot = self.spot
        for slot in range(4):
            seat = 2 * slot + (spot.seat + 1) % 2
            self.move(
                k, seat, self.landing(k, self.land_first, slot), spot.sibling, self.first_in.at[k]
            )

    def to_third(self, k):
        spot = self.spot
        self.landed(k, self.land_first, self.first_in.at[k])
        for slot in range(4):
            self.take_in(k, 2 * slot + spot.seat % 2, self.land_first, slot)
        for slot in range(2):
            seat = spot.seat + spot.to_third + slot * spot.to_second
            self.move(
                k, seat, self.landing(k, self.land_third, slot), spot.third, self.across_in.at[k]
            )

    def to_second(self, k):
        spot = self.spot
        self.landed(k, self.land_third, self.across_in.at[k])
        for slot in range(2):
            self.take_in(k, spot.seat + slot * spot.to_second, self.land_third, slot)
        seat = spot.seat + spot.to_second
        self.move(k, seat, self.landing(k, self.land_second, 0), spot.second, self.over_in.at[k])

    def to_owner(self, k):
        chunk, spot = self.chunks[k], self.spot
        self.landed(k, self.land_second, self.over_in.at[k])
        self.take_in(k, spot.seat, self.land_second, 0)
        target = self.sums[chunk.kind].at[spot.layer, chunk.groups, :, chunk.cols]
        for layer in spot.above:
            remote(
                chunk.block(self.partial, layer, spot.seat),
                target,
                self.shed.at[k],
                self.owner_in.at[k],
                layer * ROWS + spot.seat,
            ).start()
        self.keep(k).start()

    def keep(self, k):
        chunk, spot = self.chunks[k], self.spot
        return pltpu.make_async_copy(
            chunk.block(self.partial, spot.layer, spot.seat),
            self.sums[chunk.kind].at[spot.layer, chunk.groups, :, chunk.cols],
            self.kept.at[k],
        )

    def settle(self, k):
        chunk = self.chunks[k]
        here = self.sums[chunk.kind].at[pl.ds(0, 3), chunk.groups, :, chunk.cols]
        remote(here, here, self.shed.at[k], self.owner_in.at[k], self.spot.me).wait_recv()
        self.keep(k).wait()
        for count in (7, 3):
            there = chunk.bulk(self.partial, 3 if count == 3 else LAYERS, 1 if count == 3 else count)
            remote(there, there, self.shed.at[k], self.owner_in.at[k], self.spot.me).wait_send()


def interleave(count, body, steps=()):
    assert len(steps) <= count

    def one(index, carry):
        body(index)
        for place, thunks in enumerate(steps):
            if thunks:

                @pl.when(index == place)
                def _():
                    for thunk in thunks:
                        thunk()

        return carry

    lax.fori_loop(0, count, one, 0)


def unroll(count, body, steps):
    for index in range(count):
        body(index)
        for thunk in steps[index]:
            thunk()


def spread(thunks, slots):
    return [
        thunks[len(thunks) * place // slots : len(thunks) * (place + 1) // slots]
        for place in range(slots)
    ]


PACES = 3, 3, 2, 1, 1, 1, 5, 3, 1
LEAD, TOKENS_EACH, COTANGENT_FROM, COTANGENT_EACH = 1, 6, 4, 4


def step_kernel(trees, *given):
    given, named = list(given), {}
    for tree in trees:
        named.update(jax.tree.unflatten(tree, given[: tree.num_leaves]))
        given = given[tree.num_leaves :]
    refs = types.SimpleNamespace(**named)
    spot = Spot()
    me = spot.me
    traffic = Traffic(spot, named)
    chunks = range(len(traffic.chunks))
    tokens, cotangent = refs.tokens, refs.cotangent
    sequence, upstream = refs.sequence, refs.upstream
    first_spare, second_spare = refs.first_spare, refs.second_spare

    locals_ = [
        pltpu.make_async_copy(
            traffic.shards[kind], traffic.full[kind].at[spot.layer, spot.seat], traffic.local.at[kind]
        )
        for kind in range(4)
    ] + [
        pltpu.make_async_copy(cotangent.at[:, me], upstream.at[:, me], traffic.local.at[5]),
        pltpu.make_async_copy(refs.small_own, refs.small.at[me], traffic.local.at[6]),
    ]
    early = [
        pltpu.make_async_copy(tokens, first_spare, traffic.local.at[4]),
        pltpu.make_async_copy(refs.lengths, refs.lengths_here, traffic.local.at[7]),
        pltpu.make_async_copy(refs.order, refs.order_here, traffic.local.at[8]),
    ]
    for copy in early + locals_:
        copy.start()
    for copy in early:
        copy.wait()
    for batch in range(2):
        for seat in range(COUNT):
            second_spare[batch, seat] = first_spare[batch, refs.order_here[batch, seat]]
    own_sequence = pltpu.make_async_copy(
        second_spare.at[:, me], sequence.at[:, me], traffic.local.at[4]
    )
    own_sequence.start()
    meet_all(me)

    def piece_of(source, target, which, first, last):
        return lambda: traffic.exchange(source, target, which, first, last)

    def do(method, *args):
        return lambda: method(*args)

    layer = Layer(named)
    layer.context_grad, layer.preact_grad = refs.hidden_low, refs.active
    layer.result, layer.input_grad = first_spare, second_spare
    layer.weight_in, layer.weight_mix, layer.weight_up, layer.weight_down = refs.full
    layer.in_grad, layer.mix_grad, layer.up_grad, layer.down_grad = refs.partial
    layer.lengths = [
        refs.lengths_here[batch, refs.order_here[batch, me]] for batch in range(2)
    ]
    tiles, wide = layer.width // TILE, layer.hidden_width // TILE
    pairs = 2 * (layer.width // PAIR)
    ins = 3
    ups = wide // tiles
    assert len(chunks) == ins + 1 + 2 * ups

    ticks = []
    for tick in range(-LEAD, len(chunks) + 2):
        here = []
        if 0 <= tick + LEAD < len(chunks):
            here.append(do(traffic.own, tick + LEAD))
        first = (tick + LEAD) * TOKENS_EACH
        if first < COUNT - 1:
            last = min(first + TOKENS_EACH, COUNT - 1)
            here.append(piece_of(second_spare, sequence, 0, first, last))
        if tick == -LEAD:
            here.append(do(traffic.exchange_small, refs.small_own, refs.small, 4))
        if 0 <= tick < len(chunks):
            here.append(do(traffic.from_line, tick))
        if 0 <= tick - 1 < len(chunks):
            here.append(do(traffic.from_second, tick - 1))
            here.append(do(traffic.from_third, tick - 1, 0))
        if 0 <= tick - 2 < len(chunks):
            here.append(do(traffic.from_third, tick - 2, 1))
        first = (tick - COTANGENT_FROM) * COTANGENT_EACH
        if 0 <= first < COUNT - 1:
            last = min(first + COTANGENT_EACH, COUNT - 1)
            here.append(piece_of(cotangent, upstream, 1, first, last))
        ticks.append(here)
    flat = lambda first, last: [thunk for here in ticks[first + LEAD : last + LEAD] for thunk in here]

    for thunk in flat(-LEAD, 0):
        thunk()
    for copy in locals_:
        copy.wait()
    layer.terms[...] = jnp.zeros_like(layer.terms)
    for thunk in flat(0, 2):
        thunk()
    traffic.exchanged_small(refs.small, 4).wait_recv()
    layer.spread_small()
    for thunk in flat(2, ins + 2):
        thunk()
    dealt = traffic.exchanged(sequence, 0)
    dealt.wait_recv()
    own_sequence.wait()
    for k in range(ins):
        traffic.complete(k)
    interleave(3 * tiles, layer.project, spread(flat(ins + 2, ins + 3), 3 * tiles))
    interleave(pairs, layer.attend, spread(flat(ins + 3, ins + 6), pairs))
    traffic.complete(ins)
    interleave(layer.rows // TILE, layer.mix)
    for thunk in flat(ins + 6, ins + ups + 3):
        thunk()
    for k in range(ins + 1, ins + 1 + ups):
        traffic.complete(k)
    interleave(wide, layer.up, spread(flat(ins + ups + 3, len(chunks) + 2), wide))
    for k in range(ins + 1 + ups, len(chunks)):
        traffic.complete(k)
    interleave(tiles, layer.down)
    cotangents = traffic.exchanged(upstream, 1)
    cotangents.wait_recv()
    interleave(layer.rows // 128, layer.finish)

    keep_result = pltpu.make_async_copy(
        first_spare.at[:, me], refs.returned.at[:, me], traffic.local.at[0]
    )
    keep_result.start()
    pieces = [
        piece_of(first_spare, refs.returned, 2, first, min(first + 4, COUNT - 1))
        for first in range(0, COUNT - 1, 4)
    ]
    interleave(LAYERS, layer.down_weight_grad, spread(pieces, LAYERS))

    queue = list(range(ins + 1 + ups, len(chunks))) + list(range(ins + 1, ins + 1 + ups))
    queue += [ins] + list(range(ins))
    walk = []
    for tick in range(len(queue) + 2):
        for late, stage in enumerate((traffic.to_third, traffic.to_second, traffic.to_owner)):
            if 0 <= tick - late < len(queue):
                walk.append(do(stage, queue[tick - late]))

    def next_steps(count):
        taken, walk[:] = walk[:count], walk[count:]
        return taken

    def with_begin(steps, count, every, kinds):
        made = [list(step) for step in steps] + [[] for _ in range(count - len(steps))]
        for place, k in enumerate(kinds):
            made[(place + 1) * every - 1].insert(0, do(traffic.begin, k))
        return made

    for k in queue[:ups]:
        traffic.begin(k)
    paces = iter(PACES)
    interleave(LAYERS, layer.active_backward, spread(next_steps(next(paces)), LAYERS))
    interleave(
        wide,
        layer.up_weight_grad,
        with_begin(
            [[]] * tiles + spread(next_steps(next(paces)), wide - tiles),
            wide,
            tiles,
            queue[ups : 2 * ups],
        ),
    )
    unroll(tiles, layer.hidden_backward, spread(next_steps(next(paces)), tiles))
    interleave(layer.rows // 128, layer.first_backward, spread(next_steps(next(paces)), 1))
    interleave(
        tiles,
        layer.mix_weight_grad,
        with_begin(
            spread(next_steps(next(paces)), tiles), tiles, tiles, queue[2 * ups : 2 * ups + 1]
        ),
    )
    unroll(tiles, layer.mix_backward, spread(next_steps(next(paces)), tiles))
    interleave(pairs, layer.attend_backward, spread(next_steps(next(paces)), pairs))
    interleave(
        3 * tiles,
        layer.in_weight_grad,
        with_begin(
            spread(next_steps(next(paces)), 3 * tiles), 3 * tiles, tiles, queue[2 * ups + 1 :]
        ),
    )
    dealt.wait_send()
    unroll(tiles, layer.input_backward, spread(next_steps(next(paces)), tiles))
    keep_grad = pltpu.make_async_copy(
        second_spare.at[:, me], refs.tokens_grad.at[:, me], traffic.local.at[2]
    )
    keep_grad.start()
    left = next_steps(len(walk))

    def small_out():
        layer.gather_terms()
        traffic.exchange_small(refs.small_grad, refs.small_sums, 5)
        keep_small.start()

    keep_small = pltpu.make_async_copy(
        refs.small_grad.at[me], refs.small_sums.at[me], traffic.local.at[1]
    )
    left.insert(2, small_out)
    cuts = list(range(0, COUNT - 1, 4))
    for place in range(max(len(left), len(cuts))):
        if place < len(cuts):
            piece_of(
                second_spare, refs.tokens_grad, 3, cuts[place], min(cuts[place] + 4, COUNT - 1)
            )()
        if place < len(left):
            left[place]()
    for k in queue:
        traffic.settle(k)
        traffic.own_sent(k)
    cotangents.wait_send()
    for target, which in ((refs.returned, 2), (refs.tokens_grad, 3)):
        copy = traffic.exchanged(target, which)
        copy.wait_recv()
        copy.wait_send()
    traffic.exchanged_small(refs.small, 4).wait_send()
    small = traffic.exchanged_small(refs.small_sums, 5)
    small.wait_recv()
    small.wait_send()
    for copy in (keep_result, keep_small, keep_grad):
        copy.wait()


def encoder_step(lengths, order, tokens, cotangent, shards, small_own):
    low, full = jnp.bfloat16, jnp.float32
    width, hidden_width = tokens.shape[-1], shards[2].shape[-1]
    rows = tokens.shape[0] * COUNT * tokens.shape[2]
    anywhere = pl.BlockSpec(memory_space=pl.ANY)
    inputs = dict(
        lengths=lengths,
        order=order,
        tokens=tokens,
        cotangent=cotangent,
        shards=shards,
        small_own=small_own,
    )
    shapes = [shard.shape for shard in shards]
    smalls = ((COUNT,) + small_own.shape, full)
    outputs = dict(
        returned=jax.ShapeDtypeStruct(tokens.shape, low),
        tokens_grad=jax.ShapeDtypeStruct(tokens.shape, low),
        sums=[jax.ShapeDtypeStruct((LAYERS,) + shape, low) for shape in shapes],
        small_sums=jax.ShapeDtypeStruct(*smalls),
    )
    sequences = pltpu.VMEM(tokens.shape, low)
    scratch = dict(
        full=[pltpu.VMEM((LAYERS, ROWS) + shape, low) for shape in shapes],
        partial=[pltpu.VMEM((LAYERS, ROWS) + shape, low) for shape in shapes],
        land_first=[pltpu.VMEM((4, LAYERS) + shape, low) for shape in shapes],
        land_third=[pltpu.VMEM((2, LAYERS) + shape, low) for shape in shapes],
        land_second=[pltpu.VMEM((1, LAYERS) + shape, low) for shape in shapes],
        sequence=sequences,
        upstream=sequences,
        first_spare=sequences,
        second_spare=sequences,
        lengths_here=pltpu.SMEM(lengths.shape, lengths.dtype),
        order_here=pltpu.SMEM(order.shape, order.dtype),
        small=pltpu.VMEM(*smalls),
        small_grad=pltpu.VMEM(*smalls),
        **scratch_of(rows, width, hidden_width),
    )
    count = len(chunks_of(shapes))
    each = pltpu.SemaphoreType.DMA((count,))
    sems = dict(
        local=pltpu.SemaphoreType.DMA((9,)),
        given=pltpu.SemaphoreType.DMA((6,)),
        taken=pltpu.SemaphoreType.DMA((6,)),
        third_in=pltpu.SemaphoreType.DMA((count, 2)),
        sent=each,
        along_in=each,
        second_in=each,
        second_own=each,
        third_own=each,
        sibling_in=each,
        shed=each,
        first_in=each,
        across_in=each,
        over_in=each,
        owner_in=each,
        kept=each,
    )
    given, given_tree = jax.tree.flatten(inputs)
    made, made_tree = jax.tree.flatten(outputs)
    held, held_tree = jax.tree.flatten({**scratch, **sems})
    results = pl.pallas_call(
        functools.partial(step_kernel, (given_tree, made_tree, held_tree)),
        out_shape=made,
        in_specs=[anywhere] * len(given),
        out_specs=[anywhere] * len(made),
        scratch_shapes=held,
        compiler_params=pltpu.CompilerParams(
            collective_id=0, has_side_effects=True, vmem_limit_bytes=VMEM_LIMIT
        ),
        name="encoder_step",
    )(*given)
    results = jax.tree.unflatten(made_tree, results)
    return types.SimpleNamespace(**results)


VMEM_LIMIT = 63 << 20


def finish_kernel(order, *refs):
    sources, refs = refs[:7], refs[7:]
    layer_out, tokens_grad, refs = refs[0], refs[1], refs[2:]
    totals, outs, inner, sems = refs[:4], refs[4:12], refs[12:19], refs[19]
    copies = [
        pltpu.make_async_copy(source, target, sems.at[place])
        for place, (source, target) in enumerate(zip(sources, (layer_out, *inner[1:])))
    ]
    for copy in copies:
        copy.start()
    copies[1].wait()
    for batch in range(2):
        for slot in range(COUNT):
            tokens_grad[batch, order[batch, slot]] = inner[1][batch, slot]
    for total, parts, copy in zip(totals, inner[2:6], copies[2:6]):
        copy.wait()
        total[...] = sum(parts[layer].astype(jnp.float32) for layer in range(LAYERS))
    copies[0].wait()
    copies[6].wait()
    small = jnp.sum(inner[6][...], 0)
    for place, out in enumerate(outs):
        out[...] = small[place : place + 1, : out.shape[1]]


def finish_step(order, returned, tokens_grad, sums, small_sums):
    inside = pl.BlockSpec(memory_space=pltpu.VMEM)
    parts = [returned, tokens_grad, *sums, small_sums]
    return pl.pallas_call(
        finish_kernel,
        out_shape=[jax.ShapeDtypeStruct(returned.shape, returned.dtype)] * 2
        + [jax.ShapeDtypeStruct(part.shape[1:], jnp.float32) for part in sums]
        + [jax.ShapeDtypeStruct((1, width), jnp.float32) for width in WIDTHS],
        in_specs=[pl.BlockSpec(memory_space=pltpu.SMEM)]
        + [pl.BlockSpec(memory_space=pltpu.HBM)] * 7,
        out_specs=[inside] * 14,
        scratch_shapes=[pltpu.VMEM(part.shape, part.dtype) for part in parts]
        + [pltpu.SemaphoreType.DMA((7,))],
        compiler_params=pltpu.CompilerParams(vmem_limit_bytes=VMEM_LIMIT),
        name="finish_step",
    )(order, *parts)


SMALL = (1, 3, 4, 5, 7, 9, 10, 11)
LARGE = (0, 2, 6, 8)


def local(tokens, lengths, order, *rest):
    shards, cotangent = rest[:12], rest[12]
    if lax.axis_size("dp") != COUNT or tokens.shape[2] % 8:
        return portable(tokens, lengths, order, *rest)
    small = sum(
        lax.pad(
            shards[i].astype(jnp.float32)[None],
            jnp.float32(0),
            ((place, len(SMALL) - 1 - place, 0), (0, 128 - shards[i].shape[0], 0)),
        )
        for place, i in enumerate(SMALL)
    )
    made = encoder_step(
        lengths,
        order,
        tokens,
        cotangent,
        [shards[i].reshape(-1, 8, shards[i].shape[-1]) for i in LARGE],
        small,
    )
    layer_out, tokens_grad, *rest = finish_step(
        order, made.returned, made.tokens_grad, made.sums, made.small_sums
    )
    outputs = [None] * 12
    for i, total in zip(LARGE, rest[:4]):
        outputs[i] = total.reshape(-1, total.shape[-1])
    for i, total in zip(SMALL, rest[4:]):
        outputs[i] = total.reshape(-1)
    return (layer_out, tokens_grad, *outputs)


def solution(mesh):
    return jax.shard_map(
        local,
        mesh=mesh,
        in_specs=(
            P(None, None, "dp", None),
            P(),
            P(),
            P("dp", None),
            P("dp"),
            P("dp", None),
            P("dp"),
            P("dp"),
            P("dp"),
            P("dp", None),
            P("dp"),
            P("dp", None),
            P("dp"),
            P("dp"),
            P("dp"),
            P(None, None, "dp", None),
        ),
        out_specs=(
            P(None, None, "dp", None),
            P(None, None, "dp", None),
            P("dp", None),
            P("dp"),
            P("dp", None),
            P("dp"),
            P("dp"),
            P("dp"),
            P("dp", None),
            P("dp"),
            P("dp", None),
            P("dp"),
            P("dp"),
            P("dp"),
        ),
        check_vma=False,
    )
```

```python
import functools
import types

import jax
import jax.numpy as jnp
from jax import lax
from jax.experimental import pallas as pl
from jax.experimental.pallas import tpu as pltpu
from jax.sharding import PartitionSpec as P

MESH = pl.DeviceIdType.MESH

HD = 64


epsilon = 1e-12


def matmul(left, right):
    return jnp.dot(left, right, preferred_element_type=jnp.float32)


def rows_product(left, right):
    return lax.dot_general(
        left, right, (((0,), (0,)), ((), ())), preferred_element_type=jnp.float32
    )


def right_transposed(left, right):
    return lax.dot_general(
        left, right, (((1,), (1,)), ((), ())), preferred_element_type=jnp.float32
    )


def split_heads(block, heads):
    return block.reshape(block.shape[0], heads, -1).transpose(1, 0, 2)


def join_heads(block):
    return block.transpose(1, 0, 2).reshape(block.shape[1], -1)


def norm_forward(summed, norm_gain, norm_shift):
    row_mean = jnp.mean(summed, -1, keepdims=True)
    centered = summed - row_mean
    reciprocal = lax.rsqrt(jnp.mean(centered * centered, -1, keepdims=True) + epsilon)
    normed = centered * reciprocal
    return (normed * norm_gain + norm_shift, normed, reciprocal)


def norm_backward(upstream, normed, reciprocal, norm_gain):
    scaled = upstream * norm_gain
    summed_grad = reciprocal * (
        scaled
        - jnp.mean(scaled, -1, keepdims=True)
        - normed * jnp.mean(scaled * normed, -1, keepdims=True)
    )
    return (summed_grad, jnp.sum(upstream * normed, 0), jnp.sum(upstream, 0))


def head_scores(head_query, head_keys, valid):
    scores = right_transposed(head_query, head_keys) * 0.125
    return jnp.where(valid[None, :], scores, -1e30)


def attend_forward(packed, valid):
    head_query, head_keys, head_values = packed
    scores = head_scores(head_query, head_keys, valid)
    row_max = jnp.max(scores, -1, keepdims=True)
    weights_raw = jnp.exp(scores - row_max)
    row_sum = jnp.sum(weights_raw, -1, keepdims=True)
    probability = weights_raw / row_sum
    context = matmul(probability.astype(jnp.bfloat16), head_values)
    return (context, (row_max + jnp.log(row_sum))[:, 0])


def attend_backward(packed, valid):
    head_query, head_keys, head_values, context_grad, log_total = packed
    scores = head_scores(head_query, head_keys, valid)
    probability = jnp.exp(scores - log_total[:, None])
    low_prob = probability.astype(jnp.bfloat16)
    prob_grad = right_transposed(context_grad, head_values)
    value_grad = rows_product(low_prob, context_grad)
    shifted = prob_grad - jnp.sum(probability * prob_grad, -1, keepdims=True)
    score_grad = (probability * shifted).astype(jnp.bfloat16)
    query_grad = matmul(score_grad, head_keys) * 0.125
    key_grad = rows_product(score_grad, head_query) * 0.125
    return (query_grad, key_grad, value_grad)


def forward(weights, sequence, length):
    (
        weight_in,
        bias_in,
        weight_mix,
        bias_mix,
        gain_first,
        shift_first,
        weight_up,
        bias_up,
        weight_down,
        bias_down,
        gain_second,
        shift_second,
    ) = weights
    width = sequence.shape[1]
    heads = width // HD
    valid = jnp.arange(sequence.shape[0], dtype=jnp.int32) < length
    bias_full = jnp.concatenate(
        [
            bias_in[:width].astype(jnp.float32),
            jnp.zeros((width,), jnp.float32),
            bias_in[width:].astype(jnp.float32),
        ]
    )
    projected = (matmul(sequence, weight_in) + bias_full).astype(jnp.bfloat16)
    queries = split_heads(projected[:, :width], heads)
    key_heads = split_heads(projected[:, width : 2 * width], heads)
    value_heads = split_heads(projected[:, 2 * width :], heads)
    context, log_total = lax.map(
        lambda packed: attend_forward(packed, valid), (queries, key_heads, value_heads)
    )
    context_low = join_heads(context).astype(jnp.bfloat16)
    branch = matmul(context_low, weight_mix) + bias_mix.astype(jnp.float32)
    hidden, normed_first, recip_first = norm_forward(
        sequence.astype(jnp.float32) + branch,
        gain_first.astype(jnp.float32),
        shift_first.astype(jnp.float32),
    )
    hidden_low = hidden.astype(jnp.bfloat16)
    preact = matmul(hidden_low, weight_up) + bias_up.astype(jnp.float32)
    activated = jax.nn.gelu(preact, approximate=False).astype(jnp.bfloat16)
    feed_out = matmul(activated, weight_down) + bias_down.astype(jnp.float32)
    result, normed_second, recip_second = norm_forward(
        hidden + feed_out, gain_second.astype(jnp.float32), shift_second.astype(jnp.float32)
    )
    stored = (
        valid,
        queries,
        key_heads,
        value_heads,
        log_total,
        context_low,
        normed_first,
        recip_first,
        hidden_low,
        preact,
        activated,
        normed_second,
        recip_second,
    )
    return (result.astype(jnp.bfloat16), stored)


def backward(weights, sequence, upstream_low, stored):
    (
        weight_in,
        bias_in,
        weight_mix,
        bias_mix,
        gain_first,
        shift_first,
        weight_up,
        bias_up,
        weight_down,
        bias_down,
        gain_second,
        shift_second,
    ) = weights
    (
        valid,
        queries,
        key_heads,
        value_heads,
        log_total,
        context_low,
        normed_first,
        recip_first,
        hidden_low,
        preact,
        activated,
        normed_second,
        recip_second,
    ) = stored
    width = sequence.shape[1]
    heads = width // HD
    upstream = upstream_low.astype(jnp.float32)
    second_grad, gain_second_grad, shift_second_grad = norm_backward(
        upstream, normed_second, recip_second, gain_second.astype(jnp.float32)
    )
    feed_grad = second_grad.astype(jnp.bfloat16)
    bias_down_grad = jnp.sum(feed_grad.astype(jnp.float32), 0)
    weight_down_grad = rows_product(activated, feed_grad)
    act_grad = right_transposed(feed_grad, weight_down)
    slope = (
        0.5 * (1.0 + jax.scipy.special.erf(preact * 0.7071067811865476))
        + preact * jnp.exp(-0.5 * preact * preact) * 0.3989422804014327
    )
    preact_grad = (act_grad * slope).astype(jnp.bfloat16)
    bias_up_grad = jnp.sum(preact_grad.astype(jnp.float32), 0)
    weight_up_grad = rows_product(hidden_low, preact_grad)
    hidden_grad = second_grad + right_transposed(preact_grad, weight_up)
    first_grad, gain_first_grad, shift_first_grad = norm_backward(
        hidden_grad, normed_first, recip_first, gain_first.astype(jnp.float32)
    )
    branch_grad = first_grad.astype(jnp.bfloat16)
    bias_mix_grad = jnp.sum(branch_grad.astype(jnp.float32), 0)
    weight_mix_grad = rows_product(context_low, branch_grad)
    context_grad = right_transposed(branch_grad, weight_mix).astype(jnp.bfloat16)
    query_grad, key_grad, value_grad = lax.map(
        lambda packed: attend_backward(packed, valid),
        (queries, key_heads, value_heads, split_heads(context_grad, heads), log_total),
    )
    projected_grad = jnp.concatenate(
        [join_heads(query_grad), join_heads(key_grad), join_heads(value_grad)], -1
    ).astype(jnp.bfloat16)
    column_sums = jnp.sum(projected_grad.astype(jnp.float32), 0)
    bias_in_grad = jnp.concatenate([column_sums[:width], column_sums[2 * width :]])
    weight_in_grad = rows_product(sequence, projected_grad)
    input_grad = (first_grad + right_transposed(projected_grad, weight_in)).astype(jnp.bfloat16)
    gradients = (
        weight_in_grad,
        bias_in_grad,
        weight_mix_grad,
        bias_mix_grad,
        gain_first_grad,
        shift_first_grad,
        weight_up_grad,
        bias_up_grad,
        weight_down_grad,
        bias_down_grad,
        gain_second_grad,
        shift_second_grad,
    )
    return (input_grad, gradients)


def permuted(blocks, picks):
    chosen = (picks[:, None] == jnp.arange(picks.shape[0])[None, :]).astype(blocks.dtype)
    flat = blocks.reshape(blocks.shape[0], -1)
    return matmul(chosen, flat).astype(blocks.dtype).reshape(blocks.shape)


def inverse_of(picks):
    slots = jnp.arange(picks.shape[0], dtype=jnp.int32)
    return jnp.sum(jnp.where(picks[:, None] == slots[None, :], slots[:, None], 0), 0)


def fetch_weights(shards):
    return (
        lax.all_gather(shards[0], "dp", axis=0, tiled=True),
        lax.all_gather(shards[1], "dp", axis=0, tiled=True),
        lax.all_gather(shards[2], "dp", axis=0, tiled=True),
        lax.all_gather(shards[3], "dp", axis=0, tiled=True),
        lax.all_gather(shards[4], "dp", axis=0, tiled=True),
        lax.all_gather(shards[5], "dp", axis=0, tiled=True),
        lax.all_gather(shards[6], "dp", axis=0, tiled=True),
        lax.all_gather(shards[7], "dp", axis=0, tiled=True),
        lax.all_gather(shards[8], "dp", axis=0, tiled=True),
        lax.all_gather(shards[9], "dp", axis=0, tiled=True),
        lax.all_gather(shards[10], "dp", axis=0, tiled=True),
        lax.all_gather(shards[11], "dp", axis=0, tiled=True),
    )


def add_trees(first, second):
    if first is None:
        return second
    return jax.tree.map(lambda left, right: left + right, first, second)


def portable(
    tokens,
    lengths,
    order,
    weight_in,
    bias_in,
    weight_mix,
    bias_mix,
    gain_first,
    shift_first,
    weight_up,
    bias_up,
    weight_down,
    bias_down,
    gain_second,
    shift_second,
    cotangent,
):
    shards = (
        weight_in,
        bias_in,
        weight_mix,
        bias_mix,
        gain_first,
        shift_first,
        weight_up,
        bias_up,
        weight_down,
        bias_down,
        gain_second,
        shift_second,
    )
    device = lax.axis_index("dp")
    totals = None
    outputs_list = []
    grads_list = []
    for batch in range(tokens.shape[0]):
        current = fetch_weights(shards)
        picks = order[batch]
        dealt_tokens = permuted(tokens[batch], picks)
        sequence, upstream = (
            lax.all_to_all(dealt_tokens, "dp", split_axis=0, concat_axis=1, tiled=True),
            lax.all_to_all(cotangent[batch], "dp", split_axis=0, concat_axis=1, tiled=True),
        )
        length = jnp.sum(jnp.where(jnp.arange(picks.shape[0]) == picks[device], lengths[batch], 0))
        result, stored = forward(current, sequence[0], length)
        behind = (
            lax.all_gather(shards[0], "dp", axis=0, tiled=True),
            lax.all_gather(shards[1], "dp", axis=0, tiled=True),
            lax.all_gather(shards[2], "dp", axis=0, tiled=True),
            lax.all_gather(shards[3], "dp", axis=0, tiled=True),
            lax.all_gather(shards[4], "dp", axis=0, tiled=True),
            lax.all_gather(shards[5], "dp", axis=0, tiled=True),
            lax.all_gather(shards[6], "dp", axis=0, tiled=True),
            lax.all_gather(shards[7], "dp", axis=0, tiled=True),
            lax.all_gather(shards[8], "dp", axis=0, tiled=True),
            lax.all_gather(shards[9], "dp", axis=0, tiled=True),
            lax.all_gather(shards[10], "dp", axis=0, tiled=True),
            lax.all_gather(shards[11], "dp", axis=0, tiled=True),
        )
        input_grad, gradients = backward(behind, sequence[0], upstream[0], stored)
        back_out, back_grad = (
            lax.all_to_all(result[None], "dp", split_axis=1, concat_axis=0, tiled=True),
            lax.all_to_all(input_grad[None], "dp", split_axis=1, concat_axis=0, tiled=True),
        )
        restored = permuted(back_grad, inverse_of(picks))
        outputs_list.append(back_out)
        grads_list.append(restored)
        totals = add_trees(totals, gradients)
    totals = (
        lax.psum_scatter(totals[0], "dp", scatter_dimension=0, tiled=True),
        lax.psum_scatter(totals[1], "dp", scatter_dimension=0, tiled=True),
        lax.psum_scatter(totals[2], "dp", scatter_dimension=0, tiled=True),
        lax.psum_scatter(totals[3], "dp", scatter_dimension=0, tiled=True),
        lax.psum_scatter(totals[4], "dp", scatter_dimension=0, tiled=True),
        lax.psum_scatter(totals[5], "dp", scatter_dimension=0, tiled=True),
        lax.psum_scatter(totals[6], "dp", scatter_dimension=0, tiled=True),
        lax.psum_scatter(totals[7], "dp", scatter_dimension=0, tiled=True),
        lax.psum_scatter(totals[8], "dp", scatter_dimension=0, tiled=True),
        lax.psum_scatter(totals[9], "dp", scatter_dimension=0, tiled=True),
        lax.psum_scatter(totals[10], "dp", scatter_dimension=0, tiled=True),
        lax.psum_scatter(totals[11], "dp", scatter_dimension=0, tiled=True),
    )
    return (
        jnp.stack(outputs_list),
        jnp.stack(grads_list),
        totals[0],
        totals[1],
        totals[2],
        totals[3],
        totals[4],
        totals[5],
        totals[6],
        totals[7],
        totals[8],
        totals[9],
        totals[10],
        totals[11],
    )


COUNT = 32
ROWS, LAYERS = 8, 4


def meet_all(me):
    barrier = pltpu.get_barrier_semaphore()

    def greet(step, carry):
        pl.semaphore_signal(
            barrier, inc=1, device_id=(lax.rem(me + step, COUNT),), device_id_type=MESH
        )
        return carry

    lax.fori_loop(1, COUNT, greet, 0)
    pl.semaphore_wait(barrier, COUNT - 1)


def remote(source, target, send_sem, recv_sem, device):
    return pltpu.make_async_remote_copy(
        src_ref=source,
        dst_ref=target,
        send_sem=send_sem,
        recv_sem=recv_sem,
        device_id=(device,),
        device_id_type=MESH,
    )


WIDTHS = (48, 24, 24, 24, 96, 24, 24, 24)
BIAS_IN, BIAS_MIX, GAIN_FIRST, SHIFT_FIRST, BIAS_UP, BIAS_DOWN, GAIN_SECOND, SHIFT_SECOND = range(8)
TILE = 256
PAIR = 128


def contract(left, right, left_dim, right_dim):
    return lax.dot_general(
        left,
        right,
        (((left_dim,), (right_dim,)), ((), ())),
        preferred_element_type=jnp.float32,
    )


def owners(width):
    lane = lax.broadcasted_iota(jnp.int32, (COUNT, COUNT * width), 1)
    owner = (lane * (-(-(1 << 20) // width))) >> 20
    device = lax.broadcasted_iota(jnp.int32, (COUNT, COUNT * width), 0)
    return owner == device


def places(width):
    lane = lax.broadcasted_iota(jnp.int32, (PAIR, COUNT * width), 1)
    owner = (lane * (-(-(1 << 20) // width))) >> 20
    entry = lax.broadcasted_iota(jnp.int32, (PAIR, COUNT * width), 0)
    return jnp.where(lane - owner * width == entry, 1.0, 0.0).astype(jnp.bfloat16)


def columns(tile, size=TILE):
    return pl.ds(pl.multiple_of(tile * size, size), size)


def flat(value):
    return value.reshape(-1, value.shape[-1])


def take_rows(ref, start, stop):
    layers, seats, groups, small, _ = ref.shape
    pieces = []
    while start < stop:
        layer, rest = divmod(start // small, seats * groups)
        seat, group = divmod(rest, groups)
        whole = min((stop - start) // (small * groups), seats - seat)
        if group == 0 and whole:
            pieces.append(flat(ref[layer, seat : seat + whole]))
            start += whole * groups * small
        else:
            end = min(groups, group + (stop - start) // small)
            pieces.append(flat(ref[layer, seat, group:end]))
            start += (end - group) * small
    return jnp.concatenate(pieces, 0)


class Layer:
    def __init__(self, refs):
        self.__dict__.update(refs)
        self.rows, self.width = self.normed.shape
        self.hidden_width = self.slope.shape[1]

    def spread_small(self):
        for place, width in enumerate(WIDTHS):
            given = self.small[:, place, :].astype(jnp.bfloat16)
            spread = contract(given, places(width), 1, 0)
            row = jnp.sum(jnp.where(owners(width), spread, 0.0), 0, keepdims=True)
            if place == BIAS_IN:
                self.bias_row[:, : self.width] = row[:, : self.width]
                self.bias_row[:, self.width : 2 * self.width] = jnp.zeros_like(row[:, : self.width])
                self.bias_row[:, 2 * self.width :] = row[:, self.width :]
            elif place == BIAS_UP:
                self.up_row[...] = row
            else:
                self.vectors[place : place + 1, :] = row

    def vector(self, place):
        return self.vectors[place : place + 1, :]

    def project(self, tile):
        here = columns(tile)
        value = jnp.dot(
            flat(self.sequence[...]),
            flat(self.weight_in[:, :, :, :, here]),
            preferred_element_type=jnp.float32
        )
        value = (value + self.bias_row[:, here]).astype(jnp.bfloat16)
        scale = jnp.where(tile < self.width // TILE, 0.125, 1.0).astype(jnp.bfloat16)
        self.packed[:, here] = value * scale

    def heads_of(self, step):
        pairs = self.width // PAIR
        batch, pair = step // pairs, step % pairs
        rows = pl.ds(pl.multiple_of(batch * TILE, TILE), TILE)
        return batch, pair, rows

    def block(self, part, rows, pair):
        offset = pl.multiple_of(part * self.width + pair * PAIR, PAIR)
        return self.packed[rows, pl.ds(offset, PAIR)]

    def half(self, value, head):
        lane = lax.broadcasted_iota(jnp.int32, value.shape, 1)
        keep = lane < PAIR // 2 if head == 0 else lane >= PAIR // 2
        return jnp.where(keep, value, jnp.zeros_like(value))

    def attend(self, step):
        batch, pair, rows = self.heads_of(step)
        queries, key_block, value_block = (self.block(part, rows, pair) for part in range(3))
        length = jnp.where(batch == 0, self.lengths[0], self.lengths[1])
        lane = lax.broadcasted_iota(jnp.int32, (1, TILE), 1)
        blocked = jnp.where(lane < length, 0.0, -1e30)
        context = []
        for head in range(2):
            scores = contract(self.half(queries, head), key_block, 1, 1) + blocked
            weights = jnp.exp(scores - jnp.max(scores, -1, keepdims=True))
            total = jnp.sum(weights, -1, keepdims=True)
            low = (weights * (1.0 / total)).astype(jnp.bfloat16)
            self.chances[2 * step + head] = low
            context.append(jnp.dot(low, value_block, preferred_element_type=jnp.float32))
        lane = lax.broadcasted_iota(jnp.int32, context[0].shape, 1)
        joined = jnp.where(lane < PAIR // 2, context[0], context[1])
        self.context[rows, columns(pair, PAIR)] = joined.astype(jnp.bfloat16)

    def mix(self, part):
        rows = columns(part)
        branch = jnp.dot(
            self.context[rows, :], flat(self.weight_mix[...]), preferred_element_type=jnp.float32
        )
        summed = flat(self.sequence[part]).astype(jnp.float32) + (branch + self.vector(BIAS_MIX))
        centered = summed - jnp.mean(summed, -1, keepdims=True)
        factor = lax.rsqrt(jnp.mean(centered * centered, -1, keepdims=True) + epsilon)
        normed = centered * factor
        hidden = normed * self.vector(GAIN_FIRST) + self.vector(SHIFT_FIRST)
        self.normed[rows, :] = normed
        self.factor[rows, :] = factor
        self.hidden_low[rows, :] = hidden.astype(jnp.bfloat16)

    def up(self, tile):
        here = columns(tile)
        value = jnp.dot(
            self.hidden_low[...], flat(self.weight_up[:, :, :, :, here]), preferred_element_type=jnp.float32
        )
        value = value + self.up_row[:, here]
        below = 0.5 * (1.0 + lax.erf(value * 0.7071067811865476))
        density = jnp.exp(-0.5 * value * value) * 0.3989422804014327
        self.active[:, here] = (value * below).astype(jnp.bfloat16)
        self.slope[:, here] = (below + value * density).astype(self.slope.dtype)

    def down(self, tile):
        here = columns(tile)
        self.upper[:, here] = jnp.dot(
            self.active[...], flat(self.weight_down[:, :, :, :, here]), preferred_element_type=jnp.float32
        )

    def finish(self, part, size=128):
        rows = columns(part, size)
        hidden = self.normed[rows, :] * self.vector(GAIN_FIRST) + self.vector(SHIFT_FIRST)
        summed = hidden + (self.upper[rows, :] + self.vector(BIAS_DOWN))
        centered = summed - jnp.mean(summed, -1, keepdims=True)
        factor = lax.rsqrt(jnp.mean(centered * centered, -1, keepdims=True) + epsilon)
        normed = centered * factor
        gain = self.vector(GAIN_SECOND)
        low = (normed * gain + self.vector(SHIFT_SECOND)).astype(jnp.bfloat16)
        parts, seats = TILE // size, size // 8
        batch, span = part // parts, pl.ds((part % parts) * seats, seats)
        self.result[batch, span] = low.reshape(seats, 8, self.width)
        upstream = flat(self.upstream[batch, span]).astype(jnp.float32)
        grad = self.norm_backward(upstream, normed, factor, gain, GAIN_SECOND, SHIFT_SECOND)
        low = grad.astype(jnp.bfloat16)
        self.upper[rows, :] = grad
        self.feed_grad[rows, :] = low
        self.add_term(BIAS_DOWN, low.astype(jnp.float32))

    def add_term(self, place, value):
        self.terms[place : place + 1, :] += jnp.sum(value, 0, keepdims=True)

    def norm_backward(self, upstream, normed, factor, gain, gain_place, shift_place):
        self.add_term(gain_place, upstream * normed)
        self.add_term(shift_place, upstream)
        scaled = upstream * gain
        return factor * (
            scaled
            - jnp.mean(scaled, -1, keepdims=True)
            - normed * jnp.mean(scaled * normed, -1, keepdims=True)
        )

    def down_weight_grad(self, layer):
        span = self.hidden_width // LAYERS
        made = [
            contract(self.active[:, columns(layer * (span // TILE) + i)], self.feed_grad[...], 0, 0)
            for i in range(span // TILE)
        ]
        made = jnp.concatenate([part.astype(jnp.bfloat16) for part in made], 0)
        self.down_grad[layer] = made.reshape(self.down_grad.shape[1:])

    def active_backward(self, layer):
        span = self.hidden_width // LAYERS
        weight = flat(self.weight_down[layer])
        for i in range(span // TILE):
            here = columns(layer * (span // TILE) + i)
            grad = contract(self.feed_grad[...], weight[i * TILE : (i + 1) * TILE], 1, 1)
            low = (grad * self.slope[:, here].astype(jnp.float32)).astype(jnp.bfloat16)
            self.preact_grad[:, here] = low
            self.up_terms[:, here] = jnp.sum(low.astype(jnp.float32), 0, keepdims=True)

    def up_weight_grad(self, tile):
        here = columns(tile)
        grad = contract(self.hidden_low[...], self.preact_grad[:, here], 0, 0)
        self.keep_columns(self.up_grad, here, grad)

    def hidden_backward(self, tile):
        here = columns(tile)
        weight = take_rows(self.weight_up, tile * TILE, (tile + 1) * TILE)
        self.upper[:, here] += contract(self.preact_grad[...], weight, 1, 1)

    def first_backward(self, part, size=128):
        rows = columns(part, size)
        grad = self.norm_backward(
            self.upper[rows, :],
            self.normed[rows, :],
            self.factor[rows, :],
            self.vector(GAIN_FIRST),
            GAIN_FIRST,
            SHIFT_FIRST,
        )
        low = grad.astype(jnp.bfloat16)
        self.upper[rows, :] = grad
        self.feed_grad[rows, :] = low
        self.add_term(BIAS_MIX, low.astype(jnp.float32))

    def mix_weight_grad(self, tile):
        here = columns(tile)
        grad = contract(self.context[...], self.feed_grad[:, here], 0, 0)
        self.keep_columns(self.mix_grad, here, grad)

    def mix_backward(self, tile):
        here = columns(tile)
        weight = take_rows(self.weight_mix, tile * TILE, (tile + 1) * TILE)
        self.context_grad[:, here] = contract(self.feed_grad[...], weight, 1, 1).astype(
            jnp.bfloat16
        )

    def attend_backward(self, step):
        batch, pair, rows = self.heads_of(step)
        queries, key_block, value_block = (self.block(part, rows, pair) for part in range(3))
        grads = self.context_grad[rows, columns(pair, PAIR)]
        query_grad = key_grad = value_grad = 0.0
        for head in range(2):
            low = self.chances[2 * step + head]
            chance = low.astype(jnp.float32)
            mine = self.half(grads, head)
            chance_grad = contract(mine, value_block, 1, 1)
            moved = chance_grad - jnp.sum(chance * chance_grad, -1, keepdims=True)
            score_grad = (chance * moved).astype(jnp.bfloat16)
            value_grad += contract(low, mine, 0, 0)
            query_grad += jnp.dot(
                score_grad, self.half(key_block, head), preferred_element_type=jnp.float32
            )
            key_grad += contract(score_grad, self.half(queries, head), 0, 0)
        for part, grad in enumerate((query_grad * 0.125, key_grad, value_grad)):
            offset = pl.multiple_of(part * self.width + pair * PAIR, PAIR)
            self.packed[rows, pl.ds(offset, PAIR)] = grad.astype(jnp.bfloat16)

    def in_weight_grad(self, tile):
        here = columns(tile)
        grads = self.packed[:, here]
        self.keep_columns(self.in_grad, here, contract(flat(self.sequence[...]), grads, 0, 0))
        self.in_terms[:, here] = jnp.sum(grads.astype(jnp.float32), 0, keepdims=True)

    def input_backward(self, tile):
        here = columns(tile)
        weight = take_rows(self.weight_in, tile * TILE, (tile + 1) * TILE)
        grad = self.upper[:, here] + contract(self.packed[...], weight, 1, 1)
        shape = self.input_grad.shape[:3] + (TILE,)
        self.input_grad[:, :, :, here] = grad.astype(jnp.bfloat16).reshape(shape)

    def keep_columns(self, ref, here, grad):
        ref[:, :, :, :, here] = grad.astype(jnp.bfloat16).reshape(ref.shape[:4] + (TILE,))

    def gather_terms(self):
        for place, width in enumerate(WIDTHS):
            if place == BIAS_IN:
                row = jnp.concatenate(
                    [self.in_terms[:, : self.width], self.in_terms[:, 2 * self.width :]], -1
                )
            elif place == BIAS_UP:
                row = self.up_terms[...]
            else:
                row = self.terms[place : place + 1, :]
            high = row.astype(jnp.bfloat16)
            rest = row - high.astype(jnp.float32)
            middle = rest.astype(jnp.bfloat16)
            low = (rest - middle.astype(jnp.float32)).astype(jnp.bfloat16)
            keep, spots = owners(width), places(width)
            self.small_grad[:, place, :] = sum(
                contract(jnp.where(keep, part.astype(jnp.float32), 0.0).astype(jnp.bfloat16), spots, 1, 1)
                for part in (high, middle, low)
            )


def scratch_of(rows, width, hidden_width):
    low, full = jnp.bfloat16, jnp.float32
    return dict(
        bias_row=pltpu.VMEM((1, 3 * width), full),
        up_row=pltpu.VMEM((1, hidden_width), full),
        vectors=pltpu.VMEM((8, width), full),
        terms=pltpu.VMEM((8, width), full),
        up_terms=pltpu.VMEM((1, hidden_width), full),
        in_terms=pltpu.VMEM((1, 3 * width), full),
        packed=pltpu.VMEM((rows, 3 * width), low),
        chances=pltpu.VMEM((2 * rows // TILE * width // PAIR, TILE, TILE), low),
        context=pltpu.VMEM((rows, width), low),
        normed=pltpu.VMEM((rows, width), full),
        factor=pltpu.VMEM((rows, 1), full),
        hidden_low=pltpu.VMEM((rows, width), low),
        active=pltpu.VMEM((rows, hidden_width), low),
        slope=pltpu.VMEM((rows, hidden_width), low),
        upper=pltpu.VMEM((rows, width), full),
        feed_grad=pltpu.VMEM((rows, width), low),
    )


class Spot:
    def __init__(self):
        self.me = me = lax.axis_index("dp")
        core, column, row = me % 2, (me // 2) % 2, (me // 4) % 2
        self.layer, self.seat = me // 8, me % 8
        self.to_sibling = 1 - 2 * core
        across_row = 4 * (1 - 2 * row)
        across_column = 2 * (1 - 2 * column)
        self.to_second = (1 - core) * across_row + core * across_column
        self.to_third = (1 - core) * across_column + core * across_row
        self.sibling = me + self.to_sibling
        self.second = me + self.to_second
        self.third = me + self.to_third
        self.above = [lax.rem(self.layer + step, LAYERS) for step in (1, 2, 3)]


class Chunk:
    def __init__(self, kind, groups, cols):
        self.kind, self.groups, self.cols = kind, groups, cols

    def line(self, refs, seat):
        return refs[self.kind].at[:, seat, self.groups, :, self.cols]

    def block(self, refs, layer, seat):
        return refs[self.kind].at[layer, seat, self.groups, :, self.cols]

    def bulk(self, refs, layers, lines):
        return refs[self.kind].at[pl.ds(0, layers), pl.ds(0, lines), self.groups, :, self.cols]


def chunks_of(shapes):
    made = []
    for kind, (groups, _, width) in enumerate(shapes):
        if kind < 3:
            size = shapes[1][2]
            for start in range(0, width, size):
                made.append(Chunk(kind, pl.ds(0, groups), pl.ds(start, size)))
        else:
            size = shapes[0][0]
            for start in range(0, groups, size):
                made.append(Chunk(kind, pl.ds(start, size), pl.ds(0, width)))
    return made


class Traffic:
    def __init__(self, spot, refs):
        self.spot = spot
        self.__dict__.update(refs)
        self.chunks = chunks_of([tuple(shard.shape) for shard in self.shards])


    def own(self, k):
        chunk, spot = self.chunks[k], self.spot
        source = self.shards[chunk.kind].at[chunk.groups, :, chunk.cols]
        target = chunk.block(self.full, spot.layer, spot.seat)
        for layer in spot.above:
            remote(
                source, target, self.sent.at[k], self.along_in.at[k], layer * ROWS + spot.seat
            ).start()
        remote(source, target, self.sent.at[k], self.second_own.at[k], spot.second).start()
        remote(source, target, self.sent.at[k], self.third_own.at[k], spot.third).start()

    def line_out(self, k, seat, device, sem):
        line = self.chunks[k].line(self.full, seat)
        remote(line, line, self.sent.at[k], sem, device).start()

    def wait_lines(self, k, sem, count=1):
        chunk = self.chunks[k]
        layers = {0: 1, 3: 3}.get(count, LAYERS)
        here = chunk.bulk(self.full, layers, count if layers == LAYERS else 1)
        return remote(here, here, self.sent.at[k], sem, self.spot.me)

    def from_line(self, k):
        spot = self.spot
        self.wait_lines(k, self.along_in.at[k], 3).wait_recv()
        for layer in spot.above:
            block = self.chunks[k].block(self.full, layer, spot.seat)
            sent = self.sent.at[k]
            remote(block, block, sent, self.second_in.at[k], spot.second).start()
            remote(block, block, sent, self.third_in.at[k, 0], spot.third).start()
        self.line_out(k, spot.seat, spot.sibling, self.sibling_in.at[k])

    def from_second(self, k):
        spot = self.spot
        self.wait_lines(k, self.second_own.at[k], 0).wait_recv()
        self.wait_lines(k, self.second_in.at[k], 3).wait_recv()
        seat = spot.seat + spot.to_second
        self.line_out(k, seat, spot.third, self.third_in.at[k, 1])
        self.line_out(k, seat, spot.sibling, self.sibling_in.at[k])

    def from_third(self, k, which):
        spot = self.spot
        if which == 0:
            self.wait_lines(k, self.third_own.at[k], 0).wait_recv()
        self.wait_lines(k, self.third_in.at[k, which], 1 if which else 3).wait_recv()
        seat = spot.seat + spot.to_third + which * spot.to_second
        self.line_out(k, seat, spot.sibling, self.sibling_in.at[k])

    def complete(self, k):
        self.wait_lines(k, self.sibling_in.at[k], 4).wait_recv()

    def own_sent(self, k):
        self.wait_lines(k, self.sent.at[k], 7).wait_send()
        self.wait_lines(k, self.sent.at[k], 3).wait_send()


    def exchange(self, source, target, which, first=0, last=COUNT - 1):
        me = self.spot.me

        def go(step, carry):
            device = lax.rem(me + lax.rem(step * 5, COUNT), COUNT)
            remote(
                source.at[:, device],
                target.at[:, me],
                self.given.at[which],
                self.taken.at[which],
                device,
            ).start()
            return carry

        lax.fori_loop(1 + first, 1 + last, go, 0)

    def exchanged(self, target, which):
        here = target.at[:, pl.ds(0, COUNT - 1)]
        return remote(
            here,
            here,
            self.given.at[which],
            self.taken.at[which],
            self.spot.me,
        )

    def exchange_small(self, source, target, which):
        me = self.spot.me

        def go(step, carry):
            device = lax.rem(me + step, COUNT)
            remote(
                source if which == 4 else source.at[device],
                target.at[me],
                self.given.at[which],
                self.taken.at[which],
                device,
            ).start()
            return carry

        lax.fori_loop(1, COUNT, go, 0)

    def exchanged_small(self, target, which):
        here = target.at[pl.ds(0, COUNT - 1)]
        return remote(here, here, self.given.at[which], self.taken.at[which], self.spot.me)


    def move(self, k, seat, landing, device, sem):
        remote(
            self.chunks[k].line(self.partial, seat), landing, self.shed.at[k], sem, device
        ).start()

    def landing(self, k, landings, slot):
        chunk = self.chunks[k]
        return landings[chunk.kind].at[slot, :, chunk.groups, :, chunk.cols]

    def landed(self, k, landings, sem, layers=LAYERS):
        chunk = self.chunks[k]
        here = landings[chunk.kind].at[:, pl.ds(0, layers), chunk.groups, :, chunk.cols]
        remote(here, here, self.shed.at[k], sem, self.spot.me).wait_recv()

    def take_in(self, k, seat, landings, slot):
        chunk = self.chunks[k]
        line, here = chunk.line(self.partial, seat), self.landing(k, landings, slot)
        line[...] = line[...] + here[...]


    def move_block(self, k, layer, seat, landings, slot, device, sem):
        chunk = self.chunks[k]
        remote(
            chunk.block(self.partial, layer, seat),
            landings[chunk.kind].at[slot, layer, chunk.groups, :, chunk.cols],
            self.shed.at[k],
            sem,
            device,
        ).start()

    def take_block(self, k, layer, seat, landings, slot):
        chunk = self.chunks[k]
        block = chunk.block(self.partial, layer, seat)
        here = landings[chunk.kind].at[slot, layer, chunk.groups, :, chunk.cols]
        block[...] = block[...] + here[...]

    def blocks_to_third(self, k, layers, sem):
        spot = self.spot
        for layer in layers:
            for slot in range(2):
                seat = spot.seat + spot.to_third + slot * spot.to_second
                self.move_block(k, layer, seat, self.land_third, slot, spot.third, sem)

    def blocks_to_second(self, k, layers, sem, next_sem):
        spot = self.spot
        self.landed(k, self.land_third, sem, len(layers))
        for layer in layers:
            for slot in range(2):
                seat = spot.seat + slot * spot.to_second
                self.take_block(k, layer, seat, self.land_third, slot)
            seat = spot.seat + spot.to_second
            self.move_block(k, layer, seat, self.land_second, 0, spot.second, next_sem)

    def late_third(self, k):
        self.blocks_to_third(k, [self.spot.layer], self.across_own.at[k])

    def late_second(self, k):
        self.blocks_to_second(
            k, [self.spot.layer], self.across_own.at[k], self.over_own.at[k]
        )

    def late_owner(self, k):
        self.landed(k, self.land_second, self.over_own.at[k], 1)
        self.take_block(k, self.spot.layer, self.spot.seat, self.land_second, 0)
        self.keep(k).start()

    def begin(self, k):
        spot = self.spot
        for slot in range(4):
            seat = 2 * slot + (spot.seat + 1) % 2
            self.move(
                k, seat, self.landing(k, self.land_first, slot), spot.sibling, self.first_in.at[k]
            )

    def to_third(self, k):
        spot = self.spot
        self.landed(k, self.land_first, self.first_in.at[k])
        for slot in range(4):
            self.take_in(k, 2 * slot + spot.seat % 2, self.land_first, slot)
        if k in self.late:
            self.blocks_to_third(k, spot.above, self.across_in.at[k])
            return
        for slot in range(2):
            seat = spot.seat + spot.to_third + slot * spot.to_second
            self.move(
                k, seat, self.landing(k, self.land_third, slot), spot.third, self.across_in.at[k]
            )

    def to_second(self, k):
        spot = self.spot
        if k in self.late:
            self.blocks_to_second(k, spot.above, self.across_in.at[k], self.over_in.at[k])
            return
        self.landed(k, self.land_third, self.across_in.at[k])
        for slot in range(2):
            self.take_in(k, spot.seat + slot * spot.to_second, self.land_third, slot)
        seat = spot.seat + spot.to_second
        self.move(k, seat, self.landing(k, self.land_second, 0), spot.second, self.over_in.at[k])

    def to_owner(self, k):
        chunk, spot = self.chunks[k], self.spot
        if k in self.late:
            self.landed(k, self.land_second, self.over_in.at[k], 3)
            for layer in spot.above:
                self.take_block(k, layer, spot.seat, self.land_second, 0)
        else:
            self.landed(k, self.land_second, self.over_in.at[k])
            self.take_in(k, spot.seat, self.land_second, 0)
        target = self.sums[chunk.kind].at[spot.layer, chunk.groups, :, chunk.cols]
        for layer in spot.above:
            remote(
                chunk.block(self.partial, layer, spot.seat),
                target,
                self.shed.at[k],
                self.owner_in.at[k],
                layer * ROWS + spot.seat,
            ).start()
        if k not in self.late:
            self.keep(k).start()

    def keep(self, k):
        chunk, spot = self.chunks[k], self.spot
        return pltpu.make_async_copy(
            chunk.block(self.partial, spot.layer, spot.seat),
            self.sums[chunk.kind].at[spot.layer, chunk.groups, :, chunk.cols],
            self.kept.at[k],
        )

    def settle(self, k):
        chunk = self.chunks[k]
        here = self.sums[chunk.kind].at[pl.ds(0, 3), chunk.groups, :, chunk.cols]
        remote(here, here, self.shed.at[k], self.owner_in.at[k], self.spot.me).wait_recv()
        self.keep(k).wait()
        for count in (7, 3):
            there = chunk.bulk(self.partial, 3 if count == 3 else LAYERS, 1 if count == 3 else count)
            remote(there, there, self.shed.at[k], self.owner_in.at[k], self.spot.me).wait_send()


def interleave(count, body, steps=()):
    assert len(steps) <= count

    def one(index, carry):
        body(index)
        for place, thunks in enumerate(steps):
            if thunks:

                @pl.when(index == place)
                def _():
                    for thunk in thunks:
                        thunk()

        return carry

    lax.fori_loop(0, count, one, 0)


def unroll(count, body, steps):
    for index in range(count):
        body(index)
        for thunk in steps[index]:
            thunk()


def spread(thunks, slots):
    return [
        thunks[len(thunks) * place // slots : len(thunks) * (place + 1) // slots]
        for place in range(slots)
    ]


LATE = 11
PACES = 3, 3, 3, 0, 1, 2, 6, 3, 1
LEAD, TOKENS_EACH, COTANGENT_FROM, COTANGENT_EACH = 1, 6, 4, 4


def step_kernel(trees, *given):
    given, named = list(given), {}
    for tree in trees:
        named.update(jax.tree.unflatten(tree, given[: tree.num_leaves]))
        given = given[tree.num_leaves :]
    refs = types.SimpleNamespace(**named)
    spot = Spot()
    me = spot.me
    traffic = Traffic(spot, named)
    chunks = range(len(traffic.chunks))
    tokens, cotangent = refs.tokens, refs.cotangent
    sequence, upstream = refs.sequence, refs.upstream
    first_spare, second_spare = refs.first_spare, refs.second_spare

    locals_ = [
        pltpu.make_async_copy(
            traffic.shards[kind], traffic.full[kind].at[spot.layer, spot.seat], traffic.local.at[kind]
        )
        for kind in range(4)
    ] + [
        pltpu.make_async_copy(cotangent.at[:, me], upstream.at[:, me], traffic.local.at[5]),
        pltpu.make_async_copy(refs.small_own, refs.small.at[me], traffic.local.at[6]),
    ]
    early = [
        pltpu.make_async_copy(tokens, first_spare, traffic.local.at[4]),
        pltpu.make_async_copy(refs.lengths, refs.lengths_here, traffic.local.at[7]),
        pltpu.make_async_copy(refs.order, refs.order_here, traffic.local.at[8]),
    ]
    for copy in early + locals_:
        copy.start()
    for copy in early:
        copy.wait()
    for batch in range(2):
        for seat in range(COUNT):
            second_spare[batch, seat] = first_spare[batch, refs.order_here[batch, seat]]
    own_sequence = pltpu.make_async_copy(
        second_spare.at[:, me], sequence.at[:, me], traffic.local.at[4]
    )
    own_sequence.start()
    meet_all(me)

    def piece_of(source, target, which, first, last):
        return lambda: traffic.exchange(source, target, which, first, last)

    def do(method, *args):
        return lambda: method(*args)

    layer = Layer(named)
    layer.context_grad, layer.preact_grad = refs.hidden_low, refs.active
    layer.result, layer.input_grad = first_spare, second_spare
    layer.weight_in, layer.weight_mix, layer.weight_up, layer.weight_down = refs.full
    layer.in_grad, layer.mix_grad, layer.up_grad, layer.down_grad = refs.partial
    layer.lengths = [
        refs.lengths_here[batch, refs.order_here[batch, me]] for batch in range(2)
    ]
    tiles, wide = layer.width // TILE, layer.hidden_width // TILE
    pairs = 2 * (layer.width // PAIR)
    ins = 3
    ups = wide // tiles
    assert len(chunks) == ins + 1 + 2 * ups

    ticks = []
    for tick in range(-LEAD, len(chunks) + 2):
        here = []
        if 0 <= tick + LEAD < len(chunks):
            here.append(do(traffic.own, tick + LEAD))
        first = (tick + LEAD) * TOKENS_EACH
        if first < COUNT - 1:
            last = min(first + TOKENS_EACH, COUNT - 1)
            here.append(piece_of(second_spare, sequence, 0, first, last))
        if tick == -LEAD:
            here.append(do(traffic.exchange_small, refs.small_own, refs.small, 4))
        if 0 <= tick < len(chunks):
            here.append(do(traffic.from_line, tick))
        if 0 <= tick - 1 < len(chunks):
            here.append(do(traffic.from_second, tick - 1))
            here.append(do(traffic.from_third, tick - 1, 0))
        if 0 <= tick - 2 < len(chunks):
            here.append(do(traffic.from_third, tick - 2, 1))
        first = (tick - COTANGENT_FROM) * COTANGENT_EACH
        if 0 <= first < COUNT - 1:
            last = min(first + COTANGENT_EACH, COUNT - 1)
            here.append(piece_of(cotangent, upstream, 1, first, last))
        ticks.append(here)
    flat = lambda first, last: [thunk for here in ticks[first + LEAD : last + LEAD] for thunk in here]

    for thunk in flat(-LEAD, 0):
        thunk()
    for copy in locals_:
        copy.wait()
    layer.terms[...] = jnp.zeros_like(layer.terms)
    for thunk in flat(0, 2):
        thunk()
    traffic.exchanged_small(refs.small, 4).wait_recv()
    layer.spread_small()
    for thunk in flat(2, ins + 2):
        thunk()
    dealt = traffic.exchanged(sequence, 0)
    dealt.wait_recv()
    own_sequence.wait()
    for k in range(ins):
        traffic.complete(k)
    interleave(3 * tiles, layer.project, spread(flat(ins + 2, ins + 3), 3 * tiles))
    interleave(pairs, layer.attend, spread(flat(ins + 3, ins + 6), pairs))
    traffic.complete(ins)
    interleave(layer.rows // TILE, layer.mix)
    for thunk in flat(ins + 6, ins + ups + 3):
        thunk()
    for k in range(ins + 1, ins + 1 + ups):
        traffic.complete(k)
    interleave(wide, layer.up, spread(flat(ins + ups + 3, len(chunks) + 2), wide))
    for k in range(ins + 1 + ups, len(chunks)):
        traffic.complete(k)
    interleave(tiles, layer.down)
    cotangents = traffic.exchanged(upstream, 1)
    cotangents.wait_recv()
    interleave(layer.rows // 128, layer.finish)

    keep_result = pltpu.make_async_copy(
        first_spare.at[:, me], refs.returned.at[:, me], traffic.local.at[0]
    )
    keep_result.start()
    pieces = [
        piece_of(first_spare, refs.returned, 2, first, min(first + 4, COUNT - 1))
        for first in range(0, COUNT - 1, 4)
    ]
    interleave(LAYERS, layer.down_weight_grad, spread(pieces, LAYERS))

    queue = list(range(ins + 1 + ups, len(chunks))) + list(range(ins + 1, ins + 1 + ups))
    queue += [ins] + list(range(ins))
    traffic.late = queue[len(queue) - LATE :]
    walk = []
    for tick in range(len(queue) + 2):
        for late, stage in enumerate((traffic.to_third, traffic.to_second, traffic.to_owner)):
            if 0 <= tick - late < len(queue):
                walk.append(do(stage, queue[tick - late]))
        if tick == len(queue) - 1:
            walk += [do(traffic.late_third, k) for k in traffic.late]
    for stage in (traffic.late_second, traffic.late_owner):
        walk += [do(stage, k) for k in traffic.late]

    def next_steps(count):
        taken, walk[:] = walk[:count], walk[count:]
        return taken

    def with_begin(steps, count, every, kinds):
        made = [list(step) for step in steps] + [[] for _ in range(count - len(steps))]
        for place, k in enumerate(kinds):
            made[(place + 1) * every - 1].insert(0, do(traffic.begin, k))
        return made

    for k in queue[:ups]:
        traffic.begin(k)
    paces = iter(PACES)
    interleave(LAYERS, layer.active_backward, spread(next_steps(next(paces)), LAYERS))
    interleave(
        wide,
        layer.up_weight_grad,
        with_begin(
            [[]] * tiles + spread(next_steps(next(paces)), wide - tiles),
            wide,
            tiles,
            queue[ups : 2 * ups],
        ),
    )
    unroll(tiles, layer.hidden_backward, spread(next_steps(next(paces)), tiles))
    interleave(layer.rows // 128, layer.first_backward, spread(next_steps(next(paces)), 1))
    interleave(
        tiles,
        layer.mix_weight_grad,
        with_begin(
            spread(next_steps(next(paces)), tiles), tiles, tiles, queue[2 * ups : 2 * ups + 1]
        ),
    )
    unroll(tiles, layer.mix_backward, spread(next_steps(next(paces)), tiles))
    interleave(pairs, layer.attend_backward, spread(next_steps(next(paces)), pairs))
    interleave(
        3 * tiles,
        layer.in_weight_grad,
        with_begin(
            spread(next_steps(next(paces)), 3 * tiles), 3 * tiles, tiles, queue[2 * ups + 1 :]
        ),
    )
    dealt.wait_send()
    unroll(tiles, layer.input_backward, spread(next_steps(next(paces)), tiles))
    keep_grad = pltpu.make_async_copy(
        second_spare.at[:, me], refs.tokens_grad.at[:, me], traffic.local.at[2]
    )
    keep_grad.start()
    left = next_steps(len(walk))

    def small_out():
        layer.gather_terms()
        traffic.exchange_small(refs.small_grad, refs.small_sums, 5)
        keep_small.start()

    keep_small = pltpu.make_async_copy(
        refs.small_grad.at[me], refs.small_sums.at[me], traffic.local.at[1]
    )
    left.insert(2, small_out)
    cuts = list(range(0, COUNT - 1, 4))
    for place in range(max(len(left), len(cuts))):
        if place < len(cuts):
            piece_of(
                second_spare, refs.tokens_grad, 3, cuts[place], min(cuts[place] + 4, COUNT - 1)
            )()
        if place < len(left):
            left[place]()
    for k in queue:
        traffic.settle(k)
        traffic.own_sent(k)
    cotangents.wait_send()
    for target, which in ((refs.returned, 2), (refs.tokens_grad, 3)):
        copy = traffic.exchanged(target, which)
        copy.wait_recv()
        copy.wait_send()
    traffic.exchanged_small(refs.small, 4).wait_send()
    small = traffic.exchanged_small(refs.small_sums, 5)
    small.wait_recv()
    small.wait_send()
    for copy in (keep_result, keep_small, keep_grad):
        copy.wait()


def encoder_step(lengths, order, tokens, cotangent, shards, small_own):
    low, full = jnp.bfloat16, jnp.float32
    width, hidden_width = tokens.shape[-1], shards[2].shape[-1]
    rows = tokens.shape[0] * COUNT * tokens.shape[2]
    anywhere = pl.BlockSpec(memory_space=pl.ANY)
    inputs = dict(
        lengths=lengths,
        order=order,
        tokens=tokens,
        cotangent=cotangent,
        shards=shards,
        small_own=small_own,
    )
    shapes = [shard.shape for shard in shards]
    smalls = ((COUNT,) + small_own.shape, full)
    outputs = dict(
        returned=jax.ShapeDtypeStruct(tokens.shape, low),
        tokens_grad=jax.ShapeDtypeStruct(tokens.shape, low),
        sums=[jax.ShapeDtypeStruct((LAYERS,) + shape, low) for shape in shapes],
        small_sums=jax.ShapeDtypeStruct(*smalls),
    )
    sequences = pltpu.VMEM(tokens.shape, low)
    scratch = dict(
        full=[pltpu.VMEM((LAYERS, ROWS) + shape, low) for shape in shapes],
        partial=[pltpu.VMEM((LAYERS, ROWS) + shape, low) for shape in shapes],
        land_first=[pltpu.VMEM((4, LAYERS) + shape, low) for shape in shapes],
        land_third=[pltpu.VMEM((2, LAYERS) + shape, low) for shape in shapes],
        land_second=[pltpu.VMEM((1, LAYERS) + shape, low) for shape in shapes],
        sequence=sequences,
        upstream=sequences,
        first_spare=sequences,
        second_spare=sequences,
        lengths_here=pltpu.SMEM(lengths.shape, lengths.dtype),
        order_here=pltpu.SMEM(order.shape, order.dtype),
        small=pltpu.VMEM(*smalls),
        small_grad=pltpu.VMEM(*smalls),
        **scratch_of(rows, width, hidden_width),
    )
    count = len(chunks_of(shapes))
    each = pltpu.SemaphoreType.DMA((count,))
    sems = dict(
        local=pltpu.SemaphoreType.DMA((9,)),
        given=pltpu.SemaphoreType.DMA((6,)),
        taken=pltpu.SemaphoreType.DMA((6,)),
        third_in=pltpu.SemaphoreType.DMA((count, 2)),
        sent=each,
        along_in=each,
        second_in=each,
        second_own=each,
        third_own=each,
        sibling_in=each,
        shed=each,
        first_in=each,
        across_in=each,
        over_in=each,
        across_own=each,
        over_own=each,
        owner_in=each,
        kept=each,
    )
    given, given_tree = jax.tree.flatten(inputs)
    made, made_tree = jax.tree.flatten(outputs)
    held, held_tree = jax.tree.flatten({**scratch, **sems})
    results = pl.pallas_call(
        functools.partial(step_kernel, (given_tree, made_tree, held_tree)),
        out_shape=made,
        in_specs=[anywhere] * len(given),
        out_specs=[anywhere] * len(made),
        scratch_shapes=held,
        compiler_params=pltpu.CompilerParams(
            collective_id=0, has_side_effects=True, vmem_limit_bytes=VMEM_LIMIT
        ),
        name="encoder_step",
    )(*given)
    results = jax.tree.unflatten(made_tree, results)
    return types.SimpleNamespace(**results)


VMEM_LIMIT = 63 << 20


def finish_kernel(order, *refs):
    sources, targets, inner, ready = refs[:7], refs[7:21], refs[21:28], refs[28:42]
    sems, out_sems = refs[42:]
    copies = [
        pltpu.make_async_copy(source, target, sems.at[place])
        for place, (source, target) in enumerate(zip(sources, (ready[0], *inner[1:])))
    ]
    outward = [
        pltpu.make_async_copy(source, target, out_sems.at[place])
        for place, (source, target) in enumerate(zip(ready, targets))
    ]
    for place in (1, 0, 6, 2, 3, 4, 5):
        copies[place].start()
    copies[1].wait()
    for batch in range(2):
        for slot in range(COUNT):
            ready[1][batch, order[batch, slot]] = inner[1][batch, slot]
    outward[1].start()
    copies[0].wait()
    outward[0].start()
    copies[6].wait()
    small = jnp.sum(inner[6][...], 0)
    for place, out in enumerate(ready[6:]):
        out[...] = small[place : place + 1, : out.shape[1]]
        outward[6 + place].start()
    for place in (2, 3, 4, 5):
        copies[place].wait()
        parts = inner[place]
        ready[place][...] = sum(parts[layer].astype(jnp.float32) for layer in range(LAYERS))
        outward[place].start()
    for copy in outward:
        copy.wait()


def finish_step(order, returned, tokens_grad, sums, small_sums):
    outside = pl.BlockSpec(memory_space=pltpu.HBM)
    parts = [returned, tokens_grad, *sums, small_sums]
    made = (
        [jax.ShapeDtypeStruct(returned.shape, returned.dtype)] * 2
        + [jax.ShapeDtypeStruct(part.shape[1:], jnp.float32) for part in sums]
        + [jax.ShapeDtypeStruct((1, width), jnp.float32) for width in WIDTHS]
    )
    return pl.pallas_call(
        finish_kernel,
        out_shape=made,
        in_specs=[pl.BlockSpec(memory_space=pltpu.SMEM)] + [outside] * len(parts),
        out_specs=[outside] * len(made),
        scratch_shapes=[pltpu.VMEM(part.shape, part.dtype) for part in parts + made]
        + [pltpu.SemaphoreType.DMA((len(parts),)), pltpu.SemaphoreType.DMA((len(made),))],
        compiler_params=pltpu.CompilerParams(vmem_limit_bytes=VMEM_LIMIT),
        name="finish_step",
    )(order, *parts)


SMALL = (1, 3, 4, 5, 7, 9, 10, 11)
LARGE = (0, 2, 6, 8)


def local(tokens, lengths, order, *rest):
    shards, cotangent = rest[:12], rest[12]
    if lax.axis_size("dp") != COUNT or tokens.shape[2] % 8:
        return portable(tokens, lengths, order, *rest)
    small = sum(
        lax.pad(
            shards[i].astype(jnp.float32)[None],
            jnp.float32(0),
            ((place, len(SMALL) - 1 - place, 0), (0, 128 - shards[i].shape[0], 0)),
        )
        for place, i in enumerate(SMALL)
    )
    made = encoder_step(
        lengths,
        order,
        tokens,
        cotangent,
        [shards[i].reshape(-1, 8, shards[i].shape[-1]) for i in LARGE],
        small,
    )
    layer_out, tokens_grad, *rest = finish_step(
        order, made.returned, made.tokens_grad, made.sums, made.small_sums
    )
    outputs = [None] * 12
    for i, total in zip(LARGE, rest[:4]):
        outputs[i] = total.reshape(-1, total.shape[-1])
    for i, total in zip(SMALL, rest[4:]):
        outputs[i] = total.reshape(-1)
    return (layer_out, tokens_grad, *outputs)


def solution(mesh):
    return jax.shard_map(
        local,
        mesh=mesh,
        in_specs=(
            P(None, None, "dp", None),
            P(),
            P(),
            P("dp", None),
            P("dp"),
            P("dp", None),
            P("dp"),
            P("dp"),
            P("dp"),
            P("dp", None),
            P("dp"),
            P("dp", None),
            P("dp"),
            P("dp"),
            P("dp"),
            P(None, None, "dp", None),
        ),
        out_specs=(
            P(None, None, "dp", None),
            P(None, None, "dp", None),
            P("dp", None),
            P("dp"),
            P("dp", None),
            P("dp"),
            P("dp"),
            P("dp"),
            P("dp", None),
            P("dp"),
            P("dp", None),
            P("dp"),
            P("dp"),
            P("dp"),
        ),
        check_vma=False,
    )
```

```python
import functools
import types

import jax
import jax.numpy as jnp
from jax import lax
from jax.experimental import pallas as pl
from jax.experimental.pallas import tpu as pltpu
from jax.sharding import PartitionSpec as P

MESH = pl.DeviceIdType.MESH

HD = 64


epsilon = 1e-12


def matmul(left, right):
    return jnp.dot(left, right, preferred_element_type=jnp.float32)


def rows_product(left, right):
    return lax.dot_general(
        left, right, (((0,), (0,)), ((), ())), preferred_element_type=jnp.float32
    )


def right_transposed(left, right):
    return lax.dot_general(
        left, right, (((1,), (1,)), ((), ())), preferred_element_type=jnp.float32
    )


def split_heads(block, heads):
    return block.reshape(block.shape[0], heads, -1).transpose(1, 0, 2)


def join_heads(block):
    return block.transpose(1, 0, 2).reshape(block.shape[1], -1)


def norm_forward(summed, norm_gain, norm_shift):
    row_mean = jnp.mean(summed, -1, keepdims=True)
    centered = summed - row_mean
    reciprocal = lax.rsqrt(jnp.mean(centered * centered, -1, keepdims=True) + epsilon)
    normed = centered * reciprocal
    return (normed * norm_gain + norm_shift, normed, reciprocal)


def norm_backward(upstream, normed, reciprocal, norm_gain):
    scaled = upstream * norm_gain
    summed_grad = reciprocal * (
        scaled
        - jnp.mean(scaled, -1, keepdims=True)
        - normed * jnp.mean(scaled * normed, -1, keepdims=True)
    )
    return (summed_grad, jnp.sum(upstream * normed, 0), jnp.sum(upstream, 0))


def head_scores(head_query, head_keys, valid):
    scores = right_transposed(head_query, head_keys) * 0.125
    return jnp.where(valid[None, :], scores, -1e30)


def attend_forward(packed, valid):
    head_query, head_keys, head_values = packed
    scores = head_scores(head_query, head_keys, valid)
    row_max = jnp.max(scores, -1, keepdims=True)
    weights_raw = jnp.exp(scores - row_max)
    row_sum = jnp.sum(weights_raw, -1, keepdims=True)
    probability = weights_raw / row_sum
    context = matmul(probability.astype(jnp.bfloat16), head_values)
    return (context, (row_max + jnp.log(row_sum))[:, 0])


def attend_backward(packed, valid):
    head_query, head_keys, head_values, context_grad, log_total = packed
    scores = head_scores(head_query, head_keys, valid)
    probability = jnp.exp(scores - log_total[:, None])
    low_prob = probability.astype(jnp.bfloat16)
    prob_grad = right_transposed(context_grad, head_values)
    value_grad = rows_product(low_prob, context_grad)
    shifted = prob_grad - jnp.sum(probability * prob_grad, -1, keepdims=True)
    score_grad = (probability * shifted).astype(jnp.bfloat16)
    query_grad = matmul(score_grad, head_keys) * 0.125
    key_grad = rows_product(score_grad, head_query) * 0.125
    return (query_grad, key_grad, value_grad)


def forward(weights, sequence, length):
    (
        weight_in,
        bias_in,
        weight_mix,
        bias_mix,
        gain_first,
        shift_first,
        weight_up,
        bias_up,
        weight_down,
        bias_down,
        gain_second,
        shift_second,
    ) = weights
    width = sequence.shape[1]
    heads = width // HD
    valid = jnp.arange(sequence.shape[0], dtype=jnp.int32) < length
    bias_full = jnp.concatenate(
        [
            bias_in[:width].astype(jnp.float32),
            jnp.zeros((width,), jnp.float32),
            bias_in[width:].astype(jnp.float32),
        ]
    )
    projected = (matmul(sequence, weight_in) + bias_full).astype(jnp.bfloat16)
    queries = split_heads(projected[:, :width], heads)
    key_heads = split_heads(projected[:, width : 2 * width], heads)
    value_heads = split_heads(projected[:, 2 * width :], heads)
    context, log_total = lax.map(
        lambda packed: attend_forward(packed, valid), (queries, key_heads, value_heads)
    )
    context_low = join_heads(context).astype(jnp.bfloat16)
    branch = matmul(context_low, weight_mix) + bias_mix.astype(jnp.float32)
    hidden, normed_first, recip_first = norm_forward(
        sequence.astype(jnp.float32) + branch,
        gain_first.astype(jnp.float32),
        shift_first.astype(jnp.float32),
    )
    hidden_low = hidden.astype(jnp.bfloat16)
    preact = matmul(hidden_low, weight_up) + bias_up.astype(jnp.float32)
    activated = jax.nn.gelu(preact, approximate=False).astype(jnp.bfloat16)
    feed_out = matmul(activated, weight_down) + bias_down.astype(jnp.float32)
    result, normed_second, recip_second = norm_forward(
        hidden + feed_out, gain_second.astype(jnp.float32), shift_second.astype(jnp.float32)
    )
    stored = (
        valid,
        queries,
        key_heads,
        value_heads,
        log_total,
        context_low,
        normed_first,
        recip_first,
        hidden_low,
        preact,
        activated,
        normed_second,
        recip_second,
    )
    return (result.astype(jnp.bfloat16), stored)


def backward(weights, sequence, upstream_low, stored):
    (
        weight_in,
        bias_in,
        weight_mix,
        bias_mix,
        gain_first,
        shift_first,
        weight_up,
        bias_up,
        weight_down,
        bias_down,
        gain_second,
        shift_second,
    ) = weights
    (
        valid,
        queries,
        key_heads,
        value_heads,
        log_total,
        context_low,
        normed_first,
        recip_first,
        hidden_low,
        preact,
        activated,
        normed_second,
        recip_second,
    ) = stored
    width = sequence.shape[1]
    heads = width // HD
    upstream = upstream_low.astype(jnp.float32)
    second_grad, gain_second_grad, shift_second_grad = norm_backward(
        upstream, normed_second, recip_second, gain_second.astype(jnp.float32)
    )
    feed_grad = second_grad.astype(jnp.bfloat16)
    bias_down_grad = jnp.sum(feed_grad.astype(jnp.float32), 0)
    weight_down_grad = rows_product(activated, feed_grad)
    act_grad = right_transposed(feed_grad, weight_down)
    slope = (
        0.5 * (1.0 + jax.scipy.special.erf(preact * 0.7071067811865476))
        + preact * jnp.exp(-0.5 * preact * preact) * 0.3989422804014327
    )
    preact_grad = (act_grad * slope).astype(jnp.bfloat16)
    bias_up_grad = jnp.sum(preact_grad.astype(jnp.float32), 0)
    weight_up_grad = rows_product(hidden_low, preact_grad)
    hidden_grad = second_grad + right_transposed(preact_grad, weight_up)
    first_grad, gain_first_grad, shift_first_grad = norm_backward(
        hidden_grad, normed_first, recip_first, gain_first.astype(jnp.float32)
    )
    branch_grad = first_grad.astype(jnp.bfloat16)
    bias_mix_grad = jnp.sum(branch_grad.astype(jnp.float32), 0)
    weight_mix_grad = rows_product(context_low, branch_grad)
    context_grad = right_transposed(branch_grad, weight_mix).astype(jnp.bfloat16)
    query_grad, key_grad, value_grad = lax.map(
        lambda packed: attend_backward(packed, valid),
        (queries, key_heads, value_heads, split_heads(context_grad, heads), log_total),
    )
    projected_grad = jnp.concatenate(
        [join_heads(query_grad), join_heads(key_grad), join_heads(value_grad)], -1
    ).astype(jnp.bfloat16)
    column_sums = jnp.sum(projected_grad.astype(jnp.float32), 0)
    bias_in_grad = jnp.concatenate([column_sums[:width], column_sums[2 * width :]])
    weight_in_grad = rows_product(sequence, projected_grad)
    input_grad = (first_grad + right_transposed(projected_grad, weight_in)).astype(jnp.bfloat16)
    gradients = (
        weight_in_grad,
        bias_in_grad,
        weight_mix_grad,
        bias_mix_grad,
        gain_first_grad,
        shift_first_grad,
        weight_up_grad,
        bias_up_grad,
        weight_down_grad,
        bias_down_grad,
        gain_second_grad,
        shift_second_grad,
    )
    return (input_grad, gradients)


def permuted(blocks, picks):
    chosen = (picks[:, None] == jnp.arange(picks.shape[0])[None, :]).astype(blocks.dtype)
    flat = blocks.reshape(blocks.shape[0], -1)
    return matmul(chosen, flat).astype(blocks.dtype).reshape(blocks.shape)


def inverse_of(picks):
    slots = jnp.arange(picks.shape[0], dtype=jnp.int32)
    return jnp.sum(jnp.where(picks[:, None] == slots[None, :], slots[:, None], 0), 0)


def fetch_weights(shards):
    return (
        lax.all_gather(shards[0], "dp", axis=0, tiled=True),
        lax.all_gather(shards[1], "dp", axis=0, tiled=True),
        lax.all_gather(shards[2], "dp", axis=0, tiled=True),
        lax.all_gather(shards[3], "dp", axis=0, tiled=True),
        lax.all_gather(shards[4], "dp", axis=0, tiled=True),
        lax.all_gather(shards[5], "dp", axis=0, tiled=True),
        lax.all_gather(shards[6], "dp", axis=0, tiled=True),
        lax.all_gather(shards[7], "dp", axis=0, tiled=True),
        lax.all_gather(shards[8], "dp", axis=0, tiled=True),
        lax.all_gather(shards[9], "dp", axis=0, tiled=True),
        lax.all_gather(shards[10], "dp", axis=0, tiled=True),
        lax.all_gather(shards[11], "dp", axis=0, tiled=True),
    )


def add_trees(first, second):
    if first is None:
        return second
    return jax.tree.map(lambda left, right: left + right, first, second)


def portable(
    tokens,
    lengths,
    order,
    weight_in,
    bias_in,
    weight_mix,
    bias_mix,
    gain_first,
    shift_first,
    weight_up,
    bias_up,
    weight_down,
    bias_down,
    gain_second,
    shift_second,
    cotangent,
):
    shards = (
        weight_in,
        bias_in,
        weight_mix,
        bias_mix,
        gain_first,
        shift_first,
        weight_up,
        bias_up,
        weight_down,
        bias_down,
        gain_second,
        shift_second,
    )
    device = lax.axis_index("dp")
    totals = None
    outputs_list = []
    grads_list = []
    for batch in range(tokens.shape[0]):
        current = fetch_weights(shards)
        picks = order[batch]
        dealt_tokens = permuted(tokens[batch], picks)
        sequence, upstream = (
            lax.all_to_all(dealt_tokens, "dp", split_axis=0, concat_axis=1, tiled=True),
            lax.all_to_all(cotangent[batch], "dp", split_axis=0, concat_axis=1, tiled=True),
        )
        length = jnp.sum(jnp.where(jnp.arange(picks.shape[0]) == picks[device], lengths[batch], 0))
        result, stored = forward(current, sequence[0], length)
        behind = (
            lax.all_gather(shards[0], "dp", axis=0, tiled=True),
            lax.all_gather(shards[1], "dp", axis=0, tiled=True),
            lax.all_gather(shards[2], "dp", axis=0, tiled=True),
            lax.all_gather(shards[3], "dp", axis=0, tiled=True),
            lax.all_gather(shards[4], "dp", axis=0, tiled=True),
            lax.all_gather(shards[5], "dp", axis=0, tiled=True),
            lax.all_gather(shards[6], "dp", axis=0, tiled=True),
            lax.all_gather(shards[7], "dp", axis=0, tiled=True),
            lax.all_gather(shards[8], "dp", axis=0, tiled=True),
            lax.all_gather(shards[9], "dp", axis=0, tiled=True),
            lax.all_gather(shards[10], "dp", axis=0, tiled=True),
            lax.all_gather(shards[11], "dp", axis=0, tiled=True),
        )
        input_grad, gradients = backward(behind, sequence[0], upstream[0], stored)
        back_out, back_grad = (
            lax.all_to_all(result[None], "dp", split_axis=1, concat_axis=0, tiled=True),
            lax.all_to_all(input_grad[None], "dp", split_axis=1, concat_axis=0, tiled=True),
        )
        restored = permuted(back_grad, inverse_of(picks))
        outputs_list.append(back_out)
        grads_list.append(restored)
        totals = add_trees(totals, gradients)
    totals = (
        lax.psum_scatter(totals[0], "dp", scatter_dimension=0, tiled=True),
        lax.psum_scatter(totals[1], "dp", scatter_dimension=0, tiled=True),
        lax.psum_scatter(totals[2], "dp", scatter_dimension=0, tiled=True),
        lax.psum_scatter(totals[3], "dp", scatter_dimension=0, tiled=True),
        lax.psum_scatter(totals[4], "dp", scatter_dimension=0, tiled=True),
        lax.psum_scatter(totals[5], "dp", scatter_dimension=0, tiled=True),
        lax.psum_scatter(totals[6], "dp", scatter_dimension=0, tiled=True),
        lax.psum_scatter(totals[7], "dp", scatter_dimension=0, tiled=True),
        lax.psum_scatter(totals[8], "dp", scatter_dimension=0, tiled=True),
        lax.psum_scatter(totals[9], "dp", scatter_dimension=0, tiled=True),
        lax.psum_scatter(totals[10], "dp", scatter_dimension=0, tiled=True),
        lax.psum_scatter(totals[11], "dp", scatter_dimension=0, tiled=True),
    )
    return (
        jnp.stack(outputs_list),
        jnp.stack(grads_list),
        totals[0],
        totals[1],
        totals[2],
        totals[3],
        totals[4],
        totals[5],
        totals[6],
        totals[7],
        totals[8],
        totals[9],
        totals[10],
        totals[11],
    )


COUNT = 32
ROWS, LAYERS = 8, 4


def meet_all(me):
    barrier = pltpu.get_barrier_semaphore()

    def greet(step, carry):
        pl.semaphore_signal(
            barrier, inc=1, device_id=(lax.rem(me + step, COUNT),), device_id_type=MESH
        )
        return carry

    lax.fori_loop(1, COUNT, greet, 0)
    pl.semaphore_wait(barrier, COUNT - 1)


def remote(source, target, send_sem, recv_sem, device):
    return pltpu.make_async_remote_copy(
        src_ref=source,
        dst_ref=target,
        send_sem=send_sem,
        recv_sem=recv_sem,
        device_id=(device,),
        device_id_type=MESH,
    )


WIDTHS = (48, 24, 24, 24, 96, 24, 24, 24)
BIAS_IN, BIAS_MIX, GAIN_FIRST, SHIFT_FIRST, BIAS_UP, BIAS_DOWN, GAIN_SECOND, SHIFT_SECOND = range(8)
TILE = 256
PAIR = 128


def contract(left, right, left_dim, right_dim):
    return lax.dot_general(
        left,
        right,
        (((left_dim,), (right_dim,)), ((), ())),
        preferred_element_type=jnp.float32,
    )


def owners(width):
    lane = lax.broadcasted_iota(jnp.int32, (COUNT, COUNT * width), 1)
    owner = (lane * (-(-(1 << 20) // width))) >> 20
    device = lax.broadcasted_iota(jnp.int32, (COUNT, COUNT * width), 0)
    return owner == device


def places(width):
    lane = lax.broadcasted_iota(jnp.int32, (PAIR, COUNT * width), 1)
    owner = (lane * (-(-(1 << 20) // width))) >> 20
    entry = lax.broadcasted_iota(jnp.int32, (PAIR, COUNT * width), 0)
    return jnp.where(lane - owner * width == entry, 1.0, 0.0).astype(jnp.bfloat16)


def columns(tile, size=TILE):
    return pl.ds(pl.multiple_of(tile * size, size), size)


def flat(value):
    return value.reshape(-1, value.shape[-1])


def take_rows(ref, start, stop):
    layers, seats, groups, small, _ = ref.shape
    pieces = []
    while start < stop:
        layer, rest = divmod(start // small, seats * groups)
        seat, group = divmod(rest, groups)
        whole = min((stop - start) // (small * groups), seats - seat)
        if group == 0 and whole:
            pieces.append(flat(ref[layer, seat : seat + whole]))
            start += whole * groups * small
        else:
            end = min(groups, group + (stop - start) // small)
            pieces.append(flat(ref[layer, seat, group:end]))
            start += (end - group) * small
    return jnp.concatenate(pieces, 0)


class Layer:
    def __init__(self, refs):
        self.__dict__.update(refs)
        self.rows, self.width = self.normed.shape
        self.hidden_width = self.slope.shape[1]

    def spread_small(self):
        for place, width in enumerate(WIDTHS):
            given = self.small[:, place, :].astype(jnp.bfloat16)
            spread = contract(given, places(width), 1, 0)
            row = jnp.sum(jnp.where(owners(width), spread, 0.0), 0, keepdims=True)
            if place == BIAS_IN:
                self.bias_row[:, : self.width] = row[:, : self.width]
                self.bias_row[:, self.width : 2 * self.width] = jnp.zeros_like(row[:, : self.width])
                self.bias_row[:, 2 * self.width :] = row[:, self.width :]
            elif place == BIAS_UP:
                self.up_row[...] = row
            else:
                self.vectors[place : place + 1, :] = row

    def vector(self, place):
        return self.vectors[place : place + 1, :]

    def project(self, tile):
        here = columns(tile)
        value = jnp.dot(
            flat(self.sequence[...]),
            flat(self.weight_in[:, :, :, :, here]),
            preferred_element_type=jnp.float32
        )
        value = (value + self.bias_row[:, here]).astype(jnp.bfloat16)
        scale = jnp.where(tile < self.width // TILE, 0.125, 1.0).astype(jnp.bfloat16)
        self.packed[:, here] = value * scale

    def heads_of(self, step):
        pairs = self.width // PAIR
        batch, pair = step // pairs, step % pairs
        rows = pl.ds(pl.multiple_of(batch * TILE, TILE), TILE)
        return batch, pair, rows

    def block(self, part, rows, pair):
        offset = pl.multiple_of(part * self.width + pair * PAIR, PAIR)
        return self.packed[rows, pl.ds(offset, PAIR)]

    def half(self, value, head):
        lane = lax.broadcasted_iota(jnp.int32, value.shape, 1)
        keep = lane < PAIR // 2 if head == 0 else lane >= PAIR // 2
        return jnp.where(keep, value, jnp.zeros_like(value))

    def attend(self, step):
        batch, pair, rows = self.heads_of(step)
        queries, key_block, value_block = (self.block(part, rows, pair) for part in range(3))
        length = jnp.where(batch == 0, self.lengths[0], self.lengths[1])
        lane = lax.broadcasted_iota(jnp.int32, (1, TILE), 1)
        blocked = jnp.where(lane < length, 0.0, -1e30)
        context = []
        for head in range(2):
            scores = contract(self.half(queries, head), key_block, 1, 1) + blocked
            weights = jnp.exp(scores - jnp.max(scores, -1, keepdims=True))
            total = jnp.sum(weights, -1, keepdims=True)
            low = (weights * (1.0 / total)).astype(jnp.bfloat16)
            self.chances[2 * step + head] = low
            context.append(jnp.dot(low, value_block, preferred_element_type=jnp.float32))
        lane = lax.broadcasted_iota(jnp.int32, context[0].shape, 1)
        joined = jnp.where(lane < PAIR // 2, context[0], context[1])
        self.context[rows, columns(pair, PAIR)] = joined.astype(jnp.bfloat16)

    def mix(self, part):
        rows = columns(part)
        branch = jnp.dot(
            self.context[rows, :], flat(self.weight_mix[...]), preferred_element_type=jnp.float32
        )
        summed = flat(self.sequence[part]).astype(jnp.float32) + (branch + self.vector(BIAS_MIX))
        centered = summed - jnp.mean(summed, -1, keepdims=True)
        factor = lax.rsqrt(jnp.mean(centered * centered, -1, keepdims=True) + epsilon)
        normed = centered * factor
        hidden = normed * self.vector(GAIN_FIRST) + self.vector(SHIFT_FIRST)
        self.normed[rows, :] = normed
        self.factor[rows, :] = factor
        self.hidden_low[rows, :] = hidden.astype(jnp.bfloat16)

    def up(self, tile):
        here = columns(tile)
        value = jnp.dot(
            self.hidden_low[...], flat(self.weight_up[:, :, :, :, here]), preferred_element_type=jnp.float32
        )
        value = value + self.up_row[:, here]
        below = 0.5 * (1.0 + lax.erf(value * 0.7071067811865476))
        density = jnp.exp(-0.5 * value * value) * 0.3989422804014327
        self.active[:, here] = (value * below).astype(jnp.bfloat16)
        self.slope[:, here] = (below + value * density).astype(self.slope.dtype)

    def down(self, tile):
        here = columns(tile)
        self.upper[:, here] = jnp.dot(
            self.active[...], flat(self.weight_down[:, :, :, :, here]), preferred_element_type=jnp.float32
        )

    def finish(self, part, size=128):
        rows = columns(part, size)
        hidden = self.normed[rows, :] * self.vector(GAIN_FIRST) + self.vector(SHIFT_FIRST)
        summed = hidden + (self.upper[rows, :] + self.vector(BIAS_DOWN))
        centered = summed - jnp.mean(summed, -1, keepdims=True)
        factor = lax.rsqrt(jnp.mean(centered * centered, -1, keepdims=True) + epsilon)
        normed = centered * factor
        gain = self.vector(GAIN_SECOND)
        low = (normed * gain + self.vector(SHIFT_SECOND)).astype(jnp.bfloat16)
        parts, seats = TILE // size, size // 8
        batch, span = part // parts, pl.ds((part % parts) * seats, seats)
        self.result[batch, span] = low.reshape(seats, 8, self.width)
        upstream = flat(self.upstream[batch, span]).astype(jnp.float32)
        grad = self.norm_backward(upstream, normed, factor, gain, GAIN_SECOND, SHIFT_SECOND)
        low = grad.astype(jnp.bfloat16)
        self.upper[rows, :] = grad
        self.feed_grad[rows, :] = low
        self.add_term(BIAS_DOWN, low.astype(jnp.float32))

    def add_term(self, place, value):
        self.terms[place : place + 1, :] += jnp.sum(value, 0, keepdims=True)

    def norm_backward(self, upstream, normed, factor, gain, gain_place, shift_place):
        self.add_term(gain_place, upstream * normed)
        self.add_term(shift_place, upstream)
        scaled = upstream * gain
        return factor * (
            scaled
            - jnp.mean(scaled, -1, keepdims=True)
            - normed * jnp.mean(scaled * normed, -1, keepdims=True)
        )

    def down_weight_grad(self, layer):
        span = self.hidden_width // LAYERS
        made = [
            contract(self.active[:, columns(layer * (span // TILE) + i)], self.feed_grad[...], 0, 0)
            for i in range(span // TILE)
        ]
        made = jnp.concatenate([part.astype(jnp.bfloat16) for part in made], 0)
        self.down_grad[layer] = made.reshape(self.down_grad.shape[1:])

    def active_backward(self, layer):
        span = self.hidden_width // LAYERS
        weight = flat(self.weight_down[layer])
        for i in range(span // TILE):
            here = columns(layer * (span // TILE) + i)
            grad = contract(self.feed_grad[...], weight[i * TILE : (i + 1) * TILE], 1, 1)
            low = (grad * self.slope[:, here].astype(jnp.float32)).astype(jnp.bfloat16)
            self.preact_grad[:, here] = low
            self.up_terms[:, here] = jnp.sum(low.astype(jnp.float32), 0, keepdims=True)

    def up_weight_grad(self, tile):
        here = columns(tile)
        grad = contract(self.hidden_low[...], self.preact_grad[:, here], 0, 0)
        self.keep_columns(self.up_grad, here, grad)

    def hidden_backward(self, tile):
        here = columns(tile)
        weight = take_rows(self.weight_up, tile * TILE, (tile + 1) * TILE)
        self.upper[:, here] += contract(self.preact_grad[...], weight, 1, 1)

    def first_backward(self, part, size=128):
        rows = columns(part, size)
        grad = self.norm_backward(
            self.upper[rows, :],
            self.normed[rows, :],
            self.factor[rows, :],
            self.vector(GAIN_FIRST),
            GAIN_FIRST,
            SHIFT_FIRST,
        )
        low = grad.astype(jnp.bfloat16)
        self.upper[rows, :] = grad
        self.feed_grad[rows, :] = low
        self.add_term(BIAS_MIX, low.astype(jnp.float32))

    def mix_weight_grad(self, tile):
        here = columns(tile)
        grad = contract(self.context[...], self.feed_grad[:, here], 0, 0)
        self.keep_columns(self.mix_grad, here, grad)

    def mix_backward(self, tile):
        here = columns(tile)
        weight = take_rows(self.weight_mix, tile * TILE, (tile + 1) * TILE)
        self.context_grad[:, here] = contract(self.feed_grad[...], weight, 1, 1).astype(
            jnp.bfloat16
        )

    def attend_backward(self, step):
        batch, pair, rows = self.heads_of(step)
        queries, key_block, value_block = (self.block(part, rows, pair) for part in range(3))
        grads = self.context_grad[rows, columns(pair, PAIR)]
        query_grad = key_grad = value_grad = 0.0
        for head in range(2):
            low = self.chances[2 * step + head]
            chance = low.astype(jnp.float32)
            mine = self.half(grads, head)
            chance_grad = contract(mine, value_block, 1, 1)
            moved = chance_grad - jnp.sum(chance * chance_grad, -1, keepdims=True)
            score_grad = (chance * moved).astype(jnp.bfloat16)
            value_grad += contract(low, mine, 0, 0)
            query_grad += jnp.dot(
                score_grad, self.half(key_block, head), preferred_element_type=jnp.float32
            )
            key_grad += contract(score_grad, self.half(queries, head), 0, 0)
        for part, grad in enumerate((query_grad * 0.125, key_grad, value_grad)):
            offset = pl.multiple_of(part * self.width + pair * PAIR, PAIR)
            self.packed[rows, pl.ds(offset, PAIR)] = grad.astype(jnp.bfloat16)

    def in_weight_grad(self, tile):
        here = columns(tile)
        grads = self.packed[:, here]
        self.keep_columns(self.in_grad, here, contract(flat(self.sequence[...]), grads, 0, 0))
        self.in_terms[:, here] = jnp.sum(grads.astype(jnp.float32), 0, keepdims=True)

    def input_backward(self, tile):
        here = columns(tile)
        weight = take_rows(self.weight_in, tile * TILE, (tile + 1) * TILE)
        grad = self.upper[:, here] + contract(self.packed[...], weight, 1, 1)
        shape = self.input_grad.shape[:3] + (TILE,)
        self.input_grad[:, :, :, here] = grad.astype(jnp.bfloat16).reshape(shape)

    def keep_columns(self, ref, here, grad):
        ref[:, :, :, :, here] = grad.astype(jnp.bfloat16).reshape(ref.shape[:4] + (TILE,))

    def gather_terms(self):
        for place, width in enumerate(WIDTHS):
            if place == BIAS_IN:
                row = jnp.concatenate(
                    [self.in_terms[:, : self.width], self.in_terms[:, 2 * self.width :]], -1
                )
            elif place == BIAS_UP:
                row = self.up_terms[...]
            else:
                row = self.terms[place : place + 1, :]
            high = row.astype(jnp.bfloat16)
            rest = row - high.astype(jnp.float32)
            middle = rest.astype(jnp.bfloat16)
            low = (rest - middle.astype(jnp.float32)).astype(jnp.bfloat16)
            keep, spots = owners(width), places(width)
            self.small_grad[:, place, :] = sum(
                contract(jnp.where(keep, part.astype(jnp.float32), 0.0).astype(jnp.bfloat16), spots, 1, 1)
                for part in (high, middle, low)
            )


def scratch_of(rows, width, hidden_width):
    low, full = jnp.bfloat16, jnp.float32
    return dict(
        bias_row=pltpu.VMEM((1, 3 * width), full),
        up_row=pltpu.VMEM((1, hidden_width), full),
        vectors=pltpu.VMEM((8, width), full),
        terms=pltpu.VMEM((8, width), full),
        up_terms=pltpu.VMEM((1, hidden_width), full),
        in_terms=pltpu.VMEM((1, 3 * width), full),
        packed=pltpu.VMEM((rows, 3 * width), low),
        chances=pltpu.VMEM((2 * rows // TILE * width // PAIR, TILE, TILE), low),
        context=pltpu.VMEM((rows, width), low),
        normed=pltpu.VMEM((rows, width), full),
        factor=pltpu.VMEM((rows, 1), full),
        hidden_low=pltpu.VMEM((rows, width), low),
        active=pltpu.VMEM((rows, hidden_width), low),
        slope=pltpu.VMEM((rows, hidden_width), low),
        upper=pltpu.VMEM((rows, width), full),
        feed_grad=pltpu.VMEM((rows, width), low),
    )


class Spot:
    def __init__(self):
        self.me = me = lax.axis_index("dp")
        core, column, row = me % 2, (me // 2) % 2, (me // 4) % 2
        self.layer, self.seat = me // 8, me % 8
        self.to_sibling = 1 - 2 * core
        across_row = 4 * (1 - 2 * row)
        across_column = 2 * (1 - 2 * column)
        self.to_second = (1 - core) * across_row + core * across_column
        self.to_third = (1 - core) * across_column + core * across_row
        self.sibling = me + self.to_sibling
        self.second = me + self.to_second
        self.third = me + self.to_third
        self.above = [lax.rem(self.layer + step, LAYERS) for step in (1, 2, 3)]


class Chunk:
    def __init__(self, kind, groups, cols):
        self.kind, self.groups, self.cols = kind, groups, cols

    def line(self, refs, seat):
        return refs[self.kind].at[:, seat, self.groups, :, self.cols]

    def block(self, refs, layer, seat):
        return refs[self.kind].at[layer, seat, self.groups, :, self.cols]

    def bulk(self, refs, layers, lines):
        return refs[self.kind].at[pl.ds(0, layers), pl.ds(0, lines), self.groups, :, self.cols]


def chunks_of(shapes):
    made = []
    for kind, (groups, _, width) in enumerate(shapes):
        if kind < 3:
            size = shapes[1][2]
            for start in range(0, width, size):
                made.append(Chunk(kind, pl.ds(0, groups), pl.ds(start, size)))
        else:
            size = shapes[0][0]
            for start in range(0, groups, size):
                made.append(Chunk(kind, pl.ds(start, size), pl.ds(0, width)))
    return made


class Traffic:
    def __init__(self, spot, refs):
        self.spot = spot
        self.__dict__.update(refs)
        self.chunks = chunks_of([tuple(shard.shape) for shard in self.shards])


    def own(self, k):
        chunk, spot = self.chunks[k], self.spot
        source = self.shards[chunk.kind].at[chunk.groups, :, chunk.cols]
        target = chunk.block(self.full, spot.layer, spot.seat)
        for layer in spot.above:
            remote(
                source, target, self.sent.at[k], self.along_in.at[k], layer * ROWS + spot.seat
            ).start()
        remote(source, target, self.sent.at[k], self.second_own.at[k], spot.second).start()
        remote(source, target, self.sent.at[k], self.third_own.at[k], spot.third).start()

    def line_out(self, k, seat, device, sem):
        line = self.chunks[k].line(self.full, seat)
        remote(line, line, self.sent.at[k], sem, device).start()

    def wait_lines(self, k, sem, count=1):
        chunk = self.chunks[k]
        layers = {0: 1, 3: 3}.get(count, LAYERS)
        here = chunk.bulk(self.full, layers, count if layers == LAYERS else 1)
        return remote(here, here, self.sent.at[k], sem, self.spot.me)

    def from_line(self, k):
        spot = self.spot
        self.wait_lines(k, self.along_in.at[k], 3).wait_recv()
        for layer in spot.above:
            block = self.chunks[k].block(self.full, layer, spot.seat)
            sent = self.sent.at[k]
            remote(block, block, sent, self.second_in.at[k], spot.second).start()
            remote(block, block, sent, self.third_in.at[k, 0], spot.third).start()
        self.line_out(k, spot.seat, spot.sibling, self.sibling_in.at[k])

    def from_second(self, k):
        spot = self.spot
        self.wait_lines(k, self.second_own.at[k], 0).wait_recv()
        self.wait_lines(k, self.second_in.at[k], 3).wait_recv()
        seat = spot.seat + spot.to_second
        self.line_out(k, seat, spot.third, self.third_in.at[k, 1])
        self.line_out(k, seat, spot.sibling, self.sibling_in.at[k])

    def from_third(self, k, which):
        spot = self.spot
        if which == 0:
            self.wait_lines(k, self.third_own.at[k], 0).wait_recv()
        self.wait_lines(k, self.third_in.at[k, which], 1 if which else 3).wait_recv()
        seat = spot.seat + spot.to_third + which * spot.to_second
        self.line_out(k, seat, spot.sibling, self.sibling_in.at[k])

    def complete(self, k):
        self.wait_lines(k, self.sibling_in.at[k], 4).wait_recv()

    def own_sent(self, k):
        self.wait_lines(k, self.sent.at[k], 7).wait_send()
        self.wait_lines(k, self.sent.at[k], 3).wait_send()


    def exchange(self, source, target, which, first=0, last=COUNT - 1):
        me = self.spot.me

        def go(step, carry):
            device = lax.rem(me + lax.rem(step * 5, COUNT), COUNT)
            remote(
                source.at[:, device],
                target.at[:, me],
                self.given.at[which],
                self.taken.at[which],
                device,
            ).start()
            return carry

        lax.fori_loop(1 + first, 1 + last, go, 0)

    def exchanged(self, target, which):
        here = target.at[:, pl.ds(0, COUNT - 1)]
        return remote(
            here,
            here,
            self.given.at[which],
            self.taken.at[which],
            self.spot.me,
        )

    def exchange_small(self, source, target, which):
        me = self.spot.me

        def go(step, carry):
            device = lax.rem(me + step, COUNT)
            remote(
                source if which == 4 else source.at[device],
                target.at[me],
                self.given.at[which],
                self.taken.at[which],
                device,
            ).start()
            return carry

        lax.fori_loop(1, COUNT, go, 0)

    def exchanged_small(self, target, which):
        here = target.at[pl.ds(0, COUNT - 1)]
        return remote(here, here, self.given.at[which], self.taken.at[which], self.spot.me)


    def move(self, k, seat, landing, device, sem):
        remote(
            self.chunks[k].line(self.partial, seat), landing, self.shed.at[k], sem, device
        ).start()

    def landing(self, k, landings, slot):
        chunk = self.chunks[k]
        return landings[chunk.kind].at[slot, :, chunk.groups, :, chunk.cols]

    def landed(self, k, landings, sem, layers=LAYERS):
        chunk = self.chunks[k]
        here = landings[chunk.kind].at[:, pl.ds(0, layers), chunk.groups, :, chunk.cols]
        remote(here, here, self.shed.at[k], sem, self.spot.me).wait_recv()

    def take_in(self, k, seat, landings, slot):
        chunk = self.chunks[k]
        line, here = chunk.line(self.partial, seat), self.landing(k, landings, slot)
        line[...] = line[...] + here[...]


    def move_block(self, k, layer, seat, landings, slot, device, sem):
        chunk = self.chunks[k]
        remote(
            chunk.block(self.partial, layer, seat),
            landings[chunk.kind].at[slot, layer, chunk.groups, :, chunk.cols],
            self.shed.at[k],
            sem,
            device,
        ).start()

    def take_block(self, k, layer, seat, landings, slot):
        chunk = self.chunks[k]
        block = chunk.block(self.partial, layer, seat)
        here = landings[chunk.kind].at[slot, layer, chunk.groups, :, chunk.cols]
        block[...] = block[...] + here[...]

    def blocks_to_third(self, k, layers, sem):
        spot = self.spot
        for layer in layers:
            for slot in range(2):
                seat = spot.seat + spot.to_third + slot * spot.to_second
                self.move_block(k, layer, seat, self.land_third, slot, spot.third, sem)

    def blocks_to_second(self, k, layers, sem, next_sem):
        spot = self.spot
        self.landed(k, self.land_third, sem, len(layers))
        for layer in layers:
            for slot in range(2):
                seat = spot.seat + slot * spot.to_second
                self.take_block(k, layer, seat, self.land_third, slot)
            seat = spot.seat + spot.to_second
            self.move_block(k, layer, seat, self.land_second, 0, spot.second, next_sem)

    def late_third(self, k):
        self.blocks_to_third(k, [self.spot.layer], self.across_own.at[k])

    def late_second(self, k):
        self.blocks_to_second(
            k, [self.spot.layer], self.across_own.at[k], self.over_own.at[k]
        )

    def late_owner(self, k):
        self.landed(k, self.land_second, self.over_own.at[k], 1)
        self.take_block(k, self.spot.layer, self.spot.seat, self.land_second, 0)
        self.keep(k).start()

    def begin(self, k):
        spot = self.spot
        for slot in range(4):
            seat = 2 * slot + (spot.seat + 1) % 2
            self.move(
                k, seat, self.landing(k, self.land_first, slot), spot.sibling, self.first_in.at[k]
            )

    def to_third(self, k):
        spot = self.spot
        self.landed(k, self.land_first, self.first_in.at[k])
        for slot in range(4):
            self.take_in(k, 2 * slot + spot.seat % 2, self.land_first, slot)
        if k in self.late:
            self.blocks_to_third(k, spot.above, self.across_in.at[k])
            return
        for slot in range(2):
            seat = spot.seat + spot.to_third + slot * spot.to_second
            self.move(
                k, seat, self.landing(k, self.land_third, slot), spot.third, self.across_in.at[k]
            )

    def to_second(self, k):
        spot = self.spot
        if k in self.late:
            self.blocks_to_second(k, spot.above, self.across_in.at[k], self.over_in.at[k])
            return
        self.landed(k, self.land_third, self.across_in.at[k])
        for slot in range(2):
            self.take_in(k, spot.seat + slot * spot.to_second, self.land_third, slot)
        seat = spot.seat + spot.to_second
        self.move(k, seat, self.landing(k, self.land_second, 0), spot.second, self.over_in.at[k])

    def to_owner(self, k):
        chunk, spot = self.chunks[k], self.spot
        if k in self.late:
            self.landed(k, self.land_second, self.over_in.at[k], 3)
            for layer in spot.above:
                self.take_block(k, layer, spot.seat, self.land_second, 0)
        else:
            self.landed(k, self.land_second, self.over_in.at[k])
            self.take_in(k, spot.seat, self.land_second, 0)
        target = self.sums[chunk.kind].at[spot.layer, chunk.groups, :, chunk.cols]
        for layer in spot.above:
            remote(
                chunk.block(self.partial, layer, spot.seat),
                target,
                self.shed.at[k],
                self.owner_in.at[k],
                layer * ROWS + spot.seat,
            ).start()
        if k not in self.late:
            self.keep(k).start()

    def keep(self, k):
        chunk, spot = self.chunks[k], self.spot
        return pltpu.make_async_copy(
            chunk.block(self.partial, spot.layer, spot.seat),
            self.sums[chunk.kind].at[spot.layer, chunk.groups, :, chunk.cols],
            self.kept.at[k],
        )

    def settle(self, k):
        chunk = self.chunks[k]
        here = self.sums[chunk.kind].at[pl.ds(0, 3), chunk.groups, :, chunk.cols]
        remote(here, here, self.shed.at[k], self.owner_in.at[k], self.spot.me).wait_recv()
        self.keep(k).wait()
        for count in (7, 3):
            there = chunk.bulk(self.partial, 3 if count == 3 else LAYERS, 1 if count == 3 else count)
            remote(there, there, self.shed.at[k], self.owner_in.at[k], self.spot.me).wait_send()


def interleave(count, body, steps=()):
    assert len(steps) <= count

    def one(index, carry):
        body(index)
        for place, thunks in enumerate(steps):
            if thunks:

                @pl.when(index == place)
                def _():
                    for thunk in thunks:
                        thunk()

        return carry

    lax.fori_loop(0, count, one, 0)


def unroll(count, body, steps):
    for index in range(count):
        body(index)
        for thunk in steps[index]:
            thunk()


def spread(thunks, slots):
    return [
        thunks[len(thunks) * place // slots : len(thunks) * (place + 1) // slots]
        for place in range(slots)
    ]


LATE = 11
PACES = 3, 3, 3, 0, 1, 2, 6, 3, 1
LEAD, TOKENS_EACH, COTANGENT_FROM, COTANGENT_EACH = 1, 6, 4, 4


def step_kernel(trees, *given):
    given, named = list(given), {}
    for tree in trees:
        named.update(jax.tree.unflatten(tree, given[: tree.num_leaves]))
        given = given[tree.num_leaves :]
    refs = types.SimpleNamespace(**named)
    spot = Spot()
    me = spot.me
    traffic = Traffic(spot, named)
    chunks = range(len(traffic.chunks))
    tokens, cotangent = refs.tokens, refs.cotangent
    sequence, upstream = refs.sequence, refs.upstream
    first_spare, second_spare = refs.first_spare, refs.second_spare

    locals_ = [
        pltpu.make_async_copy(
            traffic.shards[kind], traffic.full[kind].at[spot.layer, spot.seat], traffic.local.at[kind]
        )
        for kind in range(4)
    ] + [
        pltpu.make_async_copy(cotangent.at[:, me], upstream.at[:, me], traffic.local.at[5]),
        pltpu.make_async_copy(refs.small_own, refs.small.at[me], traffic.local.at[6]),
    ]
    early = [
        pltpu.make_async_copy(tokens, first_spare, traffic.local.at[4]),
        pltpu.make_async_copy(refs.lengths, refs.lengths_here, traffic.local.at[7]),
        pltpu.make_async_copy(refs.order, refs.order_here, traffic.local.at[8]),
    ]
    for copy in early + locals_:
        copy.start()
    for copy in early:
        copy.wait()
    for batch in range(2):
        for seat in range(COUNT):
            second_spare[batch, seat] = first_spare[batch, refs.order_here[batch, seat]]
    own_sequence = pltpu.make_async_copy(
        second_spare.at[:, me], sequence.at[:, me], traffic.local.at[4]
    )
    own_sequence.start()
    meet_all(me)

    def piece_of(source, target, which, first, last):
        return lambda: traffic.exchange(source, target, which, first, last)

    def do(method, *args):
        return lambda: method(*args)

    layer = Layer(named)
    layer.context_grad, layer.preact_grad = refs.hidden_low, refs.active
    layer.result, layer.input_grad = first_spare, second_spare
    layer.weight_in, layer.weight_mix, layer.weight_up, layer.weight_down = refs.full
    layer.in_grad, layer.mix_grad, layer.up_grad, layer.down_grad = refs.partial
    layer.lengths = [
        refs.lengths_here[batch, refs.order_here[batch, me]] for batch in range(2)
    ]
    tiles, wide = layer.width // TILE, layer.hidden_width // TILE
    pairs = 2 * (layer.width // PAIR)
    ins = 3
    ups = wide // tiles
    assert len(chunks) == ins + 1 + 2 * ups

    ticks = []
    for tick in range(-LEAD, len(chunks) + 2):
        here = []
        if 0 <= tick + LEAD < len(chunks):
            here.append(do(traffic.own, tick + LEAD))
        first = (tick + LEAD) * TOKENS_EACH
        if first < COUNT - 1:
            last = min(first + TOKENS_EACH, COUNT - 1)
            here.append(piece_of(second_spare, sequence, 0, first, last))
        if tick == -LEAD:
            here.append(do(traffic.exchange_small, refs.small_own, refs.small, 4))
        if 0 <= tick < len(chunks):
            here.append(do(traffic.from_line, tick))
        if 0 <= tick - 1 < len(chunks):
            here.append(do(traffic.from_second, tick - 1))
            here.append(do(traffic.from_third, tick - 1, 0))
        if 0 <= tick - 2 < len(chunks):
            here.append(do(traffic.from_third, tick - 2, 1))
        first = (tick - COTANGENT_FROM) * COTANGENT_EACH
        if 0 <= first < COUNT - 1:
            last = min(first + COTANGENT_EACH, COUNT - 1)
            here.append(piece_of(cotangent, upstream, 1, first, last))
        ticks.append(here)
    flat = lambda first, last: [thunk for here in ticks[first + LEAD : last + LEAD] for thunk in here]

    for thunk in flat(-LEAD, 0):
        thunk()
    for copy in locals_:
        copy.wait()
    layer.terms[...] = jnp.zeros_like(layer.terms)
    for thunk in flat(0, 2):
        thunk()
    traffic.exchanged_small(refs.small, 4).wait_recv()
    layer.spread_small()
    for thunk in flat(2, ins + 2):
        thunk()
    dealt = traffic.exchanged(sequence, 0)
    dealt.wait_recv()
    own_sequence.wait()
    for k in range(ins):
        traffic.complete(k)
    interleave(3 * tiles, layer.project, spread(flat(ins + 2, ins + 3), 3 * tiles))
    interleave(pairs, layer.attend, spread(flat(ins + 3, ins + 6), pairs))
    traffic.complete(ins)
    interleave(layer.rows // TILE, layer.mix)
    for thunk in flat(ins + 6, ins + ups + 3):
        thunk()
    for k in range(ins + 1, ins + 1 + ups):
        traffic.complete(k)
    interleave(wide, layer.up, spread(flat(ins + ups + 3, len(chunks) + 2), wide))
    for k in range(ins + 1 + ups, len(chunks)):
        traffic.complete(k)
    interleave(tiles, layer.down)
    cotangents = traffic.exchanged(upstream, 1)
    cotangents.wait_recv()
    interleave(layer.rows // 128, layer.finish)

    keep_result = pltpu.make_async_copy(
        first_spare.at[:, me], refs.returned.at[:, me], traffic.local.at[0]
    )
    keep_result.start()
    pieces = [
        piece_of(first_spare, refs.returned, 2, first, min(first + 8, COUNT - 1))
        for first in range(0, COUNT - 1, 8)
    ]
    interleave(LAYERS, layer.down_weight_grad, spread(pieces, LAYERS))

    queue = list(range(ins + 1 + ups, len(chunks))) + list(range(ins + 1, ins + 1 + ups))
    queue += [ins] + list(range(ins))
    traffic.late = queue[len(queue) - LATE :]
    walk = []
    for tick in range(len(queue) + 2):
        for late, stage in enumerate((traffic.to_third, traffic.to_second, traffic.to_owner)):
            if 0 <= tick - late < len(queue):
                walk.append(do(stage, queue[tick - late]))
        if tick == len(queue) - 1:
            walk += [do(traffic.late_third, k) for k in traffic.late]
    for stage in (traffic.late_second, traffic.late_owner):
        walk += [do(stage, k) for k in traffic.late]

    def next_steps(count):
        taken, walk[:] = walk[:count], walk[count:]
        return taken

    def with_begin(steps, count, every, kinds):
        made = [list(step) for step in steps] + [[] for _ in range(count - len(steps))]
        for place, k in enumerate(kinds):
            made[(place + 1) * every - 1].insert(0, do(traffic.begin, k))
        return made

    for k in queue[:ups]:
        traffic.begin(k)
    paces = iter(PACES)
    interleave(LAYERS, layer.active_backward, spread(next_steps(next(paces)), LAYERS))
    interleave(
        wide,
        layer.up_weight_grad,
        with_begin(
            [[]] * tiles + spread(next_steps(next(paces)), wide - tiles),
            wide,
            tiles,
            queue[ups : 2 * ups],
        ),
    )
    unroll(tiles, layer.hidden_backward, spread(next_steps(next(paces)), tiles))
    interleave(layer.rows // 128, layer.first_backward, spread(next_steps(next(paces)), 1))
    interleave(
        tiles,
        layer.mix_weight_grad,
        with_begin(
            spread(next_steps(next(paces)), tiles), tiles, tiles, queue[2 * ups : 2 * ups + 1]
        ),
    )
    unroll(tiles, layer.mix_backward, spread(next_steps(next(paces)), tiles))
    interleave(pairs, layer.attend_backward, spread(next_steps(next(paces)), pairs))
    interleave(
        3 * tiles,
        layer.in_weight_grad,
        with_begin(
            spread(next_steps(next(paces)), 3 * tiles), 3 * tiles, tiles, queue[2 * ups + 1 :]
        ),
    )
    dealt.wait_send()
    unroll(tiles, layer.input_backward, spread(next_steps(next(paces)), tiles))
    keep_grad = pltpu.make_async_copy(
        second_spare.at[:, me], refs.tokens_grad.at[:, me], traffic.local.at[2]
    )
    keep_grad.start()
    left = next_steps(len(walk))

    def small_out():
        layer.gather_terms()
        traffic.exchange_small(refs.small_grad, refs.small_sums, 5)
        keep_small.start()

    keep_small = pltpu.make_async_copy(
        refs.small_grad.at[me], refs.small_sums.at[me], traffic.local.at[1]
    )
    left.insert(2, small_out)
    cuts = list(range(0, COUNT - 1, 4))
    for place in range(max(len(left), len(cuts))):
        if place < len(cuts):
            piece_of(
                second_spare, refs.tokens_grad, 3, cuts[place], min(cuts[place] + 4, COUNT - 1)
            )()
        if place < len(left):
            left[place]()
    for k in queue:
        traffic.settle(k)
        traffic.own_sent(k)
    cotangents.wait_send()
    for target, which in ((refs.returned, 2), (refs.tokens_grad, 3)):
        copy = traffic.exchanged(target, which)
        copy.wait_recv()
        copy.wait_send()
    traffic.exchanged_small(refs.small, 4).wait_send()
    small = traffic.exchanged_small(refs.small_sums, 5)
    small.wait_recv()
    small.wait_send()
    for copy in (keep_result, keep_small, keep_grad):
        copy.wait()


def encoder_step(lengths, order, tokens, cotangent, shards, small_own):
    low, full = jnp.bfloat16, jnp.float32
    width, hidden_width = tokens.shape[-1], shards[2].shape[-1]
    rows = tokens.shape[0] * COUNT * tokens.shape[2]
    anywhere = pl.BlockSpec(memory_space=pl.ANY)
    inputs = dict(
        lengths=lengths,
        order=order,
        tokens=tokens,
        cotangent=cotangent,
        shards=shards,
        small_own=small_own,
    )
    shapes = [shard.shape for shard in shards]
    smalls = ((COUNT,) + small_own.shape, full)
    outputs = dict(
        returned=jax.ShapeDtypeStruct(tokens.shape, low),
        tokens_grad=jax.ShapeDtypeStruct(tokens.shape, low),
        sums=[jax.ShapeDtypeStruct((LAYERS,) + shape, low) for shape in shapes],
        small_sums=jax.ShapeDtypeStruct(*smalls),
    )
    sequences = pltpu.VMEM(tokens.shape, low)
    scratch = dict(
        full=[pltpu.VMEM((LAYERS, ROWS) + shape, low) for shape in shapes],
        partial=[pltpu.VMEM((LAYERS, ROWS) + shape, low) for shape in shapes],
        land_first=[pltpu.VMEM((4, LAYERS) + shape, low) for shape in shapes],
        land_third=[pltpu.VMEM((2, LAYERS) + shape, low) for shape in shapes],
        land_second=[pltpu.VMEM((1, LAYERS) + shape, low) for shape in shapes],
        sequence=sequences,
        upstream=sequences,
        first_spare=sequences,
        second_spare=sequences,
        lengths_here=pltpu.SMEM(lengths.shape, lengths.dtype),
        order_here=pltpu.SMEM(order.shape, order.dtype),
        small=pltpu.VMEM(*smalls),
        small_grad=pltpu.VMEM(*smalls),
        **scratch_of(rows, width, hidden_width),
    )
    count = len(chunks_of(shapes))
    each = pltpu.SemaphoreType.DMA((count,))
    sems = dict(
        local=pltpu.SemaphoreType.DMA((9,)),
        given=pltpu.SemaphoreType.DMA((6,)),
        taken=pltpu.SemaphoreType.DMA((6,)),
        third_in=pltpu.SemaphoreType.DMA((count, 2)),
        sent=each,
        along_in=each,
        second_in=each,
        second_own=each,
        third_own=each,
        sibling_in=each,
        shed=each,
        first_in=each,
        across_in=each,
        over_in=each,
        across_own=each,
        over_own=each,
        owner_in=each,
        kept=each,
    )
    given, given_tree = jax.tree.flatten(inputs)
    made, made_tree = jax.tree.flatten(outputs)
    held, held_tree = jax.tree.flatten({**scratch, **sems})
    results = pl.pallas_call(
        functools.partial(step_kernel, (given_tree, made_tree, held_tree)),
        out_shape=made,
        in_specs=[anywhere] * len(given),
        out_specs=[anywhere] * len(made),
        scratch_shapes=held,
        compiler_params=pltpu.CompilerParams(
            collective_id=0, has_side_effects=True, vmem_limit_bytes=VMEM_LIMIT
        ),
        name="encoder_step",
    )(*given)
    results = jax.tree.unflatten(made_tree, results)
    return types.SimpleNamespace(**results)


VMEM_LIMIT = 63 << 20


def finish_kernel(order, *refs):
    sources, targets, inner, ready = refs[:7], refs[7:21], refs[21:28], refs[28:42]
    sems, out_sems = refs[42:]
    copies = [
        pltpu.make_async_copy(source, target, sems.at[place])
        for place, (source, target) in enumerate(zip(sources, (ready[0], *inner[1:])))
    ]
    outward = [
        pltpu.make_async_copy(source, target, out_sems.at[place])
        for place, (source, target) in enumerate(zip(ready, targets))
    ]
    for place in (1, 0, 6, 2, 3, 4, 5):
        copies[place].start()
    copies[1].wait()
    for batch in range(2):
        for slot in range(COUNT):
            ready[1][batch, order[batch, slot]] = inner[1][batch, slot]
    outward[1].start()
    copies[0].wait()
    outward[0].start()
    copies[6].wait()
    small = jnp.sum(inner[6][...], 0)
    for place, out in enumerate(ready[6:]):
        out[...] = small[place : place + 1, : out.shape[1]]
        outward[6 + place].start()
    for place in (2, 3, 4, 5):
        copies[place].wait()
        parts = inner[place]
        ready[place][...] = sum(parts[layer].astype(jnp.float32) for layer in range(LAYERS))
        outward[place].start()
    for copy in outward:
        copy.wait()


def finish_step(order, returned, tokens_grad, sums, small_sums):
    outside = pl.BlockSpec(memory_space=pltpu.HBM)
    parts = [returned, tokens_grad, *sums, small_sums]
    made = (
        [jax.ShapeDtypeStruct(returned.shape, returned.dtype)] * 2
        + [jax.ShapeDtypeStruct(part.shape[1:], jnp.float32) for part in sums]
        + [jax.ShapeDtypeStruct((1, width), jnp.float32) for width in WIDTHS]
    )
    return pl.pallas_call(
        finish_kernel,
        out_shape=made,
        in_specs=[pl.BlockSpec(memory_space=pltpu.SMEM)] + [outside] * len(parts),
        out_specs=[outside] * len(made),
        scratch_shapes=[pltpu.VMEM(part.shape, part.dtype) for part in parts + made]
        + [pltpu.SemaphoreType.DMA((len(parts),)), pltpu.SemaphoreType.DMA((len(made),))],
        compiler_params=pltpu.CompilerParams(vmem_limit_bytes=VMEM_LIMIT),
        name="finish_step",
    )(order, *parts)


SMALL = (1, 3, 4, 5, 7, 9, 10, 11)
LARGE = (0, 2, 6, 8)


def local(tokens, lengths, order, *rest):
    shards, cotangent = rest[:12], rest[12]
    if lax.axis_size("dp") != COUNT or tokens.shape[2] % 8:
        return portable(tokens, lengths, order, *rest)
    small = sum(
        lax.pad(
            shards[i].astype(jnp.float32)[None],
            jnp.float32(0),
            ((place, len(SMALL) - 1 - place, 0), (0, 128 - shards[i].shape[0], 0)),
        )
        for place, i in enumerate(SMALL)
    )
    made = encoder_step(
        lengths,
        order,
        tokens,
        cotangent,
        [shards[i].reshape(-1, 8, shards[i].shape[-1]) for i in LARGE],
        small,
    )
    layer_out, tokens_grad, *rest = finish_step(
        order, made.returned, made.tokens_grad, made.sums, made.small_sums
    )
    outputs = [None] * 12
    for i, total in zip(LARGE, rest[:4]):
        outputs[i] = total.reshape(-1, total.shape[-1])
    for i, total in zip(SMALL, rest[4:]):
        outputs[i] = total.reshape(-1)
    return (layer_out, tokens_grad, *outputs)


def solution(mesh):
    return jax.shard_map(
        local,
        mesh=mesh,
        in_specs=(
            P(None, None, "dp", None),
            P(),
            P(),
            P("dp", None),
            P("dp"),
            P("dp", None),
            P("dp"),
            P("dp"),
            P("dp"),
            P("dp", None),
            P("dp"),
            P("dp", None),
            P("dp"),
            P("dp"),
            P("dp"),
            P(None, None, "dp", None),
        ),
        out_specs=(
            P(None, None, "dp", None),
            P(None, None, "dp", None),
            P("dp", None),
            P("dp"),
            P("dp", None),
            P("dp"),
            P("dp"),
            P("dp"),
            P("dp", None),
            P("dp"),
            P("dp", None),
            P("dp"),
            P("dp"),
            P("dp"),
        ),
        check_vma=False,
    )
```
